32 devices in a mesh: seq: 16 (over z, y, x), head: 2 (over core).
Axes of the slice: x: 2, y: 2, z: 4, core: 2. Of those that a mesh axis runs over, the one named last changes fastest.
Arguments:
- queries: bfloat16 [2048, 2048], P('seq', 'head'), may hold values from -144 to 144
- keys: bfloat16 [2048, 2048], P('seq', 'head'), may hold values from -4 to 4
- values: bfloat16 [2048, 2048], P('seq', 'head'), may hold values from -6 to 6
- grad_out: bfloat16 [2048, 2048], P('seq', 'head'), may hold values from -6 to 6
- bias_table: float32 [32, 128], P('head'), may hold values from -5 to 5
- bucket_ids: int32 [16, 4, 256], P('seq'), may hold values from 0 to 127
- block_mask: int32 [16, 4], P('seq'), may hold values 0 or 1
Outputs:
- grad_queries: bfloat16 [2048, 2048], P('seq', 'head')
- grad_keys: bfloat16 [2048, 2048], P('seq', 'head')
- grad_values: bfloat16 [2048, 2048], P('seq', 'head')
- grad_bias: float32 [32, 128], replicated
The draws below stay inside these ranges and needn't reach their ends.
All inputs are finite; a program needn't handle non-finite values. No bound on the sum of `block_mask` on one device may be relied on, other than what follows from the above.
Results may differ from the reference program's by a relative error of at most 0.005.
Values may be sent and summed in bfloat16 or wider, within the bound.
No kernel may reach another device: no remote copies, remote signals or barrier semaphores. Data moves between devices by JAX's collectives and lax.ppermute only.
A program may use at most 64 MiB of HBM per device.

```python
import jax
import jax.numpy as jnp
from jax import lax

HEADS = 32
HEAD_DIM = 64
BUCKETS = 128
TOK_DEV = 128
SPAN = 4
BLOCKS = 16
TOKENS = 2048
N_SEQ = 16


def drawn_pair(key):
    width = HEADS * HEAD_DIM
    base_keys = jnp.clip(jax.random.normal(jax.random.fold_in(key, 11), (TOKENS, width), jnp.float32), -4.0, 4.0)
    base_queries = jnp.clip(jax.random.normal(jax.random.fold_in(key, 12), (TOKENS, width), jnp.float32), -4.0, 4.0)
    return (base_queries, base_keys)


def draw_queries(key, part):
    return drawn_pair(key)[0].astype(jnp.bfloat16)


def draw_keys(key, part):
    return drawn_pair(key)[1].astype(jnp.bfloat16)


def set_ends(values, key, least, high):
    index_at = [jax.random.randint(jax.random.fold_in(key, axis), (), 0, length) for axis, length in enumerate(values.shape)]
    longest = values.shape.index(max(values.shape))
    neighbour = index_at[:longest] + [(index_at[longest] + 1) % values.shape[longest]] + index_at[longest + 1:]
    return values.at[tuple(index_at)].set(least).at[tuple(neighbour)].set(high)


def levels(key, shape, split, least, top_value):
    factor_of, own = 1.0, jax.random.fold_in(key, 6)
    for axis_at, parts in split:
        steps = jnp.exp(jax.random.uniform(jax.random.fold_in(own, axis_at), (parts,), jnp.float32, least / len(split), top_value / len(split)))
        factor_of = factor_of * jnp.repeat(steps, shape[axis_at] // parts).reshape([-1 if axis == axis_at else 1 for axis in range(len(shape))])
    return factor_of


def bell_draw(rng, dims, scale, limit, cuts=(), kind=jnp.bfloat16):
    gain = levels(rng, dims, cuts, -0.22, 0.18) if cuts else 1.0
    result = jax.random.normal(rng, dims, jnp.float32) * scale * gain
    return jnp.minimum(jnp.maximum(result, -limit), limit).astype(kind)


def setup_inputs(seed: int = 0) -> dict:
    splits = jax.random.split(jax.random.key(seed), 8)
    queries = draw_queries(jax.random.fold_in(splits[7], 71), 0)
    keys = draw_keys(jax.random.fold_in(splits[7], 71), 0)
    values = bell_draw(splits[2], (TOKENS, HEADS * HEAD_DIM), 1.0, 6.0, ((0, 16), (1, 2)))
    grad_out = bell_draw(splits[3], (TOKENS, HEADS * HEAD_DIM), 1.0, 6.0, ((0, 16), (1, 2)))
    bias_table = bell_draw(splits[4], (HEADS, BUCKETS), 1.0, 5.0, ((0, 2),), jnp.float32)
    bucket_ids = set_ends(jax.random.randint(splits[5], (BLOCKS, SPAN, 2 * TOK_DEV), 0, BUCKETS), jax.random.fold_in(splits[5], 1), 0, BUCKETS - 1).astype(jnp.int32)
    block_mask = set_ends((jax.random.randint(splits[6], (BLOCKS, SPAN), 0, 4) < 3).astype(jnp.int32), jax.random.fold_in(splits[6], 1), 0, 1)
    return {"queries": queries, "keys": keys, "values": values, "grad_out": grad_out, "bias_table": bias_table, "bucket_ids": bucket_ids, "block_mask": block_mask}


def reference(queries, keys, values, grad_out, bias_table, bucket_ids, block_mask):
    tok = TOK_DEV
    width = HEADS * HEAD_DIM
    scale = HEAD_DIM ** -0.5
    margin = (SPAN - 1) * tok
    keys_pad = jnp.concatenate([jnp.zeros((margin, width), keys.dtype), keys], axis=0)
    values_pad = jnp.concatenate([jnp.zeros((margin, width), values.dtype), values], axis=0)
    rows = jnp.arange(tok, dtype=jnp.int32)
    window = jnp.arange(SPAN * tok, dtype=jnp.int32)
    offset = SPAN - 1 - window // tok
    inner = window % tok
    position = rows[:, None] - inner[None, :] + tok - 1
    highest = lax.Precision.HIGHEST

    def step(carry, block):
        key_acc, value_acc, bias_acc = carry
        start = (block * tok).astype(jnp.int32)
        query_blk = lax.dynamic_slice_in_dim(queries, start, tok, 0).astype(jnp.float32).reshape(tok, HEADS, HEAD_DIM)
        cot_blk = lax.dynamic_slice_in_dim(grad_out, start, tok, 0).astype(jnp.float32).reshape(tok, HEADS, HEAD_DIM)
        key_win = lax.dynamic_slice_in_dim(keys_pad, start, SPAN * tok, 0).astype(jnp.float32).reshape(SPAN * tok, HEADS, HEAD_DIM)
        value_win = lax.dynamic_slice_in_dim(values_pad, start, SPAN * tok, 0).astype(jnp.float32).reshape(SPAN * tok, HEADS, HEAD_DIM)
        table = lax.dynamic_index_in_dim(bucket_ids, block, 0, keepdims=False)
        ids = table[offset[None, :], position]
        bias = bias_table[:, ids]
        scores = scale * jnp.einsum("qhd,khd->hqk", query_blk, key_win, precision=highest) + bias
        flag_row = lax.dynamic_index_in_dim(block_mask, block, 0, keepdims=False)
        whole = (flag_row[offset] == 1) & (block - offset >= 0)
        valid = jnp.where(offset[None, :] == 0, rows[:, None] >= inner[None, :], whole[None, :])
        masked = jnp.where(valid[None], scores, jnp.float32(-1e30))
        top = masked.max(axis=-1, keepdims=True)
        weights = jnp.where(valid[None], jnp.exp(masked - top), jnp.float32(0.0))
        lse = top[..., 0] + jnp.log(weights.sum(axis=-1))
        prob = jnp.exp(masked - lse[..., None])
        dprob = jnp.einsum("qhd,khd->hqk", cot_blk, value_win, precision=highest)
        delta = (prob * dprob).sum(axis=-1)
        dscore = prob * (dprob - delta[..., None])
        score16 = lax.optimization_barrier(dscore.astype(jnp.bfloat16)).astype(jnp.float32)
        prob16 = lax.optimization_barrier(prob.astype(jnp.bfloat16)).astype(jnp.float32)
        grad_q = scale * jnp.einsum("hqk,khd->qhd", score16, key_win, precision=highest)
        grad_k = scale * jnp.einsum("hqk,qhd->khd", score16, query_blk, precision=highest).reshape(SPAN * tok, width)
        grad_v = jnp.einsum("hqk,qhd->khd", prob16, cot_blk, precision=highest).reshape(SPAN * tok, width)
        key_acc = lax.dynamic_update_slice_in_dim(key_acc, lax.dynamic_slice_in_dim(key_acc, start, SPAN * tok, 0) + grad_k, start, 0)
        value_acc = lax.dynamic_update_slice_in_dim(value_acc, lax.dynamic_slice_in_dim(value_acc, start, SPAN * tok, 0) + grad_v, start, 0)
        bias_acc = bias_acc.at[:, ids].add(dscore)
        return (key_acc, value_acc, bias_acc), grad_q.reshape(tok, width).astype(jnp.bfloat16)

    start_carry = (jnp.zeros((margin + TOKENS, width), jnp.float32), jnp.zeros((margin + TOKENS, width), jnp.float32), jnp.zeros((HEADS, BUCKETS), jnp.float32))
    (key_acc, value_acc, bias_acc), grad_blocks = lax.scan(step, start_carry, jnp.arange(N_SEQ, dtype=jnp.int32))
    grad_queries = grad_blocks.reshape(TOKENS, width)
    grad_keys = key_acc[margin:].astype(jnp.bfloat16)
    grad_values = value_acc[margin:].astype(jnp.bfloat16)
    return grad_queries, grad_keys, grad_values, bias_acc
```

```python
import math

import jax
import jax.numpy as jnp
from jax import lax
from jax.experimental import pallas as pl
from jax.experimental.pallas import tpu as pltpu
from jax.sharding import PartitionSpec as P

F32 = jnp.float32
BF16 = jnp.bfloat16
NEG = -1e30
NT = (((1,), (1,)), ((), ()))
NN = (((1,), (0,)), ((), ()))
CODE_ROWS = 16


def dot(a, b, dims):
    return lax.dot_general(a, b, dims, preferred_element_type=F32)


def at(start, size):
    return pl.ds(pl.multiple_of(start, size), size)


def call(kernel, outs, args, scratch=(), flops=0, name=None):
    smem = pl.BlockSpec(memory_space=pltpu.SMEM)
    vmem = pl.BlockSpec(memory_space=pltpu.VMEM)
    moved = sum(a.size * a.dtype.itemsize for a in args) + sum(
        math.prod(s) * jnp.dtype(d).itemsize for s, d in outs
    )
    return pl.pallas_call(
        kernel,
        out_shape=tuple(jax.ShapeDtypeStruct(s, d) for s, d in outs),
        in_specs=[smem] + [vmem] * (len(args) - 1),
        out_specs=tuple(vmem for _ in outs),
        scratch_shapes=list(scratch),
        cost_estimate=pl.CostEstimate(flops=flops, bytes_accessed=moved, transcendentals=0),
        name=name,
    )(*args)


class Sizes:
    def __init__(self, tok, width, heads, span, buckets, group):
        self.tok, self.width, self.heads, self.span, self.buckets = tok, width, heads, span, buckets
        self.group = group
        self.hd = width // heads
        self.hg = heads // group
        self.cw = self.hg * self.hd
        self.pairs = self.hg // 2
        self.scale = self.hd ** (-0.5)
        self.halo = span - 1
        self.ext = group + self.halo
        self.qrows = 2 * tok + CODE_ROWS
        assert heads % group == 0 and self.hg % 2 == 0 and 2 * self.hd == 128
        assert tok == 128 and buckets == 128 and group >= self.halo and self.hg <= 8
        assert math.frexp(self.scale)[0] == 0.5


def pack_kernel(z, parts, me_ref, *refs):
    ins, outs = refs[:parts], refs[parts:]
    for k in range(z.group):
        cols = at((me_ref[0] ^ k) * z.cw, z.cw)
        for n, ref in enumerate(ins[:2]):
            outs[k][n * z.tok : (n + 1) * z.tok, :] = ref[:, cols]
        if parts == 3:
            outs[k][2 * z.tok :, :] = ins[2][...]


def halo_kernel(z, rows, first, me_ref, *refs):
    out = refs[-1]
    for k in range(z.group):
        j = me_ref[0] ^ k

        @pl.when((j >= first) & (j < first + z.halo))
        def _():
            out[at((j - first) * rows, rows), :] = refs[k][...]


def onehot_of(codes, z):
    wide = codes.shape[1]
    slots = lax.broadcasted_iota(jnp.int32, (z.buckets, wide), 0) + 1
    return jnp.where(codes.astype(jnp.int32) == slots, 1.0, 0.0).astype(BF16)


def thirds(x):
    hi = x.astype(BF16)
    rest = x - hi.astype(F32)
    mid = rest.astype(BF16)
    low = (rest - mid.astype(F32)).astype(BF16)
    return jnp.concatenate([hi.astype(F32), mid.astype(F32), low.astype(F32)], axis=0).astype(BF16)


def by_offset(split, codes, z):
    got = dot(split, onehot_of(codes, z), NN)
    total = got[0:8] + got[8:16] + got[16:24]
    return total + jnp.where(codes == 0.0, NEG, 0.0)


def masked_pair(x, z):
    lane = lax.broadcasted_iota(jnp.int32, x.shape, 1)
    zero = jnp.zeros_like(x)
    return jnp.concatenate([jnp.where(lane < z.hd, x, zero), jnp.where(lane < z.hd, zero, x)], axis=0)


def toeplitz(row, z):
    base = pltpu.roll(jnp.broadcast_to(row, (8, 2 * z.tok)), z.tok + 1, 1, stride=1, stride_axis=0)
    tiles = [pltpu.roll(base, 8 * g, 1)[:, : z.tok] if g else base[:, : z.tok] for g in range(z.tok // 8)]
    return jnp.concatenate(tiles, axis=0)


def diagonals(x, z):
    tok = z.tok
    lane = lax.broadcasted_iota(jnp.int32, (8, tok), 1)
    low = jnp.zeros((8, tok), F32)
    high = jnp.zeros((8, tok), F32)
    for g in range(tok // 8):
        by = tok - 8 - 8 * g
        part = x[8 * g : 8 * g + 8]
        if by:
            part = pltpu.roll(part, by, 1)
            low = low + jnp.where(lane >= by, part, 0.0)
            high = high + jnp.where(lane < by, part, 0.0)
        else:
            low = low + part
    both = jnp.concatenate([low, high], axis=1)
    left = 7 - lax.broadcasted_iota(jnp.int32, both.shape, 0)
    for bit in (1, 2, 4):
        both = jnp.where((left & bit) != 0, pltpu.roll(both, bit, 1), both)
    return both.sum(axis=0, keepdims=True)


def causal(z):
    row = lax.broadcasted_iota(jnp.int32, (z.tok, 2 * z.tok), 0)
    col = lax.broadcasted_iota(jnp.int32, (z.tok, 2 * z.tok), 1) % z.tok
    return row <= col


def bias_tile(boff, base, pair, z):
    rows = [toeplitz(boff[pl.ds(base + 2 * pair + e, 1), :], z) for e in range(2)]
    return jnp.concatenate(rows, axis=1)


def prep_kernel(z, me_ref, *refs):
    chunks, table = refs[: z.group], refs[z.group]
    qm, dom, boff, codes = refs[z.group + 1 :]
    for k in range(z.group):
        j = me_ref[0] ^ k
        codes[at(j * CODE_ROWS, CODE_ROWS), :] = chunks[k][2 * z.tok :, :].astype(F32)
        for pair in range(z.pairs):
            lanes = slice(pair * 128, (pair + 1) * 128)
            q = chunks[k][0 : z.tok, lanes] * jnp.asarray(z.scale, BF16)
            qm[j * z.pairs + pair] = masked_pair(q, z)
            dom[j * z.pairs + pair] = masked_pair(chunks[k][z.tok : 2 * z.tok, lanes], z)
    split = thirds(table[...])
    for i in range(z.group):
        for s in range(z.span):
            row = codes[i * CODE_ROWS + s : i * CODE_ROWS + s + 1, :]
            boff[(i * z.span + s) * 8 : (i * z.span + s) * 8 + 8, :] = by_offset(split, row, z)


def stats_kernel(z, me_ref, *refs):
    chunks, halo, qm, dom, boff = refs[: z.group], *refs[z.group : z.group + 4]
    stats, kx, vx, held = refs[z.group + 4 :]
    tok = z.tok
    for b in range(z.halo):
        kx[b * tok : (b + 1) * tok, :] = halo[2 * b * tok : (2 * b + 1) * tok, :]
        vx[b * tok : (b + 1) * tok, :] = halo[(2 * b + 1) * tok : (2 * b + 2) * tok, :]
    for k in range(z.group):
        rows = at(((me_ref[0] ^ k) + z.halo) * tok, tok)
        kx[rows, :] = chunks[k][0:tok, :]
        vx[rows, :] = chunks[k][tok : 2 * tok, :]

    def unit(u, _):
        i, pair = u // z.pairs, u % z.pairs
        lanes = at(pair * 128, 128)
        q, d = qm[u], dom[u]
        most = jnp.full((8, 2 * tok), NEG, F32)
        for t in range(z.span):
            s = z.span - 1 - t
            scores = dot(kx[at((i + t) * tok, tok), lanes], q, NT)
            scores = scores + bias_tile(boff, (i * z.span + s) * 8, pair, z)
            if s == 0:
                scores = jnp.where(causal(z), scores, NEG)
            held[t * tok : (t + 1) * tok, :] = scores
            most = jnp.maximum(most, scores.reshape(tok // 8, 8, 2 * tok).max(axis=0))
        top = most.max(axis=0, keepdims=True)
        total = jnp.zeros((8, 2 * tok), F32)
        accum = jnp.zeros((8, 2 * tok), F32)
        for t in range(z.span):
            weights = jnp.exp(held[t * tok : (t + 1) * tok, :] - top)
            dprob = dot(vx[at((i + t) * tok, tok), lanes], d, NT)
            total = total + weights.reshape(tok // 8, 8, 2 * tok).sum(axis=0)
            accum = accum + (weights * dprob).reshape(tok // 8, 8, 2 * tok).sum(axis=0)
        total = total.sum(axis=0, keepdims=True)
        accum = accum.sum(axis=0, keepdims=True)
        stats[0, pl.ds(u, 1), :] = top + jnp.log(total)
        stats[1, pl.ds(u, 1), :] = accum / total
        return 0

    lax.fori_loop(0, z.group * z.pairs, unit, 0)


def tile_terms(z, key, value, q, d, bias, lse, delta, diagonal):
    scores = dot(key, q, NT) + bias
    if diagonal:
        scores = jnp.where(causal(z), scores, NEG)
    prob = jnp.exp(scores - lse)
    dscore = prob * (dot(value, d, NT) - delta)
    return prob, dscore


def own_kernel(z, me_ref, kx, vx, qm, dom, boff, stats, codes, *refs):
    dk, dv, gb = refs[:3]
    sends = refs[3 : 3 + z.group]
    dkx, dvx, kt, p16, s16, dq, offs = refs[3 + z.group :]
    tok, span = z.tok, z.span
    dkx[...] = jnp.zeros_like(dkx)
    dvx[...] = jnp.zeros_like(dvx)
    for j in range(z.ext):
        for pair in range(z.pairs):
            block = kx[j * tok : (j + 1) * tok, pair * 128 : (pair + 1) * 128]
            kt[pair, :, j * tok : (j + 1) * tok] = block.T

    def unit(u, _):
        i, pair = u // z.pairs, u % z.pairs
        lanes = at(pair * 128, 128)
        q, d = qm[u], dom[u]
        lse, delta = stats[0, pl.ds(u, 1), :], stats[1, pl.ds(u, 1), :]
        for t in range(span):
            s = span - 1 - t
            rows = at((i + t) * tok, tok)
            base = (i * span + s) * 8
            prob, dscore = tile_terms(
                z, kx[rows, lanes], vx[rows, lanes], q, d, bias_tile(boff, base, pair, z), lse, delta, s == 0
            )
            p16[t * tok : (t + 1) * tok, :] = prob.astype(BF16)
            s16[t * tok : (t + 1) * tok, :] = dscore.astype(BF16)
            for e in range(2):
                offs[pl.ds(base + 2 * pair + e, 1), :] = diagonals(dscore[:, e * tok : (e + 1) * tok], z)
        window = pl.ds(pl.multiple_of(i * tok, tok), span * tok)
        dkx[window, lanes] += dot(s16[...], q, NN)
        dvx[window, lanes] += dot(p16[...], d, NN)
        cross = dot(kt[pair, :, window], s16[...], NN)
        both = jnp.concatenate([cross[0 : z.hd, 0:tok], cross[z.hd :, tok:]], axis=0)
        dq[at(i * tok, tok), lanes] = (z.scale * both.T).astype(BF16)
        return 0

    offs[...] = jnp.zeros_like(offs)
    lax.fori_loop(0, z.group * z.pairs, unit, 0)
    dk[...] = dkx[z.halo * tok :, :]
    dv[...] = dvx[z.halo * tok :, :]
    for k in range(z.group):
        sends[k][...] = dq[at((me_ref[0] ^ k) * tok, tok), :]
    total = jnp.zeros((8, z.buckets), F32)
    for i in range(z.group):
        for s in range(span):
            row = codes[i * CODE_ROWS + s : i * CODE_ROWS + s + 1, :]
            base = (i * span + s) * 8
            got = dot(thirds(offs[base : base + 8, :]), onehot_of(row, z), NT)
            total = total + (got[0:8] + got[8:16] + got[16:24])
    mine = jnp.concatenate([total[0 : z.hg]] * (gb.shape[0] // z.hg), axis=0)
    owner = lax.broadcasted_iota(jnp.int32, gb.shape, 0) // z.hg
    gb[...] = jnp.where(owner == me_ref[1] * z.group + me_ref[0], mine, 0.0)


def tail_kernel(z, me_ref, kx, vx, halo, stats, table, dk, dv, *refs):
    sends = refs[: z.group]
    dkx, dvx, boff = refs[z.group :]
    tok, span = z.tok, z.span
    split = thirds(table[...])
    dkx[...] = dk[...]
    dvx[...] = dv[...]
    for b in range(z.halo):
        codes = halo[b * z.qrows + 2 * tok : (b + 1) * z.qrows, :].astype(F32)
        for s in range(b + 1, span):
            boff[(b * span + s) * 8 : (b * span + s) * 8 + 8, :] = by_offset(split, codes[s : s + 1, :], z)

    def each(pair, _):
        lanes = at(pair * 128, 128)
        for b in range(z.halo):
            top = b * z.qrows
            q = masked_pair(halo[top : top + tok, lanes] * jnp.asarray(z.scale, BF16), z)
            d = masked_pair(halo[top + tok : top + 2 * tok, lanes], z)
            u = b * z.pairs + pair
            lse, delta = stats[0, pl.ds(u, 1), :], stats[1, pl.ds(u, 1), :]
            for s in range(b + 1, span):
                j = z.group + b - s
                rows = slice((j + z.halo) * tok, (j + z.halo + 1) * tok)
                mine = slice(j * tok, (j + 1) * tok)
                bias = bias_tile(boff, (b * span + s) * 8, pair, z)
                prob, dscore = tile_terms(z, kx[rows, lanes], vx[rows, lanes], q, d, bias, lse, delta, False)
                dkx[mine, lanes] += dot(dscore.astype(BF16), q, NN)
                dvx[mine, lanes] += dot(prob.astype(BF16), d, NN)
        return 0

    lax.fori_loop(0, z.pairs, each, 0)
    for k in range(z.group):
        rows = at((me_ref[0] ^ k) * tok, tok)
        sends[k][0:tok, :] = dkx[rows, :].astype(BF16)
        sends[k][tok:, :] = dvx[rows, :].astype(BF16)


def unpack_kernel(z, me_ref, *refs):
    grads, queries, outs = refs[: z.group], refs[z.group : 2 * z.group], refs[2 * z.group :]
    for k in range(z.group):
        cols = at((me_ref[0] ^ k) * z.cw, z.cw)
        outs[0][:, cols] = queries[k][...]
        outs[1][:, cols] = grads[k][0 : z.tok, :]
        outs[2][:, cols] = grads[k][z.tok :, :]


def bind(kernel, *fixed):
    def bound(*refs):
        return kernel(*fixed, *refs)

    return bound


def body(queries, keys, values, grad_out, bias_table, bucket_ids, block_mask):
    tok, width = queries.shape
    heads, buckets = bias_table.shape
    span = block_mask.shape[1]
    group = span
    z = Sizes(tok, width, heads, span, buckets, group)
    blocks = lax.axis_size("seq")
    sides = lax.axis_size("head")
    assert blocks % group == 0 and (blocks & (blocks - 1)) == 0 and (sides & (sides - 1)) == 0
    index = lax.axis_index("seq")
    side = lax.axis_index("head")
    me = jnp.stack([index % group, side]).astype(jnp.int32)

    def swap(value, by, axis="seq"):
        return lax.ppermute(value, axis, [(i, i ^ by) for i in range(lax.axis_size(axis))])

    def shifted(value, by):
        return lax.ppermute(value, "seq", [(i, i + by) for i in range(blocks) if 0 <= i + by < blocks])

    steps = jnp.arange(span, dtype=jnp.int32)
    valid = (steps == 0) | ((block_mask[0] == 1) & (index - steps >= 0))
    codes = jnp.where(valid[:, None], bucket_ids[0] + 1, 0)
    codes = jnp.pad(codes, ((0, CODE_ROWS - span), (0, 0))).astype(BF16)
    tables = jnp.pad(bias_table.reshape(group, z.hg, buckets), ((0, 0), (0, 8 - z.hg), (0, 0)))
    table = lax.dynamic_index_in_dim(tables, index % group, 0, keepdims=False)

    kv = call(bind(pack_kernel, z, 2), [((2 * tok, z.cw), BF16)] * group, (me, keys, values), name="pack_kv")
    kv_got = [kv[0]] + [swap(kv[k], k) for k in range(1, group)]
    qd = call(
        bind(pack_kernel, z, 3), [((z.qrows, z.cw), BF16)] * group, (me, queries, grad_out, codes), name="pack_qd"
    )
    qd_got = [qd[0]] + [swap(qd[k], k) for k in range(1, group)]
    (kv_out,) = call(
        bind(halo_kernel, z, 2 * tok, group - z.halo), [((z.halo * 2 * tok, z.cw), BF16)], (me, *kv_got), name="halo_kv"
    )
    kv_halo = shifted(kv_out, group)
    (qd_out,) = call(
        bind(halo_kernel, z, z.qrows, 0), [((z.halo * z.qrows, z.cw), BF16)], (me, *qd_got), name="halo_qd"
    )
    qd_halo = shifted(qd_out, -group)

    units = group * z.pairs
    wide = 2 * tok
    qm, dom, boff, own_codes = call(
        bind(prep_kernel, z),
        [
            ((units, 2 * tok, 128), BF16),
            ((units, 2 * tok, 128), BF16),
            ((group * span * 8, wide), F32),
            ((group * CODE_ROWS, wide), F32),
        ],
        (me, *qd_got, table),
        name="prep",
    )
    stats, kx, vx = call(
        bind(stats_kernel, z),
        [((2, units, wide), F32), ((z.ext * tok, z.cw), BF16), ((z.ext * tok, z.cw), BF16)],
        (me, *kv_got, kv_halo, qm, dom, boff),
        scratch=[pltpu.VMEM((span * tok, wide), F32)],
        flops=2 * units * span * 2 * tok * wide * 128,
        name="stats",
    )
    stats_halo = shifted(stats, -group)
    dk, dv, gb, *dq = call(
        bind(own_kernel, z),
        [((group * tok, z.cw), F32)] * 2 + [((heads * sides, buckets), F32)] + [((tok, z.cw), BF16)] * group,
        (me, kx, vx, qm, dom, boff, stats, own_codes),
        scratch=[
            pltpu.VMEM((z.ext * tok, z.cw), F32),
            pltpu.VMEM((z.ext * tok, z.cw), F32),
            pltpu.VMEM((z.pairs, 128, z.ext * tok), BF16),
            pltpu.VMEM((span * tok, wide), BF16),
            pltpu.VMEM((span * tok, wide), BF16),
            pltpu.VMEM((group * tok, z.cw), BF16),
            pltpu.VMEM((group * span * 8, wide), F32),
        ],
        flops=2 * units * span * 5 * tok * wide * 128,
        name="own",
    )
    dq_got = [dq[0]] + [swap(dq[k], k) for k in range(1, group)]
    by = group
    while by < blocks:
        if by * 2 < blocks:
            gb = (gb + swap(gb, by)) + (swap(gb, 2 * by) + swap(gb, 3 * by))
            by *= 4
        else:
            gb = gb + swap(gb, by)
            by *= 2
    ret = call(
        bind(tail_kernel, z),
        [((2 * tok, z.cw), BF16)] * group,
        (me, kx, vx, qd_halo, stats_halo, table, dk, dv),
        scratch=[
            pltpu.VMEM((group * tok, z.cw), F32),
            pltpu.VMEM((group * tok, z.cw), F32),
            pltpu.VMEM((z.halo * span * 8, wide), F32),
        ],
        flops=2 * 6 * z.pairs * 4 * tok * wide * 128,
        name="tail",
    )
    ret_got = [ret[0]] + [swap(ret[k], k) for k in range(1, group)]
    more = gb
    for k in range(1, group):
        more = more + swap(gb, k)
    gb = more
    by = 1
    while by < sides:
        gb = gb + swap(gb, by, "head")
        by *= 2
    grad_q, grad_k, grad_v = call(
        bind(unpack_kernel, z), [((tok, width), BF16)] * 3, (me, *ret_got, *dq_got), name="unpack"
    )
    return grad_q, grad_k, grad_v, gb


def solution(mesh):
    placed = (
        P("seq", "head"),
        P("seq", "head"),
        P("seq", "head"),
        P("seq", "head"),
        P("head", None),
        P("seq", None, None),
        P("seq", None),
    )
    return jax.shard_map(
        body,
        mesh=mesh,
        in_specs=placed,
        out_specs=(P("seq", "head"), P("seq", "head"), P("seq", "head"), P()),
        check_vma=False,
    )
```

```python
import math

import jax
import jax.numpy as jnp
from jax import lax
from jax.experimental import pallas as pl
from jax.experimental.pallas import tpu as pltpu
from jax.sharding import PartitionSpec as P

F32 = jnp.float32
BF16 = jnp.bfloat16
NEG = -1e30
NT = (((1,), (1,)), ((), ()))
NN = (((1,), (0,)), ((), ()))
CODE_ROWS = 16


def dot(a, b, dims):
    return lax.dot_general(a, b, dims, preferred_element_type=F32)


def at(start, size):
    return pl.ds(pl.multiple_of(start, size), size)


def call(kernel, outs, args, name, scratch=(), spaces=None, out_space=pltpu.VMEM, flops=0, limit=16 << 20):
    spaces = spaces or [pltpu.VMEM] * len(args)
    moved = sum(a.size * a.dtype.itemsize for a in args)
    args = [
        pltpu.with_memory_space_constraint(a, s) if s == pltpu.VMEM else a for a, s in zip(args, spaces, strict=True)
    ]
    return pl.pallas_call(
        kernel,
        out_shape=tuple(out_space(s, d) for s, d in outs),
        in_specs=[pl.BlockSpec(memory_space=s) for s in spaces],
        out_specs=tuple(pl.BlockSpec(memory_space=out_space) for _ in outs),
        scratch_shapes=list(scratch),
        compiler_params=pltpu.CompilerParams(vmem_limit_bytes=limit),
        cost_estimate=pl.CostEstimate(flops=flops, bytes_accessed=moved, transcendentals=0),
        name=name,
    )(*args)


class Sizes:
    def __init__(self, tok, width, heads, span, buckets, group):
        self.tok, self.width, self.heads, self.span, self.buckets = tok, width, heads, span, buckets
        self.group = group
        self.hd = width // heads
        self.hg = heads // group
        self.cw = self.hg * self.hd
        self.pairs = self.hg // 2
        self.scale = self.hd ** (-0.5)
        self.halo = span - 1
        self.ext = group + self.halo
        self.wide = 2 * tok
        self.qrows = 2 * tok + CODE_ROWS
        self.near = [(i, s) for i in range(group) for s in range(span) if s <= i]
        self.far = [(i, s) for i in range(group) for s in range(span) if s > i]
        assert heads % group == 0 and self.hg % 2 == 0 and 2 * self.hd == 128
        assert tok == 128 and buckets == 128 and group >= self.halo and self.hg <= 8
        assert math.frexp(self.scale)[0] == 0.5

    def me(self):
        return lax.rem(lax.axis_index("seq"), self.group)


def pack_kernel(z, q, k, v, d, ids, mask, *refs):
    kv, qd, sem = refs[: z.group], refs[z.group : 2 * z.group], refs[2 * z.group]
    index = lax.axis_index("seq")
    me = z.me()
    copies = []
    for g in range(z.group):
        cols = at((me ^ g) * z.cw, z.cw)
        for n, (src, dst) in enumerate(((k, kv), (v, kv), (q, qd), (d, qd))):
            rows = pl.ds((n % 2) * z.tok, z.tok)
            copies.append(pltpu.make_async_copy(src.at[:, cols], dst[g].at[rows, :], sem.at[len(copies)]))
    for copy in copies:
        copy.start()
    rows = []
    for s in range(z.span):
        valid = True if s == 0 else (mask[0, s] == 1) & (index >= s)
        rows.append(jnp.where(valid, ids[0, s : s + 1, :] + 1, 0))
    rows.append(jnp.zeros((CODE_ROWS - z.span, z.wide), jnp.int32))
    codes = jnp.concatenate(rows, axis=0).astype(F32).astype(BF16)
    for g in range(z.group):
        qd[g][2 * z.tok :, :] = codes
    for copy in copies:
        copy.wait()


def halo_kernel(z, rows, first, *refs):
    out = refs[-1]
    me = z.me()
    for k in range(z.group):
        j = me ^ k

        @pl.when((j >= first) & (j < first + z.halo))
        def _():
            out[at((j - first) * rows, rows), :] = refs[k][...]


def onehot_of(codes, z):
    slots = lax.broadcasted_iota(jnp.int32, (z.buckets, codes.shape[1]), 0) + 1
    return jnp.where(codes.astype(jnp.int32) == slots, 1.0, 0.0).astype(BF16)


def thirds(x):
    hi = x.astype(BF16)
    rest = x - hi.astype(F32)
    mid = rest.astype(BF16)
    low = (rest - mid.astype(F32)).astype(BF16)
    return jnp.concatenate([hi.astype(F32), mid.astype(F32), low.astype(F32)], axis=0).astype(BF16)


def by_offset(split, codes, z):
    got = dot(split, onehot_of(codes, z), NN)
    return got[0:8] + got[8:16] + got[16:24] + jnp.where(codes == 0.0, NEG, 0.0)


def masked_pair(x, z):
    lane = lax.broadcasted_iota(jnp.int32, x.shape, 1)
    zero = jnp.zeros_like(x)
    return jnp.concatenate([jnp.where(lane < z.hd, x, zero), jnp.where(lane < z.hd, zero, x)], axis=0)


def toeplitz(row, z):
    base = pltpu.roll(jnp.broadcast_to(row, (8, z.wide)), z.tok + 1, 1, stride=1, stride_axis=0)
    tiles = [pltpu.roll(base, 8 * g, 1)[:, : z.tok] if g else base[:, : z.tok] for g in range(z.tok // 8)]
    return jnp.concatenate(tiles, axis=0)


def diagonals(x, z):
    tok = z.tok
    lane = lax.broadcasted_iota(jnp.int32, (8, tok), 1)
    total = x[tok - 8 :]
    high = jnp.zeros((8, tok), F32)
    for g in range(tok // 8 - 1):
        by = tok - 8 - 8 * g
        part = pltpu.roll(x[8 * g : 8 * g + 8], by, 1)
        total = total + part
        high = high + jnp.where(lane < by, part, 0.0)
    both = jnp.concatenate([total - high, high], axis=1)
    left = 7 - lax.broadcasted_iota(jnp.int32, both.shape, 0)
    for bit in (1, 2, 4):
        both = jnp.where((left & bit) != 0, pltpu.roll(both, bit, 1), both)
    return both.sum(axis=0, keepdims=True)


def causal(z):
    row = lax.broadcasted_iota(jnp.int32, (z.tok, z.wide), 0)
    col = lax.broadcasted_iota(jnp.int32, (z.tok, z.wide), 1) % z.tok
    return row <= col


def folded(x, how):
    return how(how(x.reshape(x.shape[0] // 8, 8, x.shape[1]), 0), 0, keepdims=True)


def biased_scores(z, key, q, boff, base, pair, diagonal):
    scores = dot(key, q, NT)
    rows = [toeplitz(boff[pl.ds(base + 2 * pair + e, 1), :], z) for e in range(2)]
    scores = scores + jnp.concatenate(rows, axis=1)
    return jnp.where(causal(z), scores, NEG) if diagonal else scores


def forward_tile(z, key, value, q, d, boff, base, pair, diagonal, at_row, outs):
    weights, dprobs, tops, totals, accums = outs
    scores = biased_scores(z, key, q, boff, base, pair, diagonal)
    top = folded(scores, jnp.max)
    w = jnp.exp(scores - top)
    dprob = dot(value, d, NT)
    weights[at_row] = w
    dprobs[at_row] = dprob
    tops[pl.ds(at_row, 1), :] = top
    totals[pl.ds(at_row, 1), :] = folded(w, jnp.sum)
    accums[pl.ds(at_row, 1), :] = folded(w * dprob, jnp.sum)


def near_kernel(z, *refs):
    kv, qd, table = refs[: z.group], refs[z.group : 2 * z.group], refs[2 * z.group]
    keys, values, qm, dom, boff, codes, *outs = refs[2 * z.group + 1 :]
    tok = z.tok
    me = z.me()
    for k in range(z.group):
        j = me ^ k
        keys[at(j * tok, tok), :] = kv[k][0:tok, :]
        values[at(j * tok, tok), :] = kv[k][tok:, :]
        codes[at(j * CODE_ROWS, CODE_ROWS), :] = qd[k][2 * tok :, :].astype(F32)
        for pair in range(z.pairs):
            lanes = slice(pair * 128, (pair + 1) * 128)
            rows = at(j * z.wide, z.wide)
            qm[pair, rows, :] = masked_pair(qd[k][0:tok, lanes] * jnp.asarray(z.scale, BF16), z)
            dom[pair, rows, :] = masked_pair(qd[k][tok : 2 * tok, lanes], z)
    split = thirds(table[...])
    for i in range(z.group):
        for s in range(z.span):
            row = codes[i * CODE_ROWS + s : i * CODE_ROWS + s + 1, :]
            boff[(i * z.span + s) * 8 : (i * z.span + s) * 8 + 8, :] = by_offset(split, row, z)

    def each(pair, _):
        lanes = at(pair * 128, 128)
        for t, (i, s) in enumerate(z.near):
            rows = slice((i - s) * tok, (i - s + 1) * tok)
            wide = slice(i * z.wide, (i + 1) * z.wide)
            forward_tile(
                z, keys[rows, lanes], values[rows, lanes], qm[pair, wide, :], dom[pair, wide, :],
                boff, (i * z.span + s) * 8, pair, s == 0, t * z.pairs + pair, outs,
            )
        return 0

    lax.fori_loop(0, z.pairs, each, 0)


def far_kernel(z, halo, qm, dom, boff, tops, totals, accums, stats, fnear, ffar, *outs):
    tok = z.tok

    def each(pair, _):
        lanes = at(pair * 128, 128)
        for t, (i, s) in enumerate(z.far):
            b = z.halo + i - s
            wide = slice(i * z.wide, (i + 1) * z.wide)
            forward_tile(
                z, halo[2 * b * tok : (2 * b + 1) * tok, lanes], halo[(2 * b + 1) * tok : (2 * b + 2) * tok, lanes],
                qm[pair, wide, :], dom[pair, wide, :],
                boff, (i * z.span + s) * 8, pair, False, t * z.pairs + pair, outs,
            )
        for i in range(z.group):
            mine = [(tops, totals, accums, fnear, t) for t, (n, _) in enumerate(z.near) if n == i]
            mine += [(outs[2], outs[3], outs[4], ffar, t) for t, (n, _) in enumerate(z.far) if n == i]
            rows = [pl.ds(t * z.pairs + pair, 1) for *_, t in mine]
            peaks = [m[0][row, :] for m, row in zip(mine, rows, strict=True)]
            top = peaks[0]
            for peak in peaks[1:]:
                top = jnp.maximum(top, peak)
            total = jnp.zeros_like(top)
            accum = jnp.zeros_like(top)
            for m, row, peak in zip(mine, rows, peaks, strict=True):
                share = jnp.exp(peak - top)
                total = total + share * m[1][row, :]
                accum = accum + share * m[2][row, :]
            lse = top + jnp.log(total)
            for m, row, peak in zip(mine, rows, peaks, strict=True):
                m[3][row, :] = jnp.exp(peak - lse)
            stats[0, pl.ds(i * z.pairs + pair, 1), :] = lse
            stats[1, pl.ds(i * z.pairs + pair, 1), :] = accum / total
        return 0

    lax.fori_loop(0, z.pairs, each, 0)


def own_kernel(z, keys, halo, codes, stats, fnear, ffar, wnear, dnear, wfar, dfar, *refs):
    p16, s16, dq, gb, offs = refs
    tok, span = z.tok, z.span
    offs[...] = jnp.zeros_like(offs)

    def each(pair, _):
        lanes = at(pair * 128, 128)
        blocks = [halo[2 * b * tok : (2 * b + 1) * tok, lanes] for b in range(z.halo)]
        blocks += [keys[j * tok : (j + 1) * tok, lanes] for j in range(z.group)]
        turned = jnp.concatenate([block.T for block in blocks], axis=1)
        for i in range(z.group):
            wide = slice(i * z.wide, (i + 1) * z.wide)
            delta = stats[1, pl.ds(i * z.pairs + pair, 1), :]
            parts = []
            for s in reversed(range(span)):
                close = s <= i
                t = (z.near if close else z.far).index((i, s)) * z.pairs + pair
                w, d, f = (wnear, dnear, fnear) if close else (wfar, dfar, ffar)
                prob = w[t] * f[pl.ds(t, 1), :]
                dscore = prob * (d[t] - delta)
                half = dscore.astype(BF16)
                parts.append(half)
                if close:
                    rows = slice((i - s) * tok, (i - s + 1) * tok)
                    p16[pair, rows, wide] = prob.astype(BF16)
                    s16[pair, rows, wide] = half
                for e in range(2):
                    row = pl.ds((i * span + s) * 8 + 2 * pair + e, 1)
                    offs[row, :] = diagonals(dscore[:, e * tok : (e + 1) * tok], z)
            cross = dot(turned[:, i * tok : (i + span) * tok], jnp.concatenate(parts, axis=0), NN)
            both = jnp.concatenate([cross[0 : z.hd, 0:tok], cross[z.hd :, tok:]], axis=0)
            dq[i * tok : (i + 1) * tok, lanes] = (z.scale * both.T).astype(BF16)
        return 0

    lax.fori_loop(0, z.pairs, each, 0)
    total = jnp.zeros((8, z.buckets), F32)
    for i in range(z.group):
        for s in range(span):
            row = codes[i * CODE_ROWS + s : i * CODE_ROWS + s + 1, :]
            base = (i * span + s) * 8
            got = dot(thirds(offs[base : base + 8, :]), onehot_of(row, z), NT)
            total = total + (got[0:8] + got[8:16] + got[16:24])
    mine = jnp.concatenate([total[0 : z.hg]] * (gb.shape[0] // z.hg), axis=0)
    owner = lax.broadcasted_iota(jnp.int32, gb.shape, 0) // z.hg
    gb[...] = jnp.where(owner == lax.axis_index("head") * z.group + z.me(), mine, 0.0)


def tail_kernel(z, keys, values, qm, dom, p16, s16, dq, halo, stats, table, *refs):
    sends = refs[: z.group]
    qh, dh, ph, sh, boff, dk, dv = refs[z.group :]
    tok, span = z.tok, z.span
    split = thirds(table[...])
    for b in range(z.halo):
        codes = halo[b * z.qrows + 2 * tok : (b + 1) * z.qrows, :].astype(F32)
        for s in range(b + 1, span):
            boff[(b * span + s) * 8 : (b * span + s) * 8 + 8, :] = by_offset(split, codes[s : s + 1, :], z)

    def each(pair, _):
        lanes = at(pair * 128, 128)
        for b in range(z.halo):
            top = b * z.qrows
            wide = slice(b * z.wide, (b + 1) * z.wide)
            q = masked_pair(halo[top : top + tok, lanes] * jnp.asarray(z.scale, BF16), z)
            d = masked_pair(halo[top + tok : top + 2 * tok, lanes], z)
            qh[wide, :] = q
            dh[wide, :] = d
            u = b * z.pairs + pair
            lse, delta = stats[0, pl.ds(u, 1), :], stats[1, pl.ds(u, 1), :]
            for s in range(b + 1, span):
                j = z.group + b - s
                rows = slice(j * tok, (j + 1) * tok)
                scores = biased_scores(z, keys[rows, lanes], q, boff, (b * span + s) * 8, pair, False)
                prob = jnp.exp(scores - lse)
                dscore = prob * (dot(values[rows, lanes], d, NT) - delta)
                ph[rows, wide] = prob.astype(BF16)
                sh[rows, wide] = dscore.astype(BF16)
        for j in range(z.group):
            rows = slice(j * tok, (j + 1) * tok)
            near = slice(j * z.wide, z.group * z.wide)
            gk = dot(s16[pair, rows, near], qm[pair, near, :], NN)
            gv = dot(p16[pair, rows, near], dom[pair, near, :], NN)
            count = min(z.halo, j + span - z.group)
            if count > 0:
                past = slice(0, count * z.wide)
                gk = gk + dot(sh[rows, past], qh[past, :], NN)
                gv = gv + dot(ph[rows, past], dh[past, :], NN)
            dk[rows, lanes] = gk.astype(BF16)
            dv[rows, lanes] = gv.astype(BF16)
        return 0

    lax.fori_loop(0, z.pairs, each, 0)
    me = z.me()
    for k in range(z.group):
        rows = at((me ^ k) * tok, tok)
        for n, ref in enumerate((dq, dk, dv)):
            sends[k][n * tok : (n + 1) * tok, :] = ref[rows, :]


def add_kernel(*refs):
    total = refs[0][...]
    for ref in refs[1:-1]:
        total = total + ref[...]
    refs[-1][...] = total


def unpack_kernel(z, parts, *refs):
    got, sums = refs[: z.group], refs[z.group : z.group + parts]
    outs, gb, held, sem = refs[z.group + parts : -3], refs[-3], refs[-2], refs[-1]
    me = z.me()
    copies = []
    for k in range(z.group):
        cols = at((me ^ k) * z.cw, z.cw)
        for n, out in enumerate(outs):
            src = got[k].at[n * z.tok : (n + 1) * z.tok, :]
            copies.append(pltpu.make_async_copy(src, out.at[:, cols], sem.at[len(copies)]))
    for copy in copies:
        copy.start()
    add_kernel(*sums, held)
    last = pltpu.make_async_copy(held, gb, sem.at[len(copies)])
    last.start()
    for copy in copies + [last]:
        copy.wait()


def bind(kernel, *fixed):
    def bound(*refs):
        return kernel(*fixed, *refs)

    return bound


def body(queries, keys, values, grad_out, bias_table, bucket_ids, block_mask):
    tok, width = queries.shape
    heads, buckets = bias_table.shape
    span = block_mask.shape[1]
    group = span
    z = Sizes(tok, width, heads, span, buckets, group)
    blocks = lax.axis_size("seq")
    sides = lax.axis_size("head")
    assert blocks % group == 0 and (blocks & (blocks - 1)) == 0 and (sides & (sides - 1)) == 0

    def swap(value, by, axis="seq"):
        return lax.ppermute(value, axis, [(i, i ^ by) for i in range(lax.axis_size(axis))])

    def shifted(value, by):
        return lax.ppermute(value, "seq", [(i, i + by) for i in range(blocks) if 0 <= i + by < blocks])

    def added(*terms):
        (total,) = call(add_kernel, [(terms[0].shape, terms[0].dtype)], terms, name="add")
        return total

    tables = jnp.pad(bias_table.reshape(group, z.hg, buckets), ((0, 0), (0, 8 - z.hg), (0, 0)))
    table = lax.dynamic_index_in_dim(tables, lax.axis_index("seq") % group, 0, keepdims=False)

    hbm = pltpu.HBM
    packed = call(
        bind(pack_kernel, z),
        [((2 * tok, z.cw), BF16)] * group + [((z.qrows, z.cw), BF16)] * group,
        (queries, keys, values, grad_out, bucket_ids, block_mask),
        spaces=[hbm, hbm, hbm, hbm, pltpu.VMEM, pltpu.SMEM],
        scratch=[pltpu.SemaphoreType.DMA((4 * group,))],
        name="pack",
    )
    kv, qd = packed[:group], packed[group:]
    kv_got = [kv[0]] + [swap(kv[k], k) for k in range(1, group)]
    qd_got = [qd[0]] + [swap(qd[k], k) for k in range(1, group)]
    (kv_out,) = call(
        bind(halo_kernel, z, 2 * tok, group - z.halo), [((z.halo * 2 * tok, z.cw), BF16)], kv_got, name="halo_kv"
    )
    kv_halo = shifted(kv_out, group)
    (qd_out,) = call(bind(halo_kernel, z, z.qrows, 0), [((z.halo * z.qrows, z.cw), BF16)], qd_got, name="halo_qd")
    qd_halo = shifted(qd_out, -group)

    def tile_outs(count):
        tile = ((count * z.pairs, tok, z.wide), F32)
        row = ((count * z.pairs, z.wide), F32)
        return [tile, tile, row, row, row]

    near, far = len(z.near), len(z.far)
    unit = 2 * 128 * tok * z.wide
    own_k, own_v, qm, dom, boff, codes, wnear, dnear, *sums = call(
        bind(near_kernel, z),
        [((group * tok, z.cw), BF16)] * 2
        + [((z.pairs, group * z.wide, 128), BF16)] * 2
        + [((group * span * 8, z.wide), F32), ((group * CODE_ROWS, z.wide), F32)]
        + tile_outs(near),
        (*kv_got, *qd_got, table),
        flops=2 * near * z.pairs * unit,
        name="near",
    )
    stats, fnear, ffar, wfar, dfar, *_ = call(
        bind(far_kernel, z),
        [((2, group * z.pairs, z.wide), F32), ((near * z.pairs, z.wide), F32), ((far * z.pairs, z.wide), F32)]
        + tile_outs(far),
        (kv_halo, qm, dom, boff, *sums),
        flops=2 * far * z.pairs * unit,
        name="far",
    )
    stats_halo = shifted(stats, -group)
    p16, s16, dq, gb = call(
        bind(own_kernel, z),
        [((z.pairs, group * tok, group * z.wide), BF16)] * 2
        + [((group * tok, z.cw), BF16), ((heads * sides, buckets), F32)],
        (own_k, kv_halo, codes, stats, fnear, ffar, wnear, dnear, wfar, dfar),
        scratch=[pltpu.VMEM((group * span * 8, z.wide), F32)],
        flops=2 * (near + far) * z.pairs * unit,
        name="own",
    )
    by = group
    while by < blocks:
        if by * 2 < blocks:
            gb = added(gb, swap(gb, by), swap(gb, 2 * by), swap(gb, 3 * by))
            by *= 4
        else:
            gb = added(gb, swap(gb, by))
            by *= 2
    ret = call(
        bind(tail_kernel, z),
        [((3 * tok, z.cw), BF16)] * group,
        (own_k, own_v, qm, dom, p16, s16, dq, qd_halo, stats_halo, table),
        scratch=[
            pltpu.VMEM((z.halo * z.wide, 128), BF16),
            pltpu.VMEM((z.halo * z.wide, 128), BF16),
            pltpu.VMEM((group * tok, z.halo * z.wide), BF16),
            pltpu.VMEM((group * tok, z.halo * z.wide), BF16),
            pltpu.VMEM((z.halo * span * 8, z.wide), F32),
            pltpu.VMEM((group * tok, z.cw), BF16),
            pltpu.VMEM((group * tok, z.cw), BF16),
        ],
        flops=4 * far * z.pairs * unit,
        name="tail",
    )
    ret_got = [ret[0]] + [swap(ret[k], k) for k in range(1, group)]
    gb = added(gb, *[swap(gb, k) for k in range(1, group)])
    terms = [gb] + [swap(gb, k, "head") for k in range(1, sides)]
    return call(
        bind(unpack_kernel, z, len(terms)),
        [((tok, width), BF16)] * 3 + [((heads * sides, buckets), F32)],
        (*ret_got, *terms),
        out_space=hbm,
        scratch=[pltpu.VMEM((heads * sides, buckets), F32), pltpu.SemaphoreType.DMA((3 * group + 1,))],
        name="unpack",
    )


def solution(mesh):
    placed = (
        P("seq", "head"),
        P("seq", "head"),
        P("seq", "head"),
        P("seq", "head"),
        P("head", None),
        P("seq", None, None),
        P("seq", None),
    )
    return jax.shard_map(
        body,
        mesh=mesh,
        in_specs=placed,
        out_specs=(P("seq", "head"), P("seq", "head"), P("seq", "head"), P()),
        check_vma=False,
    )
```

```python
import math

import jax
import jax.numpy as jnp
from jax import lax
from jax.experimental import pallas as pl
from jax.experimental.pallas import tpu as pltpu
from jax.sharding import PartitionSpec as P


F32 = jnp.float32
BF16 = jnp.bfloat16
NEG = -1e30
NT = (((1,), (1,)), ((), ()))
NN = (((1,), (0,)), ((), ()))
CODE_ROWS = 16
VMEM_BYTES = 67043328


def dot(a, b, dims):
    return lax.dot_general(a, b, dims, preferred_element_type=F32)


def at(start, size):
    return pl.ds(pl.multiple_of(start, size), size)


def call(kernel, outs, args, scratch=(), spaces=None, out_space=pltpu.VMEM, flops=0, limit=16 << 20):
    spaces = spaces or [pltpu.VMEM] * len(args)
    moved = sum(a.size * a.dtype.itemsize for a in args)
    args = [
        pltpu.with_memory_space_constraint(a, s) if s == pltpu.VMEM else a for a, s in zip(args, spaces, strict=True)
    ]
    return pl.pallas_call(
        kernel,
        out_shape=tuple(out_space(s, d) for s, d in outs),
        in_specs=[pl.BlockSpec(memory_space=s) for s in spaces],
        out_specs=tuple(pl.BlockSpec(memory_space=out_space) for _ in outs),
        scratch_shapes=list(scratch),
        compiler_params=pltpu.CompilerParams(vmem_limit_bytes=limit),
        cost_estimate=pl.CostEstimate(flops=flops, bytes_accessed=moved, transcendentals=0),
    )(*args)


class Sizes:
    def __init__(self, tok, width, heads, span, buckets, group):
        self.tok, self.width, self.heads, self.span, self.buckets = tok, width, heads, span, buckets
        self.group = group
        self.hd = width // heads
        self.hg = heads // group
        self.cw = self.hg * self.hd
        self.pairs = self.hg // 2
        self.scale = self.hd ** (-0.5)
        self.halo = span - 1
        self.wide = 2 * tok
        self.rows = 2 * tok + CODE_ROWS
        self.near = [(i, s) for i in range(group) for s in range(span) if s <= i]
        self.far = [(i, s) for i in range(group) for s in range(span) if s > i]
        assert heads % group == 0 and self.hg % 2 == 0 and 2 * self.hd == 128
        assert tok == 128 and buckets == 128 and group >= self.halo and self.hg <= 8
        assert math.frexp(self.scale)[0] == 0.5

    def me(self):
        return lax.rem(lax.axis_index("seq"), self.group)


def pack_kernel(z, q, k, v, d, ids, mask, *refs):
    kv, qd = refs[: z.group], refs[z.group : 2 * z.group]
    slots, flags, sem = refs[2 * z.group :]
    index = lax.axis_index("seq")
    me = z.me()
    copies = [
        pltpu.make_async_copy(ids.at[0], slots, sem.at[0]),
        pltpu.make_async_copy(mask, flags, sem.at[1]),
    ]
    for sources, dst in (((k, v), kv), ((q, d), qd)):
        for g in range(z.group):
            cols = at((me ^ g) * z.cw, z.cw)
            for n, src in enumerate(sources):
                rows = pl.ds(n * z.tok, z.tok)
                copies.append(pltpu.make_async_copy(src.at[:, cols], dst[g].at[rows, :], sem.at[len(copies)]))
    for copy in copies:
        copy.start()
    for copy in copies[:2]:
        copy.wait()
    rows = []
    for s in range(z.span):
        valid = True if s == 0 else (flags[0, s] == 1) & (index >= s)
        rows.append(jnp.where(valid, slots[s : s + 1, :] + 1, 0))
    rows.append(jnp.zeros((CODE_ROWS - z.span, z.wide), jnp.int32))
    codes = jnp.concatenate(rows, axis=0).astype(F32).astype(BF16)
    for g in range(z.group):
        kv[g][2 * z.tok :, :] = codes
    for copy in copies[2:]:
        copy.wait()


def kv_halo_kernel(z, *refs):
    out = refs[-1]
    me = z.me()
    first = z.group - z.halo
    for k in range(z.group):
        j = me ^ k

        @pl.when(j >= first)
        def _():
            out[at((j - first) * 2 * z.tok, 2 * z.tok), :] = refs[k][0 : 2 * z.tok, :]


def qd_halo_kernel(z, *refs):
    qd, kv, out = refs[: z.group], refs[z.group : -1], refs[-1]
    me = z.me()
    for k in range(z.group):
        j = me ^ k

        @pl.when(j < z.halo)
        def _():
            top = pl.multiple_of(j * z.rows, 16)
            out[pl.ds(top, 2 * z.tok), :] = qd[k][...]
            out[pl.ds(top + 2 * z.tok, CODE_ROWS), :] = kv[k][2 * z.tok :, :]


def onehot_of(codes, z):
    slots = lax.broadcasted_iota(jnp.int32, (z.buckets, codes.shape[1]), 0) + 1
    return jnp.where(codes.astype(jnp.int32) == slots, 1.0, 0.0).astype(BF16)


def thirds(x):
    hi = x.astype(BF16)
    rest = x - hi.astype(F32)
    mid = rest.astype(BF16)
    low = (rest - mid.astype(F32)).astype(BF16)
    return jnp.concatenate([hi.astype(F32), mid.astype(F32), low.astype(F32)], axis=0).astype(BF16)


def by_offset(split, codes, z):
    got = dot(split, onehot_of(codes, z), NN)
    return got[0:8] + got[8:16] + got[16:24] + jnp.where(codes == 0.0, NEG, 0.0)


def masked_pair(x, z):
    lane = lax.broadcasted_iota(jnp.int32, x.shape, 1)
    zero = jnp.zeros_like(x)
    return jnp.concatenate([jnp.where(lane < z.hd, x, zero), jnp.where(lane < z.hd, zero, x)], axis=0)


def toeplitz(row, z):
    base = pltpu.roll(jnp.broadcast_to(row, (8, z.wide)), z.tok + 1, 1, stride=1, stride_axis=0)
    tiles = [pltpu.roll(base, 8 * g, 1)[:, : z.tok] if g else base[:, : z.tok] for g in range(z.tok // 8)]
    return jnp.concatenate(tiles, axis=0)


def diagonals(x, z):
    tok = z.tok
    lane = lax.broadcasted_iota(jnp.int32, (8, tok), 1)
    total = x[tok - 8 :]
    high = jnp.zeros((8, tok), F32)
    for g in range(tok // 8 - 1):
        by = tok - 8 - 8 * g
        part = pltpu.roll(x[8 * g : 8 * g + 8], by, 1)
        total = total + part
        high = high + jnp.where(lane < by, part, 0.0)
    return total - high, high


def aligned(both):
    left = 7 - (lax.broadcasted_iota(jnp.int32, both.shape, 0) & 7)
    for bit in (1, 2, 4):
        both = jnp.where((left & bit) != 0, pltpu.roll(both, bit, 1), both)
    return both


def causal(z):
    row = lax.broadcasted_iota(jnp.int32, (z.tok, z.wide), 0)
    col = lax.broadcasted_iota(jnp.int32, (z.tok, z.wide), 1) % z.tok
    return row <= col


def folded(x, how):
    return how(how(x.reshape(x.shape[0] // 8, 8, x.shape[1]), 0), 0, keepdims=True)


def bias_rows(z, boff, base, pair):
    rows = [toeplitz(boff[pl.ds(base + 2 * pair + e, 1), :], z) for e in range(2)]
    return jnp.concatenate(rows, axis=1)


def bias_kernel(z, *refs):
    kv, table = refs[: z.group], refs[z.group]
    keys, values, near, far, codes, boff = refs[z.group + 1 :]
    tok = z.tok
    me = z.me()
    for k in range(z.group):
        j = me ^ k
        keys[at(j * tok, tok), :] = kv[k][0:tok, :]
        values[at(j * tok, tok), :] = kv[k][tok : 2 * tok, :]
        codes[at(j * CODE_ROWS, CODE_ROWS), :] = kv[k][2 * tok :, :].astype(F32)
    split = thirds(table[...])
    for i in range(z.group):
        for s in range(z.span):
            row = codes[i * CODE_ROWS + s : i * CODE_ROWS + s + 1, :]
            boff[(i * z.span + s) * 8 : (i * z.span + s) * 8 + 8, :] = by_offset(split, row, z)

    def each(pair, _):
        for tiles, out in ((z.near, near), (z.far, far)):
            for t, (i, s) in enumerate(tiles):
                bias = bias_rows(z, boff, (i * z.span + s) * 8, pair)
                out[t * z.pairs + pair] = jnp.where(causal(z), bias, NEG) if s == 0 else bias
        return 0

    lax.fori_loop(0, z.pairs, each, 0)


def forward_tile(key, value, q, d, bias, row, outs):
    weights, dprobs, tops, totals, accums = outs
    scores = dot(key, q, NT) + bias[row]
    top = folded(scores, jnp.max)
    w = jnp.exp(scores - top)
    dprob = dot(value, d, NT)
    weights[row] = w
    dprobs[row] = dprob
    tops[pl.ds(row, 1), :] = top
    totals[pl.ds(row, 1), :] = folded(w, jnp.sum)
    accums[pl.ds(row, 1), :] = folded(w * dprob, jnp.sum)


def near_kernel(z, *refs):
    qd, keys, values, bias = refs[: z.group], *refs[z.group : z.group + 3]
    qm, dom, *outs = refs[z.group + 3 :]
    tok = z.tok
    me = z.me()
    for k in range(z.group):
        j = me ^ k
        for pair in range(z.pairs):
            lanes = slice(pair * 128, (pair + 1) * 128)
            rows = at(j * z.wide, z.wide)
            qm[pair, rows, :] = masked_pair(qd[k][0:tok, lanes] * jnp.asarray(z.scale, BF16), z)
            dom[pair, rows, :] = masked_pair(qd[k][tok : 2 * tok, lanes], z)

    def each(pair, _):
        lanes = at(pair * 128, 128)
        for t, (i, s) in enumerate(z.near):
            rows = slice((i - s) * tok, (i - s + 1) * tok)
            wide = slice(i * z.wide, (i + 1) * z.wide)
            forward_tile(
                keys[rows, lanes], values[rows, lanes], qm[pair, wide, :], dom[pair, wide, :],
                bias, t * z.pairs + pair, outs,
            )
        return 0

    lax.fori_loop(0, z.pairs, each, 0)


def far_kernel(z, halo, qm, dom, bias, tops, totals, accums, stats, fnear, ffar, *outs):
    tok = z.tok

    def each(pair, _):
        lanes = at(pair * 128, 128)
        for t, (i, s) in enumerate(z.far):
            b = z.halo + i - s
            wide = slice(i * z.wide, (i + 1) * z.wide)
            forward_tile(
                halo[2 * b * tok : (2 * b + 1) * tok, lanes], halo[(2 * b + 1) * tok : (2 * b + 2) * tok, lanes],
                qm[pair, wide, :], dom[pair, wide, :], bias, t * z.pairs + pair, outs,
            )
        for i in range(z.group):
            mine = [(tops, totals, accums, fnear, t) for t, (n, _) in enumerate(z.near) if n == i]
            mine += [(outs[2], outs[3], outs[4], ffar, t) for t, (n, _) in enumerate(z.far) if n == i]
            rows = [pl.ds(t * z.pairs + pair, 1) for *_, t in mine]
            peaks = [m[0][row, :] for m, row in zip(mine, rows, strict=True)]
            top = peaks[0]
            for peak in peaks[1:]:
                top = jnp.maximum(top, peak)
            total = jnp.zeros_like(top)
            accum = jnp.zeros_like(top)
            for m, row, peak in zip(mine, rows, peaks, strict=True):
                share = jnp.exp(peak - top)
                total = total + share * m[1][row, :]
                accum = accum + share * m[2][row, :]
            lse = top + jnp.log(total)
            for m, row, peak in zip(mine, rows, peaks, strict=True):
                m[3][row, :] = jnp.exp(peak - lse)
            stats[0, pl.ds(i * z.pairs + pair, 1), :] = lse
            stats[1, pl.ds(i * z.pairs + pair, 1), :] = accum / total
        return 0

    lax.fori_loop(0, z.pairs, each, 0)


def own_kernel(z, keys, halo, codes, stats, fnear, ffar, wnear, dnear, wfar, dfar, *refs):
    p16, s16, dq, gb, offs = refs
    tok, span = z.tok, z.span

    def each(pair, _):
        lanes = at(pair * 128, 128)
        blocks = [halo[2 * b * tok : (2 * b + 1) * tok, lanes] for b in range(z.halo)]
        blocks += [keys[j * tok : (j + 1) * tok, lanes] for j in range(z.group)]
        turned = jnp.concatenate([block.T for block in blocks], axis=1)
        for i in range(z.group):
            wide = slice(i * z.wide, (i + 1) * z.wide)
            delta = stats[1, pl.ds(i * z.pairs + pair, 1), :]
            parts = []
            for s in reversed(range(span)):
                close = s <= i
                t = (z.near if close else z.far).index((i, s)) * z.pairs + pair
                w, d, f = (wnear, dnear, fnear) if close else (wfar, dfar, ffar)
                prob = w[t] * f[pl.ds(t, 1), :]
                dscore = prob * (d[t] - delta)
                half = dscore.astype(BF16)
                parts.append(half)
                if close:
                    rows = slice((i - s) * tok, (i - s + 1) * tok)
                    p16[pair, rows, wide] = prob.astype(BF16)
                    s16[pair, rows, wide] = half
                for e in range(2):
                    low, high = diagonals(dscore[:, e * tok : (e + 1) * tok], z)
                    row = at(((i * span + s) * z.hg + 2 * pair + e) * 8, 8)
                    offs[row, 0:tok] = low
                    offs[row, tok:] = high
            cross = dot(turned[:, i * tok : (i + span) * tok], jnp.concatenate(parts, axis=0), NN)
            both = jnp.concatenate([cross[0 : z.hd, 0:tok], cross[z.hd :, tok:]], axis=0)
            dq[i * tok : (i + 1) * tok, lanes] = (z.scale * both.T).astype(BF16)
        return 0

    lax.fori_loop(0, z.pairs, each, 0)
    head = lax.broadcasted_iota(jnp.int32, (8, z.wide), 0)

    def bucket(n, total):
        i, s = n // span, n % span
        both = aligned(offs[at(n * z.hg * 8, z.hg * 8), :])
        sums = jnp.zeros((8, z.wide), F32)
        for h in range(z.hg):
            sums = sums + jnp.where(head == h, both[8 * h : 8 * h + 8].sum(axis=0, keepdims=True), 0.0)
        got = dot(thirds(sums), onehot_of(codes[pl.ds(i * CODE_ROWS + s, 1), :], z), NT)
        return total + (got[0:8] + got[8:16] + got[16:24])

    gb[...] = lax.fori_loop(0, z.group * span, bucket, jnp.zeros((8, z.buckets), F32))


def tail_kernel(z, keys, values, qm, dom, p16, s16, halo, stats, table, dk, dv, qh, dh, ph, sh, boff):
    tok, span = z.tok, z.span
    split = thirds(table[...])
    for b in range(z.halo):
        codes = halo[b * z.rows + 2 * tok : (b + 1) * z.rows, :].astype(F32)
        for s in range(b + 1, span):
            boff[(b * span + s) * 8 : (b * span + s) * 8 + 8, :] = by_offset(split, codes[s : s + 1, :], z)

    def each(pair, _):
        lanes = at(pair * 128, 128)
        for b in range(z.halo):
            top = b * z.rows
            wide = slice(b * z.wide, (b + 1) * z.wide)
            q = masked_pair(halo[top : top + tok, lanes] * jnp.asarray(z.scale, BF16), z)
            d = masked_pair(halo[top + tok : top + 2 * tok, lanes], z)
            qh[wide, :] = q
            dh[wide, :] = d
            u = b * z.pairs + pair
            lse, delta = stats[0, pl.ds(u, 1), :], stats[1, pl.ds(u, 1), :]
            for s in range(b + 1, span):
                j = z.group + b - s
                rows = slice(j * tok, (j + 1) * tok)
                scores = dot(keys[rows, lanes], q, NT) + bias_rows(z, boff, (b * span + s) * 8, pair)
                prob = jnp.exp(scores - lse)
                dscore = prob * (dot(values[rows, lanes], d, NT) - delta)
                ph[rows, wide] = prob.astype(BF16)
                sh[rows, wide] = dscore.astype(BF16)
        for j in range(z.group):
            rows = slice(j * tok, (j + 1) * tok)
            near = slice(j * z.wide, z.group * z.wide)
            gk = dot(s16[pair, rows, near], qm[pair, near, :], NN)
            gv = dot(p16[pair, rows, near], dom[pair, near, :], NN)
            count = min(z.halo, j + span - z.group)
            if count > 0:
                past = slice(0, count * z.wide)
                gk = gk + dot(sh[rows, past], qh[past, :], NN)
                gv = gv + dot(ph[rows, past], dh[past, :], NN)
            dk[rows, lanes] = gk.astype(BF16)
            dv[rows, lanes] = gv.astype(BF16)
        return 0

    lax.fori_loop(0, z.pairs, each, 0)


def seal_kernel(z, parts, dq, dk, dv, *refs):
    sums, sends = refs[:parts], refs[parts:]
    tok = z.tok
    total = sums[0][...]
    for ref in sums[1:]:
        total = total + ref[...]
    split = thirds(total).astype(F32)
    low = jnp.concatenate([split[16:24], jnp.zeros((8, z.buckets), F32)], axis=0)
    rows16 = jnp.concatenate([split[0:16], low], axis=1).astype(BF16)
    me = z.me()
    for k in range(z.group):
        rows = at((me ^ k) * tok, tok)
        for n, ref in enumerate((dq, dk, dv)):
            sends[k][n * tok : (n + 1) * tok, :] = ref[rows, :]
        sends[k][3 * tok :, :] = rows16


def add_kernel(*refs):
    total = refs[0][...]
    for ref in refs[1:-1]:
        total = total + ref[...]
    refs[-1][...] = total


def collect_kernel(z, *refs):
    got, out = refs[:-1], refs[-1]
    me = z.me()
    owner = lax.broadcasted_iota(jnp.int32, out.shape, 0) // z.hg
    total = jnp.zeros(out.shape, F32)
    for k in range(z.group):
        rows = got[k][3 * z.tok :, :].astype(F32)
        sums = rows[0:8, 0 : z.buckets] + rows[8:16, 0 : z.buckets] + rows[0:8, z.buckets :]
        wide = jnp.concatenate([sums[0 : z.hg]] * (out.shape[0] // z.hg), axis=0)
        total = total + jnp.where(owner == lax.axis_index("head") * z.group + (me ^ k), wide, 0.0)
    out[...] = total


def unpack_kernel(z, *refs):
    got, outs, sem = refs[: z.group], refs[z.group : -1], refs[-1]
    me = z.me()
    copies = []
    for k in range(z.group):
        cols = at((me ^ k) * z.cw, z.cw)
        for n, out in enumerate(outs):
            src = got[k].at[n * z.tok : (n + 1) * z.tok, :]
            copies.append(pltpu.make_async_copy(src, out.at[:, cols], sem.at[len(copies)]))
    for copy in copies:
        copy.start()
    for copy in copies:
        copy.wait()


def bind(kernel, *fixed):
    def bound(*refs):
        return kernel(*fixed, *refs)

    return bound


def body(queries, keys, values, grad_out, bias_table, bucket_ids, block_mask):
    tok, width = queries.shape
    heads, buckets = bias_table.shape
    span = block_mask.shape[1]
    group = span
    z = Sizes(tok, width, heads, span, buckets, group)
    blocks = lax.axis_size("seq")
    sides = lax.axis_size("head")
    assert blocks % group == 0 and (blocks & (blocks - 1)) == 0 and (sides & (sides - 1)) == 0

    def swap(value, by, axis="seq"):
        return lax.ppermute(value, axis, [(i, i ^ by) for i in range(lax.axis_size(axis))])

    def shifted(value, by):
        return lax.ppermute(value, "seq", [(i, i + by) for i in range(blocks) if 0 <= i + by < blocks])

    def added(*terms):
        (total,) = call(add_kernel, [(terms[0].shape, terms[0].dtype)], terms)
        return total

    tables = jnp.pad(bias_table.reshape(group, z.hg, buckets), ((0, 0), (0, 8 - z.hg), (0, 0)))
    table = lax.dynamic_index_in_dim(tables, lax.axis_index("seq") % group, 0, keepdims=False)

    hbm = pltpu.HBM
    pack_bytes = group * (z.rows + 2 * tok) * z.cw * 2
    packed = call(
        bind(pack_kernel, z),
        [((z.rows, z.cw), BF16)] * group + [((2 * tok, z.cw), BF16)] * group,
        (queries, keys, values, grad_out, bucket_ids, block_mask),
        spaces=[hbm] * 6,
        scratch=[
            pltpu.VMEM((span, z.wide), jnp.int32),
            pltpu.SMEM((1, span), jnp.int32),
            pltpu.SemaphoreType.DMA((4 * group + 2,)),
        ],
        limit=VMEM_BYTES - pack_bytes - (520 << 10),
    )
    kv, qd = packed[:group], packed[group:]
    kv_got = [kv[0]] + [swap(kv[k], k) for k in range(1, group)]
    qd_got = [qd[0]] + [swap(qd[k], k) for k in range(1, group)]
    (kv_out,) = call(bind(kv_halo_kernel, z), [((z.halo * 2 * tok, z.cw), BF16)], kv_got)
    kv_halo = shifted(kv_out, group)
    (qd_out,) = call(bind(qd_halo_kernel, z), [((z.halo * z.rows, z.cw), BF16)], (*qd_got, *kv_got))
    qd_halo = shifted(qd_out, -group)

    def tile_outs(count):
        tile = ((count * z.pairs, tok, z.wide), F32)
        row = ((count * z.pairs, z.wide), F32)
        return [tile, tile, row, row, row]

    near, far = len(z.near), len(z.far)
    unit = 2 * 128 * tok * z.wide
    own_k, own_v, bias_near, bias_far, codes = call(
        bind(bias_kernel, z),
        [((group * tok, z.cw), BF16)] * 2
        + [((near * z.pairs, tok, z.wide), F32), ((far * z.pairs, tok, z.wide), F32)]
        + [((group * CODE_ROWS, z.wide), F32)],
        (*kv_got, table),
        scratch=[pltpu.VMEM((group * span * 8, z.wide), F32)],
    )
    qm, dom, wnear, dnear, *sums = call(
        bind(near_kernel, z),
        [((z.pairs, group * z.wide, 128), BF16)] * 2 + tile_outs(near),
        (*qd_got, own_k, own_v, bias_near),
        flops=2 * near * z.pairs * unit,
    )
    stats, fnear, ffar, wfar, dfar, *_ = call(
        bind(far_kernel, z),
        [((2, group * z.pairs, z.wide), F32), ((near * z.pairs, z.wide), F32), ((far * z.pairs, z.wide), F32)]
        + tile_outs(far),
        (kv_halo, qm, dom, bias_far, *sums),
        flops=2 * far * z.pairs * unit,
    )
    stats_halo = lax.ppermute(stats, "seq", [(i, (i - group) % blocks) for i in range(blocks)])
    p16, s16, dq, gb = call(
        bind(own_kernel, z),
        [((z.pairs, group * tok, group * z.wide), BF16)] * 2
        + [((group * tok, z.cw), BF16), ((8, buckets), F32)],
        (own_k, kv_halo, codes, stats, fnear, ffar, wnear, dnear, wfar, dfar),
        scratch=[pltpu.VMEM((group * span * z.hg * 8, z.wide), F32)],
        flops=2 * (near + far) * z.pairs * unit,
    )
    terms = [gb]
    by = group
    while by < blocks:
        if len(terms) > 1:
            terms = [added(*terms)]
        ways = 4 if by * 2 < blocks else 2
        terms += [swap(terms[0], by * n) for n in range(1, ways)]
        by *= ways
    dk, dv = call(
        bind(tail_kernel, z),
        [((group * tok, z.cw), BF16)] * 2,
        (own_k, own_v, qm, dom, p16, s16, qd_halo, stats_halo, table),
        scratch=[
            pltpu.VMEM((z.halo * z.wide, 128), BF16),
            pltpu.VMEM((z.halo * z.wide, 128), BF16),
            pltpu.VMEM((group * tok, z.halo * z.wide), BF16),
            pltpu.VMEM((group * tok, z.halo * z.wide), BF16),
            pltpu.VMEM((z.halo * span * 8, z.wide), F32),
        ],
        flops=4 * far * z.pairs * unit,
    )
    ret = call(bind(seal_kernel, z, len(terms)), [((3 * tok + CODE_ROWS, z.cw), BF16)] * group, (dq, dk, dv, *terms))
    ret_got = [ret[0]] + [swap(ret[k], k) for k in range(1, group)]
    (side,) = call(bind(collect_kernel, z), [((heads * sides, buckets), F32)], ret_got)
    parts = [side] + [swap(side, k, "head") for k in range(1, sides)]
    grads = call(
        bind(unpack_kernel, z),
        [((tok, width), BF16)] * 3,
        ret_got,
        out_space=hbm,
        scratch=[pltpu.SemaphoreType.DMA((3 * group,))],
    )
    return (*grads, sum(parts[1:], parts[0]))


def solution(mesh):
    placed = (
        P("seq", "head"),
        P("seq", "head"),
        P("seq", "head"),
        P("seq", "head"),
        P("head", None),
        P("seq", None, None),
        P("seq", None),
    )

    return jax.shard_map(
        body,
        mesh=mesh,
        in_specs=placed,
        out_specs=(P("seq", "head"), P("seq", "head"), P("seq", "head"), P()),
        check_vma=False,
    )
```

```python
import math

import jax
import jax.numpy as jnp
from jax import lax
from jax.experimental import pallas as pl
from jax.experimental.pallas import tpu as pltpu
from jax.sharding import PartitionSpec as P


F32 = jnp.float32
BF16 = jnp.bfloat16
NEG = -1e30
NT = (((1,), (1,)), ((), ()))
NN = (((1,), (0,)), ((), ()))
CODE_ROWS = 16
VMEM_BYTES = 67043328


def dot(a, b, dims):
    return lax.dot_general(a, b, dims, preferred_element_type=F32)


def at(start, size):
    return pl.ds(pl.multiple_of(start, size), size)


def call(kernel, outs, args, scratch=(), spaces=None, out_space=pltpu.VMEM, flops=0, limit=16 << 20):
    spaces = spaces or [pltpu.VMEM] * len(args)
    moved = sum(a.size * a.dtype.itemsize for a in args)
    args = [
        pltpu.with_memory_space_constraint(a, s) if s == pltpu.VMEM else a for a, s in zip(args, spaces, strict=True)
    ]
    return pl.pallas_call(
        kernel,
        out_shape=tuple(out_space(s, d) for s, d in outs),
        in_specs=[pl.BlockSpec(memory_space=s) for s in spaces],
        out_specs=tuple(pl.BlockSpec(memory_space=out_space) for _ in outs),
        scratch_shapes=list(scratch),
        compiler_params=pltpu.CompilerParams(vmem_limit_bytes=limit),
        cost_estimate=pl.CostEstimate(flops=flops, bytes_accessed=moved, transcendentals=0),
    )(*args)


class Sizes:
    def __init__(self, tok, width, heads, span, buckets, group):
        self.tok, self.width, self.heads, self.span, self.buckets = tok, width, heads, span, buckets
        self.group = group
        self.hd = width // heads
        self.hg = heads // group
        self.cw = self.hg * self.hd
        self.pairs = self.hg // 2
        self.scale = self.hd ** (-0.5)
        self.halo = span - 1
        self.ext = group + self.halo
        self.wide = 2 * tok
        self.rows = 2 * tok + CODE_ROWS
        self.near = [(i, s) for i in range(group) for s in range(span) if s <= i]
        self.far = [(i, s) for i in range(group) for s in range(span) if s > i]
        assert heads % group == 0 and self.hg % 2 == 0 and 2 * self.hd == 128
        assert tok == 128 and buckets == 128 and group >= self.halo and self.hg <= 8
        assert math.frexp(self.scale)[0] == 0.5

    def me(self):
        return lax.rem(lax.axis_index("seq"), self.group)


def pack_kernel(z, q, k, v, d, ids, mask, *refs):
    kv, qd = refs[: z.group], refs[z.group : 2 * z.group]
    slots, flags, sem = refs[2 * z.group :]
    index = lax.axis_index("seq")
    me = z.me()
    copies = [
        pltpu.make_async_copy(ids.at[0], slots, sem.at[0]),
        pltpu.make_async_copy(mask, flags, sem.at[1]),
    ]
    for sources, dst in (((k, v), kv), ((q, d), qd)):
        for g in range(z.group):
            cols = at((me ^ g) * z.cw, z.cw)
            for n, src in enumerate(sources):
                rows = pl.ds(n * z.tok, z.tok)
                copies.append(pltpu.make_async_copy(src.at[:, cols], dst[g].at[rows, :], sem.at[len(copies)]))
    for copy in copies:
        copy.start()
    for copy in copies[:2]:
        copy.wait()
    rows = []
    for s in range(z.span):
        valid = True if s == 0 else (flags[0, s] == 1) & (index >= s)
        rows.append(jnp.where(valid, slots[s : s + 1, :] + 1, 0))
    rows.append(jnp.zeros((CODE_ROWS - z.span, z.wide), jnp.int32))
    codes = jnp.concatenate(rows, axis=0).astype(F32).astype(BF16)
    for g in range(z.group):
        kv[g][2 * z.tok :, :] = codes
    for copy in copies[2:]:
        copy.wait()


def kv_halo_kernel(z, *refs):
    out = refs[-1]
    me = z.me()
    first = z.group - z.halo
    for k in range(z.group):
        j = me ^ k

        @pl.when(j >= first)
        def _():
            out[at((j - first) * 2 * z.tok, 2 * z.tok), :] = refs[k][0 : 2 * z.tok, :]


def qd_halo_kernel(z, *refs):
    qd, kv, out = refs[: z.group], refs[z.group : -1], refs[-1]
    me = z.me()
    for k in range(z.group):
        j = me ^ k

        @pl.when(j < z.halo)
        def _():
            top = pl.multiple_of(j * z.rows, 16)
            out[pl.ds(top, 2 * z.tok), :] = qd[k][...]
            out[pl.ds(top + 2 * z.tok, CODE_ROWS), :] = kv[k][2 * z.tok :, :]


def onehot_of(codes, z):
    slots = lax.broadcasted_iota(jnp.int32, (z.buckets, codes.shape[1]), 0) + 1
    return jnp.where(codes.astype(jnp.int32) == slots, 1.0, 0.0).astype(BF16)


def thirds(x):
    hi = x.astype(BF16)
    rest = x - hi.astype(F32)
    mid = rest.astype(BF16)
    low = (rest - mid.astype(F32)).astype(BF16)
    return jnp.concatenate([hi.astype(F32), mid.astype(F32), low.astype(F32)], axis=0).astype(BF16)


def by_offset(split, codes, z):
    got = dot(split, onehot_of(codes, z), NN)
    return got[0:8] + got[8:16] + got[16:24] + jnp.where(codes == 0.0, NEG, 0.0)


def masked_pair(x, z):
    lane = lax.broadcasted_iota(jnp.int32, x.shape, 1)
    zero = jnp.zeros_like(x)
    return jnp.concatenate([jnp.where(lane < z.hd, x, zero), jnp.where(lane < z.hd, zero, x)], axis=0)


def slanted(row, z):
    return pltpu.roll(jnp.broadcast_to(row, (8, z.wide)), z.tok + 1, 1, stride=1, stride_axis=0)


def toeplitz(base, z):
    tok = z.tok
    lane = lax.broadcasted_iota(jnp.int32, (8, tok), 1)
    low, high = base[:, 0:tok], base[:, tok:]
    tiles = [low]
    for g in range(1, tok // 8):
        tiles.append(pltpu.roll(jnp.where(lane >= tok - 8 * g, high, low), 8 * g, 1))
    return jnp.concatenate(tiles, axis=0)


def my_table(table, z):
    head = lax.broadcasted_iota(jnp.int32, (8, z.buckets), 0)
    rows = jnp.zeros((8, z.buckets), F32)
    for h in range(z.hg):
        rows = jnp.where(head == h, table[pl.ds(z.me() * z.hg + h, 1), :], rows)
    return rows


def slant_tables(z, table, code_rows, bases):
    split = thirds(my_table(table, z))
    for n, codes in enumerate(code_rows):
        rows = by_offset(split, codes, z)
        for h in range(z.hg):
            at_row = (n * z.hg + h) * 8
            bases[at_row : at_row + 8, :] = slanted(rows[h : h + 1, :], z)


def diagonals(x, z):
    tok = z.tok
    lane = lax.broadcasted_iota(jnp.int32, (8, tok), 1)
    total = x[tok - 8 :]
    high = jnp.zeros((8, tok), F32)
    for g in range(tok // 8 - 1):
        by = tok - 8 - 8 * g
        part = pltpu.roll(x[8 * g : 8 * g + 8], by, 1)
        total = total + part
        high = high + jnp.where(lane < by, part, 0.0)
    return total - high, high


def aligned(both):
    left = 7 - (lax.broadcasted_iota(jnp.int32, both.shape, 0) & 7)
    for bit in (1, 2, 4):
        both = jnp.where((left & bit) != 0, pltpu.roll(both, bit, 1), both)
    return both


def causal(z):
    row = lax.broadcasted_iota(jnp.int32, (z.tok, z.wide), 0)
    col = lax.broadcasted_iota(jnp.int32, (z.tok, z.wide), 1) % z.tok
    return row <= col


def folded(x, how):
    return how(how(x.reshape(x.shape[0] // 8, 8, x.shape[1]), 0), 0, keepdims=True)


def bias_rows(z, bases, n, pair):
    rows = [toeplitz(bases[(n * z.hg + 2 * pair + e) * 8 : (n * z.hg + 2 * pair + e + 1) * 8, :], z) for e in range(2)]
    return jnp.concatenate(rows, axis=1)


def bias_kernel(z, *refs):
    kv, table = refs[: z.group], refs[z.group]
    keys, values, near, far, codes, bases = refs[z.group + 1 :]
    tok = z.tok
    me = z.me()
    for k in range(z.group):
        j = me ^ k
        keys[at(j * tok, tok), :] = kv[k][0:tok, :]
        values[at(j * tok, tok), :] = kv[k][tok : 2 * tok, :]
        codes[at(j * CODE_ROWS, CODE_ROWS), :] = kv[k][2 * tok :, :].astype(F32)
    tables = [(i, s) for i in range(z.group) for s in range(z.span)]
    slant_tables(z, table, [codes[i * CODE_ROWS + s : i * CODE_ROWS + s + 1, :] for i, s in tables], bases)
    for tiles, out in ((z.near, near), (z.far, far)):
        for t, (i, s) in enumerate(tiles):
            for pair in range(z.pairs):
                bias = bias_rows(z, bases, i * z.span + s, pair)
                out[t * z.pairs + pair] = jnp.where(causal(z), bias, NEG) if s == 0 else bias


def forward_tile(key, value, q, d, bias, row, outs):
    weights, dprobs, tops, totals, accums = outs
    scores = dot(key, q, NT) + bias[row]
    top = folded(scores, jnp.max)
    w = jnp.exp(scores - top)
    dprob = dot(value, d, NT)
    weights[row] = w
    dprobs[row] = dprob
    tops[pl.ds(row, 1), :] = top
    totals[pl.ds(row, 1), :] = folded(w, jnp.sum)
    accums[pl.ds(row, 1), :] = folded(w * dprob, jnp.sum)


def near_kernel(z, *refs):
    qd, keys, values, bias = refs[: z.group], *refs[z.group : z.group + 3]
    qm, dom, *outs = refs[z.group + 3 :]
    tok = z.tok
    me = z.me()
    for k in range(z.group):
        j = me ^ k
        for pair in range(z.pairs):
            lanes = slice(pair * 128, (pair + 1) * 128)
            rows = at(j * z.wide, z.wide)
            qm[pair, rows, :] = masked_pair(qd[k][0:tok, lanes] * jnp.asarray(z.scale, BF16), z)
            dom[pair, rows, :] = masked_pair(qd[k][tok : 2 * tok, lanes], z)

    def each(pair, _):
        lanes = at(pair * 128, 128)
        for t, (i, s) in enumerate(z.near):
            rows = slice((i - s) * tok, (i - s + 1) * tok)
            wide = slice(i * z.wide, (i + 1) * z.wide)
            forward_tile(
                keys[rows, lanes], values[rows, lanes], qm[pair, wide, :], dom[pair, wide, :],
                bias, t * z.pairs + pair, outs,
            )
        return 0

    lax.fori_loop(0, z.pairs, each, 0)


def far_kernel(z, halo, qm, dom, bias, tops, totals, accums, stats, fnear, ffar, *outs):
    tok = z.tok

    def each(pair, _):
        lanes = at(pair * 128, 128)
        for t, (i, s) in enumerate(z.far):
            b = z.halo + i - s
            wide = slice(i * z.wide, (i + 1) * z.wide)
            forward_tile(
                halo[2 * b * tok : (2 * b + 1) * tok, lanes], halo[(2 * b + 1) * tok : (2 * b + 2) * tok, lanes],
                qm[pair, wide, :], dom[pair, wide, :], bias, t * z.pairs + pair, outs,
            )
        for i in range(z.group):
            mine = [(tops, totals, accums, fnear, t) for t, (n, _) in enumerate(z.near) if n == i]
            mine += [(outs[2], outs[3], outs[4], ffar, t) for t, (n, _) in enumerate(z.far) if n == i]
            rows = [pl.ds(t * z.pairs + pair, 1) for *_, t in mine]
            peaks = [m[0][row, :] for m, row in zip(mine, rows, strict=True)]
            top = peaks[0]
            for peak in peaks[1:]:
                top = jnp.maximum(top, peak)
            total = jnp.zeros_like(top)
            accum = jnp.zeros_like(top)
            for m, row, peak in zip(mine, rows, peaks, strict=True):
                share = jnp.exp(peak - top)
                total = total + share * m[1][row, :]
                accum = accum + share * m[2][row, :]
            lse = top + jnp.log(total)
            for m, row, peak in zip(mine, rows, peaks, strict=True):
                m[3][row, :] = jnp.exp(peak - lse)
            stats[0, pl.ds(i * z.pairs + pair, 1), :] = lse
            stats[1, pl.ds(i * z.pairs + pair, 1), :] = accum / total
        return 0

    lax.fori_loop(0, z.pairs, each, 0)


def own_kernel(z, codes, stats, fnear, ffar, wnear, dnear, wfar, dfar, p16, s16, gb, offs):
    tok, span = z.tok, z.span

    def each(pair, _):
        for i in range(z.group):
            wide = slice(i * z.wide, (i + 1) * z.wide)
            delta = stats[1, pl.ds(i * z.pairs + pair, 1), :]
            for s in range(span):
                close = s <= i
                t = (z.near if close else z.far).index((i, s)) * z.pairs + pair
                w, d, f = (wnear, dnear, fnear) if close else (wfar, dfar, ffar)
                prob = w[t] * f[pl.ds(t, 1), :]
                dscore = prob * (d[t] - delta)
                rows = slice((z.halo + i - s) * tok, (z.halo + i - s + 1) * tok)
                s16[pair, rows, wide] = dscore.astype(BF16)
                if close:
                    p16[pair, (i - s) * tok : (i - s + 1) * tok, wide] = prob.astype(BF16)
                for e in range(2):
                    low, high = diagonals(dscore[:, e * tok : (e + 1) * tok], z)
                    row = at(((i * span + s) * z.hg + 2 * pair + e) * 8, 8)
                    offs[row, 0:tok] = low
                    offs[row, tok:] = high
        return 0

    lax.fori_loop(0, z.pairs, each, 0)
    head = lax.broadcasted_iota(jnp.int32, (8, z.wide), 0)
    total = jnp.zeros((8, z.buckets), F32)
    for n in range(z.group * span):
        both = aligned(offs[n * z.hg * 8 : (n + 1) * z.hg * 8, :])
        sums = jnp.zeros((8, z.wide), F32)
        for h in range(z.hg):
            sums = sums + jnp.where(head == h, both[8 * h : 8 * h + 8].sum(axis=0, keepdims=True), 0.0)
        row = n // span * CODE_ROWS + n % span
        got = dot(thirds(sums), onehot_of(codes[row : row + 1, :], z), NT)
        total = total + (got[0:8] + got[8:16] + got[16:24])
    gb[...] = total


def grad_q_kernel(z, keys, halo, s16, dq):
    tok, span = z.tok, z.span

    def each(pair, _):
        lanes = at(pair * 128, 128)
        blocks = [halo[2 * b * tok : (2 * b + 1) * tok, lanes] for b in range(z.halo)]
        blocks += [keys[j * tok : (j + 1) * tok, lanes] for j in range(z.group)]
        turned = jnp.concatenate([block.T for block in blocks], axis=1)
        for i in range(z.group):
            window = slice(i * tok, (i + span) * tok)
            cross = dot(turned[:, window], s16[pair, window, i * z.wide : (i + 1) * z.wide], NN)
            both = jnp.concatenate([cross[0 : z.hd, 0:tok], cross[z.hd :, tok:]], axis=0)
            dq[i * tok : (i + 1) * tok, lanes] = (z.scale * both.T).astype(BF16)
        return 0

    lax.fori_loop(0, z.pairs, each, 0)


def tail_kernel(z, keys, values, halo, stats, table, qh, dh, ph, sh, bases):
    tok, span = z.tok, z.span
    tables = [(b, s) for b in range(z.halo) for s in range(b + 1, span)]
    rows = []
    for b in range(z.halo):
        codes = halo[b * z.rows + 2 * tok : (b + 1) * z.rows, :].astype(F32)
        rows += [codes[s : s + 1, :] for s in range(b + 1, span)]
    slant_tables(z, table, rows, bases)
    for pair in range(z.pairs):
        lanes = slice(pair * 128, (pair + 1) * 128)
        for b in range(z.halo):
            top = b * z.rows
            wide = slice(b * z.wide, (b + 1) * z.wide)
            q = masked_pair(halo[top : top + tok, lanes] * jnp.asarray(z.scale, BF16), z)
            d = masked_pair(halo[top + tok : top + 2 * tok, lanes], z)
            qh[pair, wide, :] = q
            dh[pair, wide, :] = d
            u = b * z.pairs + pair
            lse, delta = stats[0, u : u + 1, :], stats[1, u : u + 1, :]
            for s in range(b + 1, span):
                j = z.group + b - s
                block = slice(j * tok, (j + 1) * tok)
                bias = bias_rows(z, bases, tables.index((b, s)), pair)
                prob = jnp.exp(dot(keys[block, lanes], q, NT) + bias - lse)
                dscore = prob * (dot(values[block, lanes], d, NT) - delta)
                ph[pair, block, wide] = prob.astype(BF16)
                sh[pair, block, wide] = dscore.astype(BF16)


def grad_kv_kernel(z, qm, dom, p16, s16, qh, dh, ph, sh, dk, dv):
    tok = z.tok

    def each(pair, _):
        lanes = at(pair * 128, 128)
        for j in range(z.group):
            rows = slice(j * tok, (j + 1) * tok)
            ext = slice((z.halo + j) * tok, (z.halo + j + 1) * tok)
            near = slice(j * z.wide, z.group * z.wide)
            gk = dot(s16[pair, ext, near], qm[pair, near, :], NN)
            gv = dot(p16[pair, rows, near], dom[pair, near, :], NN)
            count = min(z.halo, j + z.span - z.group)
            if count > 0:
                past = slice(0, count * z.wide)
                gk = gk + dot(sh[pair, rows, past], qh[pair, past, :], NN)
                gv = gv + dot(ph[pair, rows, past], dh[pair, past, :], NN)
            dk[rows, lanes] = gk.astype(BF16)
            dv[rows, lanes] = gv.astype(BF16)
        return 0

    lax.fori_loop(0, z.pairs, each, 0)


def seal_kernel(z, sides, dq, dk, dv, *refs):
    sums, sends = refs[:sides], refs[sides:]
    tok = z.tok
    packs = []
    for ref in sums:
        split = thirds(ref[...]).astype(F32)
        low = jnp.concatenate([split[16:24], jnp.zeros((8, z.buckets), F32)], axis=0)
        packs.append(jnp.concatenate([split[0:16], low], axis=1).astype(BF16))
    me = z.me()
    for k in range(z.group):
        rows = at((me ^ k) * tok, tok)
        for n, ref in enumerate((dq, dk, dv)):
            sends[k][n * tok : (n + 1) * tok, :] = ref[rows, :]
        for n, pack in enumerate(packs):
            sends[k][3 * tok + n * CODE_ROWS : 3 * tok + (n + 1) * CODE_ROWS, :] = pack


def add_kernel(*refs):
    total = refs[0][...]
    for ref in refs[1:-1]:
        total = total + ref[...]
    refs[-1][...] = total


def unpack_kernel(z, sides, *refs):
    got, outs, gb, held, sem = refs[: z.group], refs[z.group : -3], refs[-3], refs[-2], refs[-1]
    me = z.me()
    copies = []
    for k in range(z.group):
        cols = at((me ^ k) * z.cw, z.cw)
        for n, out in enumerate(outs):
            src = got[k].at[n * z.tok : (n + 1) * z.tok, :]
            copies.append(pltpu.make_async_copy(src, out.at[:, cols], sem.at[len(copies)]))
    for copy in copies:
        copy.start()
    owner = lax.broadcasted_iota(jnp.int32, held.shape, 0) // z.hg
    total = jnp.zeros(held.shape, F32)
    for k in range(z.group):
        for n in range(sides):
            top = 3 * z.tok + n * CODE_ROWS
            rows = got[k][top : top + CODE_ROWS, :].astype(F32)
            sums = rows[0:8, 0 : z.buckets] + rows[8:16, 0 : z.buckets] + rows[0:8, z.buckets :]
            wide = jnp.concatenate([sums[0 : z.hg]] * (held.shape[0] // z.hg), axis=0)
            side = lax.axis_index("head") ^ n
            total = total + jnp.where(owner == side * z.group + (me ^ k), wide, 0.0)
    held[...] = total
    last = pltpu.make_async_copy(held, gb, sem.at[len(copies)])
    last.start()
    for copy in copies + [last]:
        copy.wait()


def bind(kernel, *fixed):
    def bound(*refs):
        return kernel(*fixed, *refs)

    return bound


def body(queries, keys, values, grad_out, bias_table, bucket_ids, block_mask):
    tok, width = queries.shape
    heads, buckets = bias_table.shape
    span = block_mask.shape[1]
    group = span
    z = Sizes(tok, width, heads, span, buckets, group)
    blocks = lax.axis_size("seq")
    sides = lax.axis_size("head")
    assert blocks % group == 0 and (blocks & (blocks - 1)) == 0 and (sides & (sides - 1)) == 0

    def swap(value, by, axis="seq"):
        return lax.ppermute(value, axis, [(i, i ^ by) for i in range(lax.axis_size(axis))])

    def shifted(value, by):
        return lax.ppermute(value, "seq", [(i, i + by) for i in range(blocks) if 0 <= i + by < blocks])

    def added(*terms):
        (total,) = call(add_kernel, [(terms[0].shape, terms[0].dtype)], terms)
        return total

    hbm = pltpu.HBM
    pack_bytes = group * (z.rows + 2 * tok) * z.cw * 2
    packed = call(
        bind(pack_kernel, z),
        [((z.rows, z.cw), BF16)] * group + [((2 * tok, z.cw), BF16)] * group,
        (queries, keys, values, grad_out, bucket_ids, block_mask),
        spaces=[hbm] * 6,
        scratch=[
            pltpu.VMEM((span, z.wide), jnp.int32),
            pltpu.SMEM((1, span), jnp.int32),
            pltpu.SemaphoreType.DMA((4 * group + 2,)),
        ],
        limit=VMEM_BYTES - pack_bytes - (520 << 10),
    )
    kv, qd = packed[:group], packed[group:]
    kv_got = [kv[0]] + [swap(kv[k], k) for k in range(1, group)]
    qd_got = [qd[0]] + [swap(qd[k], k) for k in range(1, group)]
    (kv_out,) = call(bind(kv_halo_kernel, z), [((z.halo * 2 * tok, z.cw), BF16)], kv_got)
    kv_halo = shifted(kv_out, group)
    (qd_out,) = call(bind(qd_halo_kernel, z), [((z.halo * z.rows, z.cw), BF16)], (*qd_got, *kv_got))
    qd_halo = shifted(qd_out, -group)

    def tile_outs(count):
        tile = ((count * z.pairs, tok, z.wide), F32)
        row = ((count * z.pairs, z.wide), F32)
        return [tile, tile, row, row, row]

    near, far = len(z.near), len(z.far)
    unit = 2 * 128 * tok * z.wide
    own_k, own_v, bias_near, bias_far, codes = call(
        bind(bias_kernel, z),
        [((group * tok, z.cw), BF16)] * 2
        + [((near * z.pairs, tok, z.wide), F32), ((far * z.pairs, tok, z.wide), F32)]
        + [((group * CODE_ROWS, z.wide), F32)],
        (*kv_got, bias_table),
        scratch=[pltpu.VMEM((group * span * z.hg * 8, z.wide), F32)],
    )
    qm, dom, wnear, dnear, *sums = call(
        bind(near_kernel, z),
        [((z.pairs, group * z.wide, 128), BF16)] * 2 + tile_outs(near),
        (*qd_got, own_k, own_v, bias_near),
        flops=2 * near * z.pairs * unit,
    )
    stats, fnear, ffar, wfar, dfar, *_ = call(
        bind(far_kernel, z),
        [((2, group * z.pairs, z.wide), F32), ((near * z.pairs, z.wide), F32), ((far * z.pairs, z.wide), F32)]
        + tile_outs(far),
        (kv_halo, qm, dom, bias_far, *sums),
        flops=2 * far * z.pairs * unit,
    )
    stats_halo = lax.ppermute(stats, "seq", [(i, (i - group) % blocks) for i in range(blocks)])
    p16, s16, gb = call(
        bind(own_kernel, z),
        [
            ((z.pairs, group * tok, group * z.wide), BF16),
            ((z.pairs, z.ext * tok, group * z.wide), BF16),
            ((8, buckets), F32),
        ],
        (codes, stats, fnear, ffar, wnear, dnear, wfar, dfar),
        scratch=[pltpu.VMEM((group * span * z.hg * 8, z.wide), F32)],
    )
    by = group
    while by < blocks:
        other = swap(gb, by)
        gb = added(gb, other)
        by = by * 2
    sums_of = [gb] + [swap(gb, k, "head") for k in range(1, sides)]
    (dq,) = call(
        bind(grad_q_kernel, z),
        [((group * tok, z.cw), BF16)],
        (own_k, kv_halo, s16),
        flops=(near + far) * z.pairs * unit,
    )
    lanes_of = ((z.pairs, group * tok, z.halo * z.wide), BF16)
    rows_of = ((z.pairs, z.halo * z.wide, 128), BF16)
    halo_terms = call(
        bind(tail_kernel, z),
        [rows_of, rows_of, lanes_of, lanes_of],
        (own_k, own_v, qd_halo, stats_halo, bias_table),
        scratch=[pltpu.VMEM((far * z.hg * 8, z.wide), F32)],
        flops=2 * far * z.pairs * unit,
    )
    dk, dv = call(
        bind(grad_kv_kernel, z),
        [((group * tok, z.cw), BF16)] * 2,
        (qm, dom, p16, s16, *halo_terms),
        flops=2 * (near + far) * z.pairs * unit,
    )
    ret = call(
        bind(seal_kernel, z, sides), [((3 * tok + sides * CODE_ROWS, z.cw), BF16)] * group, (dq, dk, dv, *sums_of)
    )
    ret_got = [ret[0]] + [swap(ret[k], k) for k in range(1, group)]
    return call(
        bind(unpack_kernel, z, sides),
        [((tok, width), BF16)] * 3 + [((heads * sides, buckets), F32)],
        ret_got,
        out_space=hbm,
        scratch=[pltpu.VMEM((heads * sides, buckets), F32), pltpu.SemaphoreType.DMA((3 * group + 1,))],
    )


def solution(mesh):
    placed = (
        P("seq", "head"),
        P("seq", "head"),
        P("seq", "head"),
        P("seq", "head"),
        P("head", None),
        P("seq", None, None),
        P("seq", None),
    )

    return jax.shard_map(
        body,
        mesh=mesh,
        in_specs=placed,
        out_specs=(P("seq", "head"), P("seq", "head"), P("seq", "head"), P()),
        check_vma=False,
    )
```

```python
import math

import jax
import jax.numpy as jnp
from jax import lax
from jax.experimental import pallas as pl
from jax.experimental.pallas import tpu as pltpu
from jax.sharding import PartitionSpec as P


F32 = jnp.float32
BF16 = jnp.bfloat16
NEG = -1e30
NT = (((1,), (1,)), ((), ()))
NN = (((1,), (0,)), ((), ()))
CODE_ROWS = 16
VMEM_BYTES = 67043328


def dot(a, b, dims):
    return lax.dot_general(a, b, dims, preferred_element_type=F32)


def at(start, size):
    return pl.ds(pl.multiple_of(start, size), size)


def call(kernel, outs, args, scratch=(), spaces=None, out_space=pltpu.VMEM, flops=0, limit=16 << 20):
    spaces = spaces or [pltpu.VMEM] * len(args)
    moved = sum(a.size * a.dtype.itemsize for a in args)
    args = [
        pltpu.with_memory_space_constraint(a, s) if s == pltpu.VMEM else a for a, s in zip(args, spaces, strict=True)
    ]
    return pl.pallas_call(
        kernel,
        out_shape=tuple(out_space(s, d) for s, d in outs),
        in_specs=[pl.BlockSpec(memory_space=s) for s in spaces],
        out_specs=tuple(pl.BlockSpec(memory_space=out_space) for _ in outs),
        scratch_shapes=list(scratch),
        compiler_params=pltpu.CompilerParams(vmem_limit_bytes=limit),
        cost_estimate=pl.CostEstimate(flops=flops, bytes_accessed=moved, transcendentals=0),
    )(*args)


class Sizes:
    def __init__(self, tok, width, heads, span, buckets, group):
        self.tok, self.width, self.heads, self.span, self.buckets = tok, width, heads, span, buckets
        self.group = group
        self.hd = width // heads
        self.hg = heads // group
        self.cw = self.hg * self.hd
        self.pairs = self.hg // 2
        self.scale = self.hd ** (-0.5)
        self.halo = span - 1
        self.ext = group + self.halo
        self.wide = 2 * tok
        self.rows = 2 * tok + CODE_ROWS
        self.near = [(i, s) for i in range(group) for s in range(span) if s <= i]
        self.far = [(i, s) for i in range(group) for s in range(span) if s > i]
        assert heads % group == 0 and self.hg % 2 == 0 and 2 * self.hd == 128
        assert tok == 128 and buckets == 128 and group >= self.halo and self.hg <= 8
        assert math.frexp(self.scale)[0] == 0.5

    def me(self):
        return lax.rem(lax.axis_index("seq"), self.group)


def pack_kernel(z, q, k, v, d, ids, mask, *refs):
    kv, qd = refs[: z.group], refs[z.group : 2 * z.group]
    slots, flags, sem = refs[2 * z.group :]
    index = lax.axis_index("seq")
    me = z.me()
    copies = [
        pltpu.make_async_copy(ids.at[0], slots, sem.at[0]),
        pltpu.make_async_copy(mask, flags, sem.at[1]),
    ]
    for sources, dst in (((k, v), kv), ((q, d), qd)):
        for g in range(z.group):
            cols = at((me ^ g) * z.cw, z.cw)
            for n, src in enumerate(sources):
                rows = pl.ds(n * z.tok, z.tok)
                copies.append(pltpu.make_async_copy(src.at[:, cols], dst[g].at[rows, :], sem.at[len(copies)]))
    for copy in copies:
        copy.start()
    for copy in copies[:2]:
        copy.wait()
    rows = []
    for s in range(z.span):
        valid = True if s == 0 else (flags[0, s] == 1) & (index >= s)
        rows.append(jnp.where(valid, slots[s : s + 1, :] + 1, 0))
    rows.append(jnp.zeros((CODE_ROWS - z.span, z.wide), jnp.int32))
    codes = jnp.concatenate(rows, axis=0).astype(F32).astype(BF16)
    for g in range(z.group):
        kv[g][2 * z.tok :, :] = codes
    for copy in copies[2:]:
        copy.wait()


def kv_halo_kernel(z, *refs):
    out = refs[-1]
    me = z.me()
    first = z.group - z.halo
    for k in range(z.group):
        j = me ^ k

        @pl.when(j >= first)
        def _():
            out[at((j - first) * 2 * z.tok, 2 * z.tok), :] = refs[k][0 : 2 * z.tok, :]


def qd_halo_kernel(z, *refs):
    qd, kv, out = refs[: z.group], refs[z.group : -1], refs[-1]
    me = z.me()
    for k in range(z.group):
        j = me ^ k

        @pl.when(j < z.halo)
        def _():
            top = pl.multiple_of(j * z.rows, 16)
            out[pl.ds(top, 2 * z.tok), :] = qd[k][...]
            out[pl.ds(top + 2 * z.tok, CODE_ROWS), :] = kv[k][2 * z.tok :, :]


def onehot_of(codes, z):
    slots = lax.broadcasted_iota(jnp.int32, (z.buckets, codes.shape[1]), 0) + 1
    return jnp.where(codes.astype(jnp.int32) == slots, 1.0, 0.0).astype(BF16)


def thirds(x):
    hi = x.astype(BF16)
    rest = x - hi.astype(F32)
    mid = rest.astype(BF16)
    low = (rest - mid.astype(F32)).astype(BF16)
    return jnp.concatenate([hi.astype(F32), mid.astype(F32), low.astype(F32)], axis=0).astype(BF16)


def by_offset(split, codes, z):
    got = dot(split, onehot_of(codes, z), NN)
    return got[0:8] + got[8:16] + got[16:24] + jnp.where(codes == 0.0, NEG, 0.0)


def masked_pair(x, z):
    lane = lax.broadcasted_iota(jnp.int32, x.shape, 1)
    zero = jnp.zeros_like(x)
    return jnp.concatenate([jnp.where(lane < z.hd, x, zero), jnp.where(lane < z.hd, zero, x)], axis=0)


def slanted(row, z):
    return pltpu.roll(jnp.broadcast_to(row, (8, z.wide)), z.tok + 1, 1, stride=1, stride_axis=0)


def toeplitz(base, z):
    tok = z.tok
    lane = lax.broadcasted_iota(jnp.int32, (8, tok), 1)
    low, high = base[:, 0:tok], base[:, tok:]
    tiles = [low]
    for g in range(1, tok // 8):
        tiles.append(pltpu.roll(jnp.where(lane >= tok - 8 * g, high, low), 8 * g, 1))
    return jnp.concatenate(tiles, axis=0)


def my_table(table, z):
    head = lax.broadcasted_iota(jnp.int32, (8, z.buckets), 0)
    rows = jnp.zeros((8, z.buckets), F32)
    for h in range(z.hg):
        rows = jnp.where(head == h, table[pl.ds(z.me() * z.hg + h, 1), :], rows)
    return rows


def slant_tables(z, table, code_rows, bases):
    split = thirds(my_table(table, z))
    for n, codes in enumerate(code_rows):
        rows = by_offset(split, codes, z)
        for h in range(z.hg):
            at_row = (n * z.hg + h) * 8
            bases[at_row : at_row + 8, :] = slanted(rows[h : h + 1, :], z)


def diagonals(x, z):
    tok = z.tok
    lane = lax.broadcasted_iota(jnp.int32, (8, tok), 1)
    total = x[tok - 8 :]
    high = jnp.zeros((8, tok), F32)
    for g in range(tok // 8 - 1):
        by = tok - 8 - 8 * g
        part = pltpu.roll(x[8 * g : 8 * g + 8], by, 1)
        total = total + part
        high = high + jnp.where(lane < by, part, 0.0)
    return total - high, high


def aligned(both):
    left = 7 - (lax.broadcasted_iota(jnp.int32, both.shape, 0) & 7)
    for bit in (1, 2, 4):
        both = jnp.where((left & bit) != 0, pltpu.roll(both, bit, 1), both)
    return both


def causal(z):
    row = lax.broadcasted_iota(jnp.int32, (z.tok, z.wide), 0)
    col = lax.broadcasted_iota(jnp.int32, (z.tok, z.wide), 1) % z.tok
    return row <= col


def folded(x, how):
    return how(how(x.reshape(x.shape[0] // 8, 8, x.shape[1]), 0), 0, keepdims=True)


def bias_rows(z, bases, n, pair):
    rows = [toeplitz(bases[(n * z.hg + 2 * pair + e) * 8 : (n * z.hg + 2 * pair + e + 1) * 8, :], z) for e in range(2)]
    return jnp.concatenate(rows, axis=1)


def bias_kernel(z, *refs):
    kv, table = refs[: z.group], refs[z.group]
    keys, values, near, far, codes, bases = refs[z.group + 1 :]
    tok = z.tok
    me = z.me()
    for k in range(z.group):
        j = me ^ k
        keys[at(j * tok, tok), :] = kv[k][0:tok, :]
        values[at(j * tok, tok), :] = kv[k][tok : 2 * tok, :]
        codes[at(j * CODE_ROWS, CODE_ROWS), :] = kv[k][2 * tok :, :].astype(F32)
    tables = [(i, s) for i in range(z.group) for s in range(z.span)]
    slant_tables(z, table, [codes[i * CODE_ROWS + s : i * CODE_ROWS + s + 1, :] for i, s in tables], bases)
    for tiles, out in ((z.near, near), (z.far, far)):
        for t, (i, s) in enumerate(tiles):
            for pair in range(z.pairs):
                bias = bias_rows(z, bases, i * z.span + s, pair)
                out[t * z.pairs + pair] = jnp.where(causal(z), bias, NEG) if s == 0 else bias


def forward_tile(key, value, q, d, bias, row, outs):
    weights, dprobs, tops, totals, accums = outs
    scores = dot(key, q, NT) + bias[row]
    top = folded(scores, jnp.max)
    w = jnp.exp(scores - top)
    dprob = dot(value, d, NT)
    weights[row] = w
    dprobs[row] = dprob
    tops[pl.ds(row, 1), :] = top
    totals[pl.ds(row, 1), :] = folded(w, jnp.sum)
    accums[pl.ds(row, 1), :] = folded(w * dprob, jnp.sum)


def near_kernel(z, *refs):
    qd, keys, values, bias = refs[: z.group], *refs[z.group : z.group + 3]
    qm, dom, *outs = refs[z.group + 3 :]
    tok = z.tok
    me = z.me()
    for k in range(z.group):
        j = me ^ k
        for pair in range(z.pairs):
            lanes = slice(pair * 128, (pair + 1) * 128)
            rows = at(j * z.wide, z.wide)
            qm[pair, rows, :] = masked_pair(qd[k][0:tok, lanes] * jnp.asarray(z.scale, BF16), z)
            dom[pair, rows, :] = masked_pair(qd[k][tok : 2 * tok, lanes], z)

    def each(pair, _):
        lanes = at(pair * 128, 128)
        for t, (i, s) in enumerate(z.near):
            rows = slice((i - s) * tok, (i - s + 1) * tok)
            wide = slice(i * z.wide, (i + 1) * z.wide)
            forward_tile(
                keys[rows, lanes], values[rows, lanes], qm[pair, wide, :], dom[pair, wide, :],
                bias, t * z.pairs + pair, outs,
            )
        return 0

    lax.fori_loop(0, z.pairs, each, 0)


def far_kernel(z, halo, qm, dom, bias, tops, totals, accums, stats, fnear, ffar, *outs):
    tok = z.tok

    def each(pair, _):
        lanes = at(pair * 128, 128)
        for t, (i, s) in enumerate(z.far):
            b = z.halo + i - s
            wide = slice(i * z.wide, (i + 1) * z.wide)
            forward_tile(
                halo[2 * b * tok : (2 * b + 1) * tok, lanes], halo[(2 * b + 1) * tok : (2 * b + 2) * tok, lanes],
                qm[pair, wide, :], dom[pair, wide, :], bias, t * z.pairs + pair, outs,
            )
        for i in range(z.group):
            mine = [(tops, totals, accums, fnear, t) for t, (n, _) in enumerate(z.near) if n == i]
            mine += [(outs[2], outs[3], outs[4], ffar, t) for t, (n, _) in enumerate(z.far) if n == i]
            rows = [pl.ds(t * z.pairs + pair, 1) for *_, t in mine]
            peaks = [m[0][row, :] for m, row in zip(mine, rows, strict=True)]
            top = peaks[0]
            for peak in peaks[1:]:
                top = jnp.maximum(top, peak)
            total = jnp.zeros_like(top)
            accum = jnp.zeros_like(top)
            for m, row, peak in zip(mine, rows, peaks, strict=True):
                share = jnp.exp(peak - top)
                total = total + share * m[1][row, :]
                accum = accum + share * m[2][row, :]
            lse = top + jnp.log(total)
            for m, row, peak in zip(mine, rows, peaks, strict=True):
                m[3][row, :] = jnp.exp(peak - lse)
            stats[0, pl.ds(i * z.pairs + pair, 1), :] = lse
            stats[1, pl.ds(i * z.pairs + pair, 1), :] = accum / total
        return 0

    lax.fori_loop(0, z.pairs, each, 0)


def own_kernel(z, codes, stats, fnear, ffar, wnear, dnear, wfar, dfar, p16, s16, gb, offs):
    tok, span = z.tok, z.span

    def each(pair, _):
        for i in range(z.group):
            wide = slice(i * z.wide, (i + 1) * z.wide)
            delta = stats[1, pl.ds(i * z.pairs + pair, 1), :]
            for s in range(span):
                close = s <= i
                t = (z.near if close else z.far).index((i, s)) * z.pairs + pair
                w, d, f = (wnear, dnear, fnear) if close else (wfar, dfar, ffar)
                prob = w[t] * f[pl.ds(t, 1), :]
                dscore = prob * (d[t] - delta)
                rows = slice((z.halo + i - s) * tok, (z.halo + i - s + 1) * tok)
                s16[pair, rows, wide] = dscore.astype(BF16)
                if close:
                    p16[pair, (i - s) * tok : (i - s + 1) * tok, wide] = prob.astype(BF16)
                for e in range(2):
                    low, high = diagonals(dscore[:, e * tok : (e + 1) * tok], z)
                    row = at(((i * span + s) * z.hg + 2 * pair + e) * 8, 8)
                    offs[row, 0:tok] = low
                    offs[row, tok:] = high
        return 0

    lax.fori_loop(0, z.pairs, each, 0)
    head = lax.broadcasted_iota(jnp.int32, (8, z.wide), 0)
    total = jnp.zeros((8, z.buckets), F32)
    for n in range(z.group * span):
        both = aligned(offs[n * z.hg * 8 : (n + 1) * z.hg * 8, :])
        sums = jnp.zeros((8, z.wide), F32)
        for h in range(z.hg):
            sums = sums + jnp.where(head == h, both[8 * h : 8 * h + 8].sum(axis=0, keepdims=True), 0.0)
        row = n // span * CODE_ROWS + n % span
        got = dot(thirds(sums), onehot_of(codes[row : row + 1, :], z), NT)
        total = total + (got[0:8] + got[8:16] + got[16:24])
    gb[...] = total


def grad_q_kernel(z, keys, halo, s16, dq):
    tok, span = z.tok, z.span

    def each(pair, _):
        lanes = at(pair * 128, 128)
        blocks = [halo[2 * b * tok : (2 * b + 1) * tok, lanes] for b in range(z.halo)]
        blocks += [keys[j * tok : (j + 1) * tok, lanes] for j in range(z.group)]
        turned = jnp.concatenate([block.T for block in blocks], axis=1)
        for i in range(z.group):
            window = slice(i * tok, (i + span) * tok)
            cross = dot(turned[:, window], s16[pair, window, i * z.wide : (i + 1) * z.wide], NN)
            both = jnp.concatenate([cross[0 : z.hd, 0:tok], cross[z.hd :, tok:]], axis=0)
            dq[i * tok : (i + 1) * tok, lanes] = (z.scale * both.T).astype(BF16)
        return 0

    lax.fori_loop(0, z.pairs, each, 0)


def tail_kernel(z, keys, values, halo, even, odd, table, qh, dh, ph, sh, bases):
    tok, span = z.tok, z.span
    tables = [(b, s) for b in range(z.halo) for s in range(b + 1, span)]
    rows = []
    for b in range(z.halo):
        codes = halo[b * z.rows + 2 * tok : (b + 1) * z.rows, :].astype(F32)
        rows += [codes[s : s + 1, :] for s in range(b + 1, span)]
    slant_tables(z, table, rows, bases)
    second = lax.rem(lax.div(lax.axis_index("seq"), z.group), 2) == 1
    for pair in range(z.pairs):
        lanes = slice(pair * 128, (pair + 1) * 128)
        for b in range(z.halo):
            top = b * z.rows
            wide = slice(b * z.wide, (b + 1) * z.wide)
            q = masked_pair(halo[top : top + tok, lanes] * jnp.asarray(z.scale, BF16), z)
            d = masked_pair(halo[top + tok : top + 2 * tok, lanes], z)
            qh[pair, wide, :] = q
            dh[pair, wide, :] = d
            u = b * z.pairs + pair
            lse, delta = (jnp.where(second, odd[n, u : u + 1, :], even[n, u : u + 1, :]) for n in range(2))
            for s in range(b + 1, span):
                j = z.group + b - s
                block = slice(j * tok, (j + 1) * tok)
                bias = bias_rows(z, bases, tables.index((b, s)), pair)
                prob = jnp.exp(dot(keys[block, lanes], q, NT) + bias - lse)
                dscore = prob * (dot(values[block, lanes], d, NT) - delta)
                ph[pair, block, wide] = prob.astype(BF16)
                sh[pair, block, wide] = dscore.astype(BF16)


def grad_kv_kernel(z, qm, dom, p16, s16, qh, dh, ph, sh, dk, dv):
    tok = z.tok

    def each(pair, _):
        lanes = at(pair * 128, 128)
        for j in range(z.group):
            rows = slice(j * tok, (j + 1) * tok)
            ext = slice((z.halo + j) * tok, (z.halo + j + 1) * tok)
            near = slice(j * z.wide, z.group * z.wide)
            gk = dot(s16[pair, ext, near], qm[pair, near, :], NN)
            gv = dot(p16[pair, rows, near], dom[pair, near, :], NN)
            count = min(z.halo, j + z.span - z.group)
            if count > 0:
                past = slice(0, count * z.wide)
                gk = gk + dot(sh[pair, rows, past], qh[pair, past, :], NN)
                gv = gv + dot(ph[pair, rows, past], dh[pair, past, :], NN)
            dk[rows, lanes] = gk.astype(BF16)
            dv[rows, lanes] = gv.astype(BF16)
        return 0

    lax.fori_loop(0, z.pairs, each, 0)


def seal_kernel(z, sides, dq, dk, dv, *refs):
    sums, sends = refs[:sides], refs[sides:]
    tok = z.tok
    packs = []
    for ref in sums:
        split = thirds(ref[...]).astype(F32)
        low = jnp.concatenate([split[16:24], jnp.zeros((8, z.buckets), F32)], axis=0)
        packs.append(jnp.concatenate([split[0:16], low], axis=1).astype(BF16))
    me = z.me()
    for k in range(z.group):
        rows = at((me ^ k) * tok, tok)
        for n, ref in enumerate((dq, dk, dv)):
            sends[k][n * tok : (n + 1) * tok, :] = ref[rows, :]
        for n, pack in enumerate(packs):
            sends[k][3 * tok + n * CODE_ROWS : 3 * tok + (n + 1) * CODE_ROWS, :] = pack


def add_kernel(*refs):
    total = refs[0][...]
    for ref in refs[1:-1]:
        total = total + ref[...]
    refs[-1][...] = total


def unpack_kernel(z, sides, *refs):
    got, outs, gb, held, sem = refs[: z.group], refs[z.group : -3], refs[-3], refs[-2], refs[-1]
    me = z.me()
    copies = []
    for k in range(z.group):
        cols = at((me ^ k) * z.cw, z.cw)
        for n, out in enumerate(outs):
            src = got[k].at[n * z.tok : (n + 1) * z.tok, :]
            copies.append(pltpu.make_async_copy(src, out.at[:, cols], sem.at[len(copies)]))
    for copy in copies:
        copy.start()
    owner = lax.broadcasted_iota(jnp.int32, held.shape, 0) // z.hg
    total = jnp.zeros(held.shape, F32)
    for k in range(z.group):
        for n in range(sides):
            top = 3 * z.tok + n * CODE_ROWS
            rows = got[k][top : top + CODE_ROWS, :].astype(F32)
            sums = rows[0:8, 0 : z.buckets] + rows[8:16, 0 : z.buckets] + rows[0:8, z.buckets :]
            wide = jnp.concatenate([sums[0 : z.hg]] * (held.shape[0] // z.hg), axis=0)
            side = lax.axis_index("head") ^ n
            total = total + jnp.where(owner == side * z.group + (me ^ k), wide, 0.0)
    held[...] = total
    last = pltpu.make_async_copy(held, gb, sem.at[len(copies)])
    last.start()
    for copy in copies + [last]:
        copy.wait()


def bind(kernel, *fixed):
    def bound(*refs):
        return kernel(*fixed, *refs)

    return bound


def body(queries, keys, values, grad_out, bias_table, bucket_ids, block_mask):
    tok, width = queries.shape
    heads, buckets = bias_table.shape
    span = block_mask.shape[1]
    group = span
    z = Sizes(tok, width, heads, span, buckets, group)
    blocks = lax.axis_size("seq")
    sides = lax.axis_size("head")
    assert blocks % group == 0 and (blocks & (blocks - 1)) == 0 and (sides & (sides - 1)) == 0

    def swap(value, by, axis="seq"):
        return lax.ppermute(value, axis, [(i, i ^ by) for i in range(lax.axis_size(axis))])

    def shifted(value, by):
        return lax.ppermute(value, "seq", [(i, i + by) for i in range(blocks) if 0 <= i + by < blocks])

    def neighbours(first):
        pairs = []
        for i in range(blocks):
            g = (i // group - first) ^ 1
            g = g + first if i // group >= first else i // group
            pairs.append((i, i if g * group >= blocks else g * group + i % group))
        return pairs

    def added(*terms):
        (total,) = call(add_kernel, [(terms[0].shape, terms[0].dtype)], terms)
        return total

    hbm = pltpu.HBM
    pack_bytes = group * (z.rows + 2 * tok) * z.cw * 2
    packed = call(
        bind(pack_kernel, z),
        [((z.rows, z.cw), BF16)] * group + [((2 * tok, z.cw), BF16)] * group,
        (queries, keys, values, grad_out, bucket_ids, block_mask),
        spaces=[hbm] * 6,
        scratch=[
            pltpu.VMEM((span, z.wide), jnp.int32),
            pltpu.SMEM((1, span), jnp.int32),
            pltpu.SemaphoreType.DMA((4 * group + 2,)),
        ],
        limit=VMEM_BYTES - pack_bytes - (520 << 10),
    )
    kv, qd = packed[:group], packed[group:]
    kv_got = [kv[0]] + [swap(kv[k], k) for k in range(1, group)]
    qd_got = [qd[0]] + [swap(qd[k], k) for k in range(1, group)]
    (kv_out,) = call(bind(kv_halo_kernel, z), [((z.halo * 2 * tok, z.cw), BF16)], kv_got)
    kv_halo = shifted(kv_out, group)
    (qd_out,) = call(bind(qd_halo_kernel, z), [((z.halo * z.rows, z.cw), BF16)], (*qd_got, *kv_got))
    qd_halo = shifted(qd_out, -group)

    def tile_outs(count):
        tile = ((count * z.pairs, tok, z.wide), F32)
        row = ((count * z.pairs, z.wide), F32)
        return [tile, tile, row, row, row]

    near, far = len(z.near), len(z.far)
    unit = 2 * 128 * tok * z.wide
    own_k, own_v, bias_near, bias_far, codes = call(
        bind(bias_kernel, z),
        [((group * tok, z.cw), BF16)] * 2
        + [((near * z.pairs, tok, z.wide), F32), ((far * z.pairs, tok, z.wide), F32)]
        + [((group * CODE_ROWS, z.wide), F32)],
        (*kv_got, bias_table),
        scratch=[pltpu.VMEM((group * span * z.hg * 8, z.wide), F32)],
    )
    qm, dom, wnear, dnear, *sums = call(
        bind(near_kernel, z),
        [((z.pairs, group * z.wide, 128), BF16)] * 2 + tile_outs(near),
        (*qd_got, own_k, own_v, bias_near),
        flops=2 * near * z.pairs * unit,
    )
    stats, fnear, ffar, wfar, dfar, *_ = call(
        bind(far_kernel, z),
        [((2, group * z.pairs, z.wide), F32), ((near * z.pairs, z.wide), F32), ((far * z.pairs, z.wide), F32)]
        + tile_outs(far),
        (kv_halo, qm, dom, bias_far, *sums),
        flops=2 * far * z.pairs * unit,
    )
    stats_halo = [lax.ppermute(stats, "seq", neighbours(n)) for n in range(2)]
    p16, s16, gb = call(
        bind(own_kernel, z),
        [
            ((z.pairs, group * tok, group * z.wide), BF16),
            ((z.pairs, z.ext * tok, group * z.wide), BF16),
            ((8, buckets), F32),
        ],
        (codes, stats, fnear, ffar, wnear, dnear, wfar, dfar),
        scratch=[pltpu.VMEM((group * span * z.hg * 8, z.wide), F32)],
    )
    by = group
    while by < blocks:
        other = swap(gb, by)
        gb = added(gb, other)
        by = by * 2
    sums_of = [gb] + [swap(gb, k, "head") for k in range(1, sides)]
    (dq,) = call(
        bind(grad_q_kernel, z),
        [((group * tok, z.cw), BF16)],
        (own_k, kv_halo, s16),
        flops=(near + far) * z.pairs * unit,
    )
    lanes_of = ((z.pairs, group * tok, z.halo * z.wide), BF16)
    rows_of = ((z.pairs, z.halo * z.wide, 128), BF16)
    halo_terms = call(
        bind(tail_kernel, z),
        [rows_of, rows_of, lanes_of, lanes_of],
        (own_k, own_v, qd_halo, *stats_halo, bias_table),
        scratch=[pltpu.VMEM((far * z.hg * 8, z.wide), F32)],
        flops=2 * far * z.pairs * unit,
    )
    dk, dv = call(
        bind(grad_kv_kernel, z),
        [((group * tok, z.cw), BF16)] * 2,
        (qm, dom, p16, s16, *halo_terms),
        flops=2 * (near + far) * z.pairs * unit,
    )
    ret = call(
        bind(seal_kernel, z, sides), [((3 * tok + sides * CODE_ROWS, z.cw), BF16)] * group, (dq, dk, dv, *sums_of)
    )
    ret_got = [ret[0]] + [swap(ret[k], k) for k in range(1, group)]
    return call(
        bind(unpack_kernel, z, sides),
        [((tok, width), BF16)] * 3 + [((heads * sides, buckets), F32)],
        ret_got,
        out_space=hbm,
        scratch=[pltpu.VMEM((heads * sides, buckets), F32), pltpu.SemaphoreType.DMA((3 * group + 1,))],
    )


def solution(mesh):
    placed = (
        P("seq", "head"),
        P("seq", "head"),
        P("seq", "head"),
        P("seq", "head"),
        P("head", None),
        P("seq", None, None),
        P("seq", None),
    )

    return jax.shard_map(
        body,
        mesh=mesh,
        in_specs=placed,
        out_specs=(P("seq", "head"), P("seq", "head"), P("seq", "head"), P()),
        check_vma=False,
    )
```

```python
import math

import jax
import jax.numpy as jnp
from jax import lax
from jax.experimental import pallas as pl
from jax.experimental.pallas import tpu as pltpu
from jax.sharding import PartitionSpec as P


F32 = jnp.float32
BF16 = jnp.bfloat16
NEG = -1e30
NT = (((1,), (1,)), ((), ()))
NN = (((1,), (0,)), ((), ()))
CODE_ROWS = 16
VMEM_BYTES = 67043328


def dot(a, b, dims):
    return lax.dot_general(a, b, dims, preferred_element_type=F32)


def at(start, size):
    return pl.ds(pl.multiple_of(start, size), size)


def call(kernel, outs, args, scratch=(), spaces=None, out_space=pltpu.VMEM, flops=0, limit=16 << 20):
    spaces = spaces or [pltpu.VMEM] * len(args)
    moved = sum(a.size * a.dtype.itemsize for a in args)
    args = [
        pltpu.with_memory_space_constraint(a, s) if s == pltpu.VMEM else a for a, s in zip(args, spaces, strict=True)
    ]
    return pl.pallas_call(
        kernel,
        out_shape=tuple(out_space(s, d) for s, d in outs),
        in_specs=[pl.BlockSpec(memory_space=s) for s in spaces],
        out_specs=tuple(pl.BlockSpec(memory_space=out_space) for _ in outs),
        scratch_shapes=list(scratch),
        compiler_params=pltpu.CompilerParams(vmem_limit_bytes=limit),
        cost_estimate=pl.CostEstimate(flops=flops, bytes_accessed=moved, transcendentals=0),
    )(*args)


class Sizes:
    def __init__(self, tok, width, heads, span, buckets, group):
        self.tok, self.width, self.heads, self.span, self.buckets = tok, width, heads, span, buckets
        self.group = group
        self.hd = width // heads
        self.hg = heads // group
        self.cw = self.hg * self.hd
        self.pairs = self.hg // 2
        self.scale = self.hd ** (-0.5)
        self.halo = span - 1
        self.ext = group + self.halo
        self.wide = 2 * tok
        self.rows = 2 * tok + CODE_ROWS
        self.near = [(i, s) for i in range(group) for s in range(span) if s <= i]
        self.far = [(i, s) for i in range(group) for s in range(span) if s > i]
        assert heads % group == 0 and self.hg % 2 == 0 and 2 * self.hd == 128
        assert tok == 128 and buckets == 128 and group >= self.halo and self.hg <= 8
        assert math.frexp(self.scale)[0] == 0.5

    def me(self):
        return lax.rem(lax.axis_index("seq"), self.group)


def pack_kernel(z, q, k, v, d, bias, ids, mask, *refs):
    kv, qd = refs[: z.group], refs[z.group : 2 * z.group]
    table, slots, flags, sem = refs[2 * z.group :]
    index = lax.axis_index("seq")
    me = z.me()
    copies = [
        pltpu.make_async_copy(ids.at[0], slots, sem.at[0]),
        pltpu.make_async_copy(mask, flags, sem.at[1]),
        pltpu.make_async_copy(bias, table, sem.at[2]),
    ]
    for sources, dst in (((k, v), kv), ((q, d), qd)):
        for g in range(z.group):
            cols = at((me ^ g) * z.cw, z.cw)
            for n, src in enumerate(sources):
                rows = pl.ds(n * z.tok, z.tok)
                copies.append(pltpu.make_async_copy(src.at[:, cols], dst[g].at[rows, :], sem.at[len(copies)]))
    for copy in copies:
        copy.start()
    for copy in copies[:2]:
        copy.wait()
    rows = []
    for s in range(z.span):
        valid = True if s == 0 else (flags[0, s] == 1) & (index >= s)
        rows.append(jnp.where(valid, slots[s : s + 1, :] + 1, 0))
    rows.append(jnp.zeros((CODE_ROWS - z.span, z.wide), jnp.int32))
    codes = jnp.concatenate(rows, axis=0).astype(F32).astype(BF16)
    for g in range(z.group):
        kv[g][2 * z.tok :, :] = codes
    for copy in copies[2:]:
        copy.wait()


def kv_halo_kernel(z, *refs):
    out = refs[-1]
    me = z.me()
    first = z.group - z.halo
    for k in range(z.group):
        j = me ^ k

        @pl.when(j >= first)
        def _():
            out[at((j - first) * 2 * z.tok, 2 * z.tok), :] = refs[k][0 : 2 * z.tok, :]


def qd_halo_kernel(z, *refs):
    qd, kv, out = refs[: z.group], refs[z.group : -1], refs[-1]
    me = z.me()
    for k in range(z.group):
        j = me ^ k

        @pl.when(j < z.halo)
        def _():
            top = pl.multiple_of(j * z.rows, 16)
            out[pl.ds(top, 2 * z.tok), :] = qd[k][...]
            out[pl.ds(top + 2 * z.tok, CODE_ROWS), :] = kv[k][2 * z.tok :, :]


def onehot_of(codes, z):
    slots = lax.broadcasted_iota(jnp.int32, (z.buckets, codes.shape[1]), 0) + 1
    return jnp.where(codes.astype(jnp.int32) == slots, 1.0, 0.0).astype(BF16)


def thirds(x):
    hi = x.astype(BF16)
    rest = x - hi.astype(F32)
    mid = rest.astype(BF16)
    low = (rest - mid.astype(F32)).astype(BF16)
    return jnp.concatenate([hi.astype(F32), mid.astype(F32), low.astype(F32)], axis=0).astype(BF16)


def by_offset(split, codes, z):
    got = dot(split, onehot_of(codes, z), NN)
    return got[0:8] + got[8:16] + got[16:24] + jnp.where(codes == 0.0, NEG, 0.0)


def masked_pair(x, z):
    lane = lax.broadcasted_iota(jnp.int32, x.shape, 1)
    zero = jnp.zeros_like(x)
    return jnp.concatenate([jnp.where(lane < z.hd, x, zero), jnp.where(lane < z.hd, zero, x)], axis=0)


def slanted(row, z):
    return pltpu.roll(jnp.broadcast_to(row, (8, z.wide)), z.tok + 1, 1, stride=1, stride_axis=0)


def toeplitz(base, z):
    tok = z.tok
    lane = lax.broadcasted_iota(jnp.int32, (8, tok), 1)
    low, high = base[:, 0:tok], base[:, tok:]
    tiles = [low]
    for g in range(1, tok // 8):
        tiles.append(pltpu.roll(jnp.where(lane >= tok - 8 * g, high, low), 8 * g, 1))
    return jnp.concatenate(tiles, axis=0)


def my_table(table, z):
    head = lax.broadcasted_iota(jnp.int32, (8, z.buckets), 0)
    rows = jnp.zeros((8, z.buckets), F32)
    for h in range(z.hg):
        rows = jnp.where(head == h, table[pl.ds(z.me() * z.hg + h, 1), :], rows)
    return rows


def slant_tables(z, table, code_rows, bases):
    split = thirds(my_table(table, z))
    for n, codes in enumerate(code_rows):
        rows = by_offset(split, codes, z)
        for h in range(z.hg):
            at_row = (n * z.hg + h) * 8
            bases[at_row : at_row + 8, :] = slanted(rows[h : h + 1, :], z)


def diagonals(x, z):
    tok = z.tok
    lane = lax.broadcasted_iota(jnp.int32, (8, tok), 1)
    total = x[tok - 8 :]
    high = jnp.zeros((8, tok), F32)
    for g in range(tok // 8 - 1):
        by = tok - 8 - 8 * g
        part = pltpu.roll(x[8 * g : 8 * g + 8], by, 1)
        total = total + part
        high = high + jnp.where(lane < by, part, 0.0)
    return total - high, high


def aligned(both):
    left = 7 - (lax.broadcasted_iota(jnp.int32, both.shape, 0) & 7)
    for bit in (1, 2, 4):
        both = jnp.where((left & bit) != 0, pltpu.roll(both, bit, 1), both)
    return both


def causal(z):
    row = lax.broadcasted_iota(jnp.int32, (z.tok, z.wide), 0)
    col = lax.broadcasted_iota(jnp.int32, (z.tok, z.wide), 1) % z.tok
    return row <= col


def folded(x, how):
    return how(how(x.reshape(x.shape[0] // 8, 8, x.shape[1]), 0), 0, keepdims=True)


def bias_rows(z, bases, n, pair):
    rows = [toeplitz(bases[(n * z.hg + 2 * pair + e) * 8 : (n * z.hg + 2 * pair + e + 1) * 8, :], z) for e in range(2)]
    return jnp.concatenate(rows, axis=1)


def bias_kernel(z, *refs):
    kv, table = refs[: z.group], refs[z.group]
    keys, values, near, far, codes, bases = refs[z.group + 1 :]
    tok = z.tok
    me = z.me()
    for k in range(z.group):
        j = me ^ k
        keys[at(j * tok, tok), :] = kv[k][0:tok, :]
        values[at(j * tok, tok), :] = kv[k][tok : 2 * tok, :]
        codes[at(j * CODE_ROWS, CODE_ROWS), :] = kv[k][2 * tok :, :].astype(F32)
    tables = [(i, s) for i in range(z.group) for s in range(z.span)]
    slant_tables(z, table, [codes[i * CODE_ROWS + s : i * CODE_ROWS + s + 1, :] for i, s in tables], bases)
    for tiles, out in ((z.near, near), (z.far, far)):
        for t, (i, s) in enumerate(tiles):
            for pair in range(z.pairs):
                bias = bias_rows(z, bases, i * z.span + s, pair)
                out[t * z.pairs + pair] = jnp.where(causal(z), bias, NEG) if s == 0 else bias


def forward_tile(key, value, q, d, bias, row, outs):
    weights, dprobs, tops, totals, accums = outs
    scores = dot(key, q, NT) + bias[row]
    top = folded(scores, jnp.max)
    w = jnp.exp(scores - top)
    dprob = dot(value, d, NT)
    weights[row] = w
    dprobs[row] = dprob
    tops[pl.ds(row, 1), :] = top
    totals[pl.ds(row, 1), :] = folded(w, jnp.sum)
    accums[pl.ds(row, 1), :] = folded(w * dprob, jnp.sum)


def near_kernel(z, *refs):
    qd, keys, values, bias = refs[: z.group], *refs[z.group : z.group + 3]
    qm, dom, *outs = refs[z.group + 3 :]
    tok = z.tok
    me = z.me()
    for k in range(z.group):
        j = me ^ k
        for pair in range(z.pairs):
            lanes = slice(pair * 128, (pair + 1) * 128)
            rows = at(j * z.wide, z.wide)
            qm[pair, rows, :] = masked_pair(qd[k][0:tok, lanes] * jnp.asarray(z.scale, BF16), z)
            dom[pair, rows, :] = masked_pair(qd[k][tok : 2 * tok, lanes], z)

    def each(pair, _):
        lanes = at(pair * 128, 128)
        for t, (i, s) in enumerate(z.near):
            rows = slice((i - s) * tok, (i - s + 1) * tok)
            wide = slice(i * z.wide, (i + 1) * z.wide)
            forward_tile(
                keys[rows, lanes], values[rows, lanes], qm[pair, wide, :], dom[pair, wide, :],
                bias, t * z.pairs + pair, outs,
            )
        return 0

    lax.fori_loop(0, z.pairs, each, 0)


def far_kernel(z, halo, qm, dom, bias, tops, totals, accums, stats, fnear, ffar, *outs):
    tok = z.tok

    def each(pair, _):
        lanes = at(pair * 128, 128)
        for t, (i, s) in enumerate(z.far):
            b = z.halo + i - s
            wide = slice(i * z.wide, (i + 1) * z.wide)
            forward_tile(
                halo[2 * b * tok : (2 * b + 1) * tok, lanes], halo[(2 * b + 1) * tok : (2 * b + 2) * tok, lanes],
                qm[pair, wide, :], dom[pair, wide, :], bias, t * z.pairs + pair, outs,
            )
        for i in range(z.group):
            mine = [(tops, totals, accums, fnear, t) for t, (n, _) in enumerate(z.near) if n == i]
            mine += [(outs[2], outs[3], outs[4], ffar, t) for t, (n, _) in enumerate(z.far) if n == i]
            rows = [pl.ds(t * z.pairs + pair, 1) for *_, t in mine]
            peaks = [m[0][row, :] for m, row in zip(mine, rows, strict=True)]
            top = peaks[0]
            for peak in peaks[1:]:
                top = jnp.maximum(top, peak)
            total = jnp.zeros_like(top)
            accum = jnp.zeros_like(top)
            for m, row, peak in zip(mine, rows, peaks, strict=True):
                share = jnp.exp(peak - top)
                total = total + share * m[1][row, :]
                accum = accum + share * m[2][row, :]
            lse = top + jnp.log(total)
            for m, row, peak in zip(mine, rows, peaks, strict=True):
                m[3][row, :] = jnp.exp(peak - lse)
            stats[0, pl.ds(i * z.pairs + pair, 1), :] = lse
            stats[1, pl.ds(i * z.pairs + pair, 1), :] = accum / total
        return 0

    lax.fori_loop(0, z.pairs, each, 0)


def own_kernel(z, codes, stats, fnear, ffar, wnear, dnear, wfar, dfar, p16, s16, gb, offs):
    tok, span = z.tok, z.span

    def each(pair, _):
        for i in range(z.group):
            wide = slice(i * z.wide, (i + 1) * z.wide)
            delta = stats[1, pl.ds(i * z.pairs + pair, 1), :]
            for s in range(span):
                close = s <= i
                t = (z.near if close else z.far).index((i, s)) * z.pairs + pair
                w, d, f = (wnear, dnear, fnear) if close else (wfar, dfar, ffar)
                prob = w[t] * f[pl.ds(t, 1), :]
                dscore = prob * (d[t] - delta)
                rows = slice((z.halo + i - s) * tok, (z.halo + i - s + 1) * tok)
                s16[pair, rows, wide] = dscore.astype(BF16)
                if close:
                    p16[pair, (i - s) * tok : (i - s + 1) * tok, wide] = prob.astype(BF16)
                for e in range(2):
                    low, high = diagonals(dscore[:, e * tok : (e + 1) * tok], z)
                    row = at(((i * span + s) * z.hg + 2 * pair + e) * 8, 8)
                    offs[row, 0:tok] = low
                    offs[row, tok:] = high
        return 0

    lax.fori_loop(0, z.pairs, each, 0)
    head = lax.broadcasted_iota(jnp.int32, (8, z.wide), 0)
    total = jnp.zeros((8, z.buckets), F32)
    for n in range(z.group * span):
        both = aligned(offs[n * z.hg * 8 : (n + 1) * z.hg * 8, :])
        sums = jnp.zeros((8, z.wide), F32)
        for h in range(z.hg):
            sums = sums + jnp.where(head == h, both[8 * h : 8 * h + 8].sum(axis=0, keepdims=True), 0.0)
        row = n // span * CODE_ROWS + n % span
        got = dot(thirds(sums), onehot_of(codes[row : row + 1, :], z), NT)
        total = total + (got[0:8] + got[8:16] + got[16:24])
    gb[...] = total


def grad_q_kernel(z, keys, halo, s16, dq):
    tok, span = z.tok, z.span

    def each(pair, _):
        lanes = at(pair * 128, 128)
        blocks = [halo[2 * b * tok : (2 * b + 1) * tok, lanes] for b in range(z.halo)]
        blocks += [keys[j * tok : (j + 1) * tok, lanes] for j in range(z.group)]
        turned = jnp.concatenate([block.T for block in blocks], axis=1)
        for i in range(z.group):
            window = slice(i * tok, (i + span) * tok)
            cross = dot(turned[:, window], s16[pair, window, i * z.wide : (i + 1) * z.wide], NN)
            both = jnp.concatenate([cross[0 : z.hd, 0:tok], cross[z.hd :, tok:]], axis=0)
            dq[i * tok : (i + 1) * tok, lanes] = (z.scale * both.T).astype(BF16)
        return 0

    lax.fori_loop(0, z.pairs, each, 0)


def tail_kernel(z, keys, values, halo, stats, table, qh, dh, ph, sh, bases):
    tok, span = z.tok, z.span
    tables = [(b, s) for b in range(z.halo) for s in range(b + 1, span)]
    rows = []
    for b in range(z.halo):
        codes = halo[b * z.rows + 2 * tok : (b + 1) * z.rows, :].astype(F32)
        rows += [codes[s : s + 1, :] for s in range(b + 1, span)]
    slant_tables(z, table, rows, bases)
    for pair in range(z.pairs):
        lanes = slice(pair * 128, (pair + 1) * 128)
        for b in range(z.halo):
            top = b * z.rows
            wide = slice(b * z.wide, (b + 1) * z.wide)
            q = masked_pair(halo[top : top + tok, lanes] * jnp.asarray(z.scale, BF16), z)
            d = masked_pair(halo[top + tok : top + 2 * tok, lanes], z)
            qh[pair, wide, :] = q
            dh[pair, wide, :] = d
            u = b * z.pairs + pair
            lse, delta = stats[0, u : u + 1, :], stats[1, u : u + 1, :]
            for s in range(b + 1, span):
                j = z.group + b - s
                block = slice(j * tok, (j + 1) * tok)
                bias = bias_rows(z, bases, tables.index((b, s)), pair)
                prob = jnp.exp(dot(keys[block, lanes], q, NT) + bias - lse)
                dscore = prob * (dot(values[block, lanes], d, NT) - delta)
                ph[pair, block, wide] = prob.astype(BF16)
                sh[pair, block, wide] = dscore.astype(BF16)


def grad_kv_kernel(z, qm, dom, p16, s16, qh, dh, ph, sh, dk, dv):
    tok = z.tok

    def each(pair, _):
        lanes = at(pair * 128, 128)
        for j in range(z.group):
            rows = slice(j * tok, (j + 1) * tok)
            ext = slice((z.halo + j) * tok, (z.halo + j + 1) * tok)
            near = slice(j * z.wide, z.group * z.wide)
            gk = dot(s16[pair, ext, near], qm[pair, near, :], NN)
            gv = dot(p16[pair, rows, near], dom[pair, near, :], NN)
            count = min(z.halo, j + z.span - z.group)
            if count > 0:
                past = slice(0, count * z.wide)
                gk = gk + dot(sh[pair, rows, past], qh[pair, past, :], NN)
                gv = gv + dot(ph[pair, rows, past], dh[pair, past, :], NN)
            dk[rows, lanes] = gk.astype(BF16)
            dv[rows, lanes] = gv.astype(BF16)
        return 0

    lax.fori_loop(0, z.pairs, each, 0)


def seal_kernel(z, sides, grads, *refs):
    sources, sums, sends = refs[:grads], refs[grads : grads + sides], refs[grads + sides :]
    tok = z.tok
    packs = []
    for ref in sums:
        split = thirds(ref[...]).astype(F32)
        low = jnp.concatenate([split[16:24], jnp.zeros((8, z.buckets), F32)], axis=0)
        packs.append(jnp.concatenate([split[0:16], low], axis=1).astype(BF16))
    me = z.me()
    for k in range(z.group):
        rows = at((me ^ k) * tok, tok)
        for n, ref in enumerate(sources):
            sends[k][n * tok : (n + 1) * tok, :] = ref[rows, :]
        for n, pack in enumerate(packs):
            top = grads * tok + n * CODE_ROWS
            sends[k][top : top + CODE_ROWS, :] = pack


def add_kernel(*refs):
    total = refs[0][...]
    for ref in refs[1:-1]:
        total = total + ref[...]
    refs[-1][...] = total


def unpack_kernel(z, grads, *refs):
    got, outs, sem = refs[: z.group], refs[z.group : z.group + grads], refs[-1]
    me = z.me()
    copies = []
    for k in range(z.group):
        cols = at((me ^ k) * z.cw, z.cw)
        for n, out in enumerate(outs):
            src = got[k].at[n * z.tok : (n + 1) * z.tok, :]
            copies.append(pltpu.make_async_copy(src, out.at[:, cols], sem.at[len(copies)]))
    for copy in copies:
        copy.start()
    return copies


def unpack_kv_kernel(z, *refs):
    for copy in unpack_kernel(z, 2, *refs):
        copy.wait()


def unpack_q_kernel(z, sides, *refs):
    got, (out, gb, held, sem) = refs[: z.group], refs[z.group :]
    me = z.me()
    copies = unpack_kernel(z, 1, *got, out, sem)
    owner = lax.broadcasted_iota(jnp.int32, held.shape, 0) // z.hg
    total = jnp.zeros(held.shape, F32)
    for k in range(z.group):
        for n in range(sides):
            top = z.tok + n * CODE_ROWS
            rows = got[k][top : top + CODE_ROWS, :].astype(F32)
            sums = rows[0:8, 0 : z.buckets] + rows[8:16, 0 : z.buckets] + rows[0:8, z.buckets :]
            wide = jnp.concatenate([sums[0 : z.hg]] * (held.shape[0] // z.hg), axis=0)
            side = lax.axis_index("head") ^ n
            total = total + jnp.where(owner == side * z.group + (me ^ k), wide, 0.0)
    held[...] = total
    last = pltpu.make_async_copy(held, gb, sem.at[len(copies)])
    last.start()
    for copy in copies + [last]:
        copy.wait()


def bind(kernel, *fixed):
    def bound(*refs):
        return kernel(*fixed, *refs)

    return bound


def body(queries, keys, values, grad_out, bias_table, bucket_ids, block_mask):
    tok, width = queries.shape
    heads, buckets = bias_table.shape
    span = block_mask.shape[1]
    group = span
    z = Sizes(tok, width, heads, span, buckets, group)
    blocks = lax.axis_size("seq")
    sides = lax.axis_size("head")
    assert blocks % group == 0 and (blocks & (blocks - 1)) == 0 and (sides & (sides - 1)) == 0

    def swap(value, by, axis="seq"):
        return lax.ppermute(value, axis, [(i, i ^ by) for i in range(lax.axis_size(axis))])

    def shifted(value, by):
        return lax.ppermute(value, "seq", [(i, (i + by) % blocks) for i in range(blocks)])

    def added(*terms):
        (total,) = call(add_kernel, [(terms[0].shape, terms[0].dtype)], terms)
        return total

    hbm = pltpu.HBM
    pack_bytes = group * (z.rows + 2 * tok) * z.cw * 2
    packed = call(
        bind(pack_kernel, z),
        [((z.rows, z.cw), BF16)] * group + [((2 * tok, z.cw), BF16)] * group + [((heads, buckets), F32)],
        (queries, keys, values, grad_out, bias_table, bucket_ids, block_mask),
        spaces=[hbm] * 7,
        scratch=[
            pltpu.VMEM((span, z.wide), jnp.int32),
            pltpu.SMEM((1, span), jnp.int32),
            pltpu.SemaphoreType.DMA((4 * group + 3,)),
        ],
        limit=VMEM_BYTES - pack_bytes - (520 << 10),
    )
    kv, qd, table = packed[:group], packed[group : 2 * group], packed[2 * group]
    kv_got = [kv[0]] + [swap(kv[k], k) for k in range(1, group)]
    qd_got = [qd[0]] + [swap(qd[k], k) for k in range(1, group)]
    (kv_out,) = call(bind(kv_halo_kernel, z), [((z.halo * 2 * tok, z.cw), BF16)], kv_got)
    kv_halo = shifted(kv_out, group)
    (qd_out,) = call(bind(qd_halo_kernel, z), [((z.halo * z.rows, z.cw), BF16)], (*qd_got, *kv_got))
    qd_halo = shifted(qd_out, -group)

    def tile_outs(count):
        tile = ((count * z.pairs, tok, z.wide), F32)
        row = ((count * z.pairs, z.wide), F32)
        return [tile, tile, row, row, row]

    near, far = len(z.near), len(z.far)
    unit = 2 * 128 * tok * z.wide
    own_k, own_v, bias_near, bias_far, codes = call(
        bind(bias_kernel, z),
        [((group * tok, z.cw), BF16)] * 2
        + [((near * z.pairs, tok, z.wide), F32), ((far * z.pairs, tok, z.wide), F32)]
        + [((group * CODE_ROWS, z.wide), F32)],
        (*kv_got, table),
        scratch=[pltpu.VMEM((group * span * z.hg * 8, z.wide), F32)],
    )
    qm, dom, wnear, dnear, *sums = call(
        bind(near_kernel, z),
        [((z.pairs, group * z.wide, 128), BF16)] * 2 + tile_outs(near),
        (*qd_got, own_k, own_v, bias_near),
        flops=2 * near * z.pairs * unit,
    )
    stats, fnear, ffar, wfar, dfar, *_ = call(
        bind(far_kernel, z),
        [((2, group * z.pairs, z.wide), F32), ((near * z.pairs, z.wide), F32), ((far * z.pairs, z.wide), F32)]
        + tile_outs(far),
        (kv_halo, qm, dom, bias_far, *sums),
        flops=2 * far * z.pairs * unit,
    )
    stats_halo = shifted(stats, -group)
    p16, s16, gb = call(
        bind(own_kernel, z),
        [
            ((z.pairs, group * tok, group * z.wide), BF16),
            ((z.pairs, z.ext * tok, group * z.wide), BF16),
            ((8, buckets), F32),
        ],
        (codes, stats, fnear, ffar, wnear, dnear, wfar, dfar),
        scratch=[pltpu.VMEM((group * span * z.hg * 8, z.wide), F32)],
    )
    by = group
    while by < blocks:
        other = swap(gb, by)
        gb = added(gb, other)
        by = by * 2
    sums_of = [gb] + [swap(gb, k, "head") for k in range(1, sides)]
    (dq,) = call(
        bind(grad_q_kernel, z),
        [((group * tok, z.cw), BF16)],
        (own_k, kv_halo, s16),
        flops=(near + far) * z.pairs * unit,
    )
    lanes_of = ((z.pairs, group * tok, z.halo * z.wide), BF16)
    rows_of = ((z.pairs, z.halo * z.wide, 128), BF16)
    halo_terms = call(
        bind(tail_kernel, z),
        [rows_of, rows_of, lanes_of, lanes_of],
        (own_k, own_v, qd_halo, stats_halo, table),
        scratch=[pltpu.VMEM((far * z.hg * 8, z.wide), F32)],
        flops=2 * far * z.pairs * unit,
    )
    dk, dv = call(
        bind(grad_kv_kernel, z),
        [((group * tok, z.cw), BF16)] * 2,
        (qm, dom, p16, s16, *halo_terms),
        flops=2 * (near + far) * z.pairs * unit,
    )
    ret = call(bind(seal_kernel, z, 0, 2), [((2 * tok, z.cw), BF16)] * group, (dk, dv))
    kv_back = [ret[0]] + [swap(ret[k], k) for k in range(1, group)]
    ret = call(bind(seal_kernel, z, sides, 1), [((tok + sides * CODE_ROWS, z.cw), BF16)] * group, (dq, *sums_of))
    q_back = [ret[0]] + [swap(ret[k], k) for k in range(1, group)]
    grad_k, grad_v = call(
        bind(unpack_kv_kernel, z),
        [((tok, width), BF16)] * 2,
        kv_back,
        out_space=hbm,
        scratch=[pltpu.SemaphoreType.DMA((2 * group,))],
    )
    grad_q, grad_bias = call(
        bind(unpack_q_kernel, z, sides),
        [((tok, width), BF16), ((heads * sides, buckets), F32)],
        q_back,
        out_space=hbm,
        scratch=[pltpu.VMEM((heads * sides, buckets), F32), pltpu.SemaphoreType.DMA((group + 1,))],
    )
    return grad_q, grad_k, grad_v, grad_bias


def solution(mesh):
    placed = (
        P("seq", "head"),
        P("seq", "head"),
        P("seq", "head"),
        P("seq", "head"),
        P("head", None),
        P("seq", None, None),
        P("seq", None),
    )

    return jax.shard_map(
        body,
        mesh=mesh,
        in_specs=placed,
        out_specs=(P("seq", "head"), P("seq", "head"), P("seq", "head"), P()),
        check_vma=False,
    )
```

```python
import math

import jax
import jax.numpy as jnp
from jax import lax
from jax.experimental import pallas as pl
from jax.experimental.pallas import tpu as pltpu
from jax.sharding import PartitionSpec as P


F32 = jnp.float32
BF16 = jnp.bfloat16
NEG = -1e30
NT = (((1,), (1,)), ((), ()))
NN = (((1,), (0,)), ((), ()))
CODE_ROWS = 16
VMEM_BYTES = 67043328


def dot(a, b, dims):
    return lax.dot_general(a, b, dims, preferred_element_type=F32)


def at(start, size):
    return pl.ds(pl.multiple_of(start, size), size)


def call(kernel, outs, args, scratch=(), spaces=None, out_space=pltpu.VMEM, flops=0, limit=16 << 20):
    spaces = spaces or [pltpu.VMEM] * len(args)
    moved = sum(a.size * a.dtype.itemsize for a in args)
    args = [
        pltpu.with_memory_space_constraint(a, s) if s == pltpu.VMEM else a for a, s in zip(args, spaces, strict=True)
    ]
    return pl.pallas_call(
        kernel,
        out_shape=tuple(out_space(s, d) for s, d in outs),
        in_specs=[pl.BlockSpec(memory_space=s) for s in spaces],
        out_specs=tuple(pl.BlockSpec(memory_space=out_space) for _ in outs),
        scratch_shapes=list(scratch),
        compiler_params=pltpu.CompilerParams(vmem_limit_bytes=limit),
        cost_estimate=pl.CostEstimate(flops=flops, bytes_accessed=moved, transcendentals=0),
    )(*args)


class Sizes:
    def __init__(self, tok, width, heads, span, buckets, group):
        self.tok, self.width, self.heads, self.span, self.buckets = tok, width, heads, span, buckets
        self.group = group
        self.hd = width // heads
        self.hg = heads // group
        self.cw = self.hg * self.hd
        self.pairs = self.hg // 2
        self.scale = self.hd ** (-0.5)
        self.halo = span - 1
        self.ext = group + self.halo
        self.wide = 2 * tok
        self.rows = 2 * tok + CODE_ROWS
        self.near = [(i, s) for i in range(group) for s in range(span) if s <= i]
        self.far = [(i, s) for i in range(group) for s in range(span) if s > i]
        assert heads % group == 0 and self.hg % 2 == 0 and 2 * self.hd == 128
        assert tok == 128 and buckets == 128 and group >= self.halo and self.hg <= 8
        assert math.frexp(self.scale)[0] == 0.5

    def me(self):
        return lax.rem(lax.axis_index("seq"), self.group)


def pack_kernel(z, q, k, v, d, bias, ids, mask, *refs):
    kv, qd = refs[: z.group], refs[z.group : 2 * z.group]
    table, slots, flags, sem = refs[2 * z.group :]
    index = lax.axis_index("seq")
    me = z.me()
    copies = [
        pltpu.make_async_copy(ids.at[0], slots, sem.at[0]),
        pltpu.make_async_copy(mask, flags, sem.at[1]),
        pltpu.make_async_copy(bias, table, sem.at[2]),
    ]
    for sources, dst in (((k, v), kv), ((q, d), qd)):
        for g in range(z.group):
            cols = at((me ^ g) * z.cw, z.cw)
            for n, src in enumerate(sources):
                rows = pl.ds(n * z.tok, z.tok)
                copies.append(pltpu.make_async_copy(src.at[:, cols], dst[g].at[rows, :], sem.at[len(copies)]))
    for copy in copies:
        copy.start()
    for copy in copies[:2]:
        copy.wait()
    rows = []
    for s in range(z.span):
        valid = True if s == 0 else (flags[0, s] == 1) & (index >= s)
        rows.append(jnp.where(valid, slots[s : s + 1, :] + 1, 0))
    rows.append(jnp.zeros((CODE_ROWS - z.span, z.wide), jnp.int32))
    codes = jnp.concatenate(rows, axis=0).astype(F32).astype(BF16)
    for g in range(z.group):
        kv[g][2 * z.tok :, :] = codes
    for copy in copies[2:]:
        copy.wait()


def kv_halo_kernel(z, *refs):
    out = refs[-1]
    me = z.me()
    first = z.group - z.halo
    for k in range(z.group):
        j = me ^ k

        @pl.when(j >= first)
        def _():
            out[at((j - first) * 2 * z.tok, 2 * z.tok), :] = refs[k][0 : 2 * z.tok, :]


def qd_halo_kernel(z, *refs):
    qd, kv, out = refs[: z.group], refs[z.group : -1], refs[-1]
    me = z.me()
    for k in range(z.group):
        j = me ^ k

        @pl.when(j < z.halo)
        def _():
            top = pl.multiple_of(j * z.rows, 16)
            out[pl.ds(top, 2 * z.tok), :] = qd[k][...]
            out[pl.ds(top + 2 * z.tok, CODE_ROWS), :] = kv[k][2 * z.tok :, :]


def onehot_of(codes, z):
    slots = lax.broadcasted_iota(jnp.int32, (z.buckets, codes.shape[1]), 0) + 1
    return jnp.where(codes.astype(jnp.int32) == slots, 1.0, 0.0).astype(BF16)


def thirds(x):
    hi = x.astype(BF16)
    rest = x - hi.astype(F32)
    mid = rest.astype(BF16)
    low = (rest - mid.astype(F32)).astype(BF16)
    return jnp.concatenate([hi.astype(F32), mid.astype(F32), low.astype(F32)], axis=0).astype(BF16)


def by_offset(split, codes, z):
    got = dot(split, onehot_of(codes, z), NN)
    return got[0:8] + got[8:16] + got[16:24] + jnp.where(codes == 0.0, NEG, 0.0)


def masked_pair(x, z):
    lane = lax.broadcasted_iota(jnp.int32, x.shape, 1)
    zero = jnp.zeros_like(x)
    return jnp.concatenate([jnp.where(lane < z.hd, x, zero), jnp.where(lane < z.hd, zero, x)], axis=0)


def slanted(row, z):
    return pltpu.roll(jnp.broadcast_to(row, (8, z.wide)), z.tok + 1, 1, stride=1, stride_axis=0)


def toeplitz(base, z):
    tok = z.tok
    lane = lax.broadcasted_iota(jnp.int32, (8, tok), 1)
    low, high = base[:, 0:tok], base[:, tok:]
    tiles = [low]
    for g in range(1, tok // 8):
        tiles.append(pltpu.roll(jnp.where(lane >= tok - 8 * g, high, low), 8 * g, 1))
    return jnp.concatenate(tiles, axis=0)


def my_table(table, z):
    head = lax.broadcasted_iota(jnp.int32, (8, z.buckets), 0)
    rows = jnp.zeros((8, z.buckets), F32)
    for h in range(z.hg):
        rows = jnp.where(head == h, table[pl.ds(z.me() * z.hg + h, 1), :], rows)
    return rows


def slant_tables(z, table, code_rows, bases):
    split = thirds(my_table(table, z))
    for n, codes in enumerate(code_rows):
        rows = by_offset(split, codes, z)
        for h in range(z.hg):
            at_row = (n * z.hg + h) * 8
            bases[at_row : at_row + 8, :] = slanted(rows[h : h + 1, :], z)


def diagonals(x, z):
    tok = z.tok
    lane = lax.broadcasted_iota(jnp.int32, (8, tok), 1)
    total = x[tok - 8 :]
    high = jnp.zeros((8, tok), F32)
    for g in range(tok // 8 - 1):
        by = tok - 8 - 8 * g
        part = pltpu.roll(x[8 * g : 8 * g + 8], by, 1)
        total = total + part
        high = high + jnp.where(lane < by, part, 0.0)
    return total - high, high


def aligned(both):
    left = 7 - (lax.broadcasted_iota(jnp.int32, both.shape, 0) & 7)
    for bit in (1, 2, 4):
        both = jnp.where((left & bit) != 0, pltpu.roll(both, bit, 1), both)
    return both


def causal(z):
    row = lax.broadcasted_iota(jnp.int32, (z.tok, z.wide), 0)
    col = lax.broadcasted_iota(jnp.int32, (z.tok, z.wide), 1) % z.tok
    return row <= col


def folded(x, how):
    return how(how(x.reshape(x.shape[0] // 8, 8, x.shape[1]), 0), 0, keepdims=True)


def bias_rows(z, bases, n, pair):
    rows = [toeplitz(bases[(n * z.hg + 2 * pair + e) * 8 : (n * z.hg + 2 * pair + e + 1) * 8, :], z) for e in range(2)]
    return jnp.concatenate(rows, axis=1)


def bias_kernel(z, *refs):
    kv, table = refs[: z.group], refs[z.group]
    keys, values, near, far, codes, bases = refs[z.group + 1 :]
    tok = z.tok
    me = z.me()
    for k in range(z.group):
        j = me ^ k
        keys[at(j * tok, tok), :] = kv[k][0:tok, :]
        values[at(j * tok, tok), :] = kv[k][tok : 2 * tok, :]
        codes[at(j * CODE_ROWS, CODE_ROWS), :] = kv[k][2 * tok :, :].astype(F32)
    tables = [(i, s) for i in range(z.group) for s in range(z.span)]
    slant_tables(z, table, [codes[i * CODE_ROWS + s : i * CODE_ROWS + s + 1, :] for i, s in tables], bases)
    for tiles, out in ((z.near, near), (z.far, far)):
        for t, (i, s) in enumerate(tiles):
            for pair in range(z.pairs):
                bias = bias_rows(z, bases, i * z.span + s, pair)
                out[t * z.pairs + pair] = jnp.where(causal(z), bias, NEG) if s == 0 else bias


def forward_tile(key, value, q, d, bias, row, outs):
    weights, dprobs, tops, totals, accums = outs
    scores = dot(key, q, NT) + bias[row]
    top = folded(scores, jnp.max)
    w = jnp.exp(scores - top)
    dprob = dot(value, d, NT)
    weights[row] = w
    dprobs[row] = dprob
    tops[pl.ds(row, 1), :] = top
    totals[pl.ds(row, 1), :] = folded(w, jnp.sum)
    accums[pl.ds(row, 1), :] = folded(w * dprob, jnp.sum)


def near_kernel(z, *refs):
    qd, keys, values, bias = refs[: z.group], *refs[z.group : z.group + 3]
    qm, dom, *outs = refs[z.group + 3 :]
    tok = z.tok
    me = z.me()
    for k in range(z.group):
        j = me ^ k
        for pair in range(z.pairs):
            lanes = slice(pair * 128, (pair + 1) * 128)
            rows = at(j * z.wide, z.wide)
            qm[pair, rows, :] = masked_pair(qd[k][0:tok, lanes] * jnp.asarray(z.scale, BF16), z)
            dom[pair, rows, :] = masked_pair(qd[k][tok : 2 * tok, lanes], z)

    def each(pair, _):
        lanes = at(pair * 128, 128)
        for t, (i, s) in enumerate(z.near):
            rows = slice((i - s) * tok, (i - s + 1) * tok)
            wide = slice(i * z.wide, (i + 1) * z.wide)
            forward_tile(
                keys[rows, lanes], values[rows, lanes], qm[pair, wide, :], dom[pair, wide, :],
                bias, t * z.pairs + pair, outs,
            )
        return 0

    lax.fori_loop(0, z.pairs, each, 0)


def far_kernel(z, halo, qm, dom, bias, tops, totals, accums, stats, fnear, ffar, *outs):
    tok = z.tok

    def each(pair, _):
        lanes = at(pair * 128, 128)
        for t, (i, s) in enumerate(z.far):
            b = z.halo + i - s
            wide = slice(i * z.wide, (i + 1) * z.wide)
            forward_tile(
                halo[2 * b * tok : (2 * b + 1) * tok, lanes], halo[(2 * b + 1) * tok : (2 * b + 2) * tok, lanes],
                qm[pair, wide, :], dom[pair, wide, :], bias, t * z.pairs + pair, outs,
            )
        for i in range(z.group):
            mine = [(tops, totals, accums, fnear, t) for t, (n, _) in enumerate(z.near) if n == i]
            mine += [(outs[2], outs[3], outs[4], ffar, t) for t, (n, _) in enumerate(z.far) if n == i]
            rows = [pl.ds(t * z.pairs + pair, 1) for *_, t in mine]
            peaks = [m[0][row, :] for m, row in zip(mine, rows, strict=True)]
            top = peaks[0]
            for peak in peaks[1:]:
                top = jnp.maximum(top, peak)
            total = jnp.zeros_like(top)
            accum = jnp.zeros_like(top)
            for m, row, peak in zip(mine, rows, peaks, strict=True):
                share = jnp.exp(peak - top)
                total = total + share * m[1][row, :]
                accum = accum + share * m[2][row, :]
            lse = top + jnp.log(total)
            for m, row, peak in zip(mine, rows, peaks, strict=True):
                m[3][row, :] = jnp.exp(peak - lse)
            stats[0, pl.ds(i * z.pairs + pair, 1), :] = lse
            stats[1, pl.ds(i * z.pairs + pair, 1), :] = accum / total
        return 0

    lax.fori_loop(0, z.pairs, each, 0)


def own_kernel(z, codes, stats, fnear, ffar, wnear, dnear, wfar, dfar, p16, s16, gb, offs):
    tok, span = z.tok, z.span

    def each(pair, _):
        for i in range(z.group):
            wide = slice(i * z.wide, (i + 1) * z.wide)
            delta = stats[1, pl.ds(i * z.pairs + pair, 1), :]
            for s in range(span):
                close = s <= i
                t = (z.near if close else z.far).index((i, s)) * z.pairs + pair
                w, d, f = (wnear, dnear, fnear) if close else (wfar, dfar, ffar)
                prob = w[t] * f[pl.ds(t, 1), :]
                dscore = prob * (d[t] - delta)
                rows = slice((z.halo + i - s) * tok, (z.halo + i - s + 1) * tok)
                s16[pair, rows, wide] = dscore.astype(BF16)
                if close:
                    p16[pair, (i - s) * tok : (i - s + 1) * tok, wide] = prob.astype(BF16)
                for e in range(2):
                    low, high = diagonals(dscore[:, e * tok : (e + 1) * tok], z)
                    row = at(((i * span + s) * z.hg + 2 * pair + e) * 8, 8)
                    offs[row, 0:tok] = low
                    offs[row, tok:] = high
        return 0

    lax.fori_loop(0, z.pairs, each, 0)
    head = lax.broadcasted_iota(jnp.int32, (8, z.wide), 0)
    total = jnp.zeros((8, z.buckets), F32)
    for n in range(z.group * span):
        both = aligned(offs[n * z.hg * 8 : (n + 1) * z.hg * 8, :])
        sums = jnp.zeros((8, z.wide), F32)
        for h in range(z.hg):
            sums = sums + jnp.where(head == h, both[8 * h : 8 * h + 8].sum(axis=0, keepdims=True), 0.0)
        row = n // span * CODE_ROWS + n % span
        got = dot(thirds(sums), onehot_of(codes[row : row + 1, :], z), NT)
        total = total + (got[0:8] + got[8:16] + got[16:24])
    gb[...] = total


def grad_q_kernel(z, keys, halo, s16, dq):
    tok, span = z.tok, z.span

    def each(pair, _):
        lanes = at(pair * 128, 128)
        blocks = [halo[2 * b * tok : (2 * b + 1) * tok, lanes] for b in range(z.halo)]
        blocks += [keys[j * tok : (j + 1) * tok, lanes] for j in range(z.group)]
        turned = jnp.concatenate([block.T for block in blocks], axis=1)
        for i in range(z.group):
            window = slice(i * tok, (i + span) * tok)
            cross = dot(turned[:, window], s16[pair, window, i * z.wide : (i + 1) * z.wide], NN)
            both = jnp.concatenate([cross[0 : z.hd, 0:tok], cross[z.hd :, tok:]], axis=0)
            dq[i * tok : (i + 1) * tok, lanes] = (z.scale * both.T).astype(BF16)
        return 0

    lax.fori_loop(0, z.pairs, each, 0)


def tail_kernel(z, keys, values, halo, stats, table, qh, dh, ph, sh, bases):
    tok, span = z.tok, z.span
    tables = [(b, s) for b in range(z.halo) for s in range(b + 1, span)]
    rows = []
    for b in range(z.halo):
        codes = halo[b * z.rows + 2 * tok : (b + 1) * z.rows, :].astype(F32)
        rows += [codes[s : s + 1, :] for s in range(b + 1, span)]
    slant_tables(z, table, rows, bases)
    for pair in range(z.pairs):
        lanes = slice(pair * 128, (pair + 1) * 128)
        for b in range(z.halo):
            top = b * z.rows
            wide = slice(b * z.wide, (b + 1) * z.wide)
            q = masked_pair(halo[top : top + tok, lanes] * jnp.asarray(z.scale, BF16), z)
            d = masked_pair(halo[top + tok : top + 2 * tok, lanes], z)
            qh[pair, wide, :] = q
            dh[pair, wide, :] = d
            u = b * z.pairs + pair
            lse, delta = stats[0, u : u + 1, :], stats[1, u : u + 1, :]
            for s in range(b + 1, span):
                j = z.group + b - s
                block = slice(j * tok, (j + 1) * tok)
                bias = bias_rows(z, bases, tables.index((b, s)), pair)
                prob = jnp.exp(dot(keys[block, lanes], q, NT) + bias - lse)
                dscore = prob * (dot(values[block, lanes], d, NT) - delta)
                ph[pair, block, wide] = prob.astype(BF16)
                sh[pair, block, wide] = dscore.astype(BF16)


def grad_kv_kernel(z, qm, dom, p16, s16, qh, dh, ph, sh, dk, dv):
    tok = z.tok

    def each(pair, _):
        lanes = at(pair * 128, 128)
        for j in range(z.group):
            rows = slice(j * tok, (j + 1) * tok)
            ext = slice((z.halo + j) * tok, (z.halo + j + 1) * tok)
            near = slice(j * z.wide, z.group * z.wide)
            gk = dot(s16[pair, ext, near], qm[pair, near, :], NN)
            gv = dot(p16[pair, rows, near], dom[pair, near, :], NN)
            count = min(z.halo, j + z.span - z.group)
            if count > 0:
                past = slice(0, count * z.wide)
                gk = gk + dot(sh[pair, rows, past], qh[pair, past, :], NN)
                gv = gv + dot(ph[pair, rows, past], dh[pair, past, :], NN)
            dk[rows, lanes] = gk.astype(BF16)
            dv[rows, lanes] = gv.astype(BF16)
        return 0

    lax.fori_loop(0, z.pairs, each, 0)


def seal_kernel(z, grads, *refs):
    sources, sends = refs[:grads], refs[grads:]
    for k in range(z.group):
        rows = at((z.me() ^ k) * z.tok, z.tok)
        for n, ref in enumerate(sources):
            sends[k][n * z.tok : (n + 1) * z.tok, :] = ref[rows, :]


def join_kernel(*refs):
    for n, ref in enumerate(refs[:-1]):
        refs[-1][8 * n : 8 * n + 8, :] = ref[...]


def add_kernel(*refs):
    total = refs[0][...]
    for ref in refs[1:-1]:
        total = total + ref[...]
    refs[-1][...] = total


def unpack_kernel(z, sides, *refs):
    got, sums = refs[: z.group], refs[z.group : 2 * z.group]
    *outs, gb, held, sem = refs[2 * z.group :]
    me = z.me()
    copies = []
    for k in range(z.group):
        cols = at((me ^ k) * z.cw, z.cw)
        for n, out in enumerate(outs):
            src = got[k].at[n * z.tok : (n + 1) * z.tok, :]
            copies.append(pltpu.make_async_copy(src, out.at[:, cols], sem.at[len(copies)]))
    for copy in copies:
        copy.start()
    owner = lax.broadcasted_iota(jnp.int32, held.shape, 0) // z.hg
    total = jnp.zeros(held.shape, F32)
    for k in range(z.group):
        for n in range(sides):
            wide = jnp.concatenate([sums[k][8 * n : 8 * n + z.hg, :]] * (held.shape[0] // z.hg), axis=0)
            side = lax.axis_index("head") ^ n
            total = total + jnp.where(owner == side * z.group + (me ^ k), wide, 0.0)
    held[...] = total
    last = pltpu.make_async_copy(held, gb, sem.at[len(copies)])
    last.start()
    for copy in copies + [last]:
        copy.wait()


def bind(kernel, *fixed):
    def bound(*refs):
        return kernel(*fixed, *refs)

    return bound


def body(queries, keys, values, grad_out, bias_table, bucket_ids, block_mask):
    tok, width = queries.shape
    heads, buckets = bias_table.shape
    span = block_mask.shape[1]
    group = span
    z = Sizes(tok, width, heads, span, buckets, group)
    blocks = lax.axis_size("seq")
    sides = lax.axis_size("head")
    assert blocks % group == 0 and (blocks & (blocks - 1)) == 0 and (sides & (sides - 1)) == 0

    def swap(value, by, axis="seq"):
        return lax.ppermute(value, axis, [(i, i ^ by) for i in range(lax.axis_size(axis))])

    def shifted(value, by):
        return lax.ppermute(value, "seq", [(i, i + by) for i in range(blocks) if 0 <= i + by < blocks])

    def added(*terms):
        (total,) = call(add_kernel, [(terms[0].shape, terms[0].dtype)], terms)
        return total

    hbm = pltpu.HBM
    pack_bytes = group * (z.rows + 2 * tok) * z.cw * 2
    packed = call(
        bind(pack_kernel, z),
        [((z.rows, z.cw), BF16)] * group + [((2 * tok, z.cw), BF16)] * group + [((heads, buckets), F32)],
        (queries, keys, values, grad_out, bias_table, bucket_ids, block_mask),
        spaces=[hbm] * 7,
        scratch=[
            pltpu.VMEM((span, z.wide), jnp.int32),
            pltpu.SMEM((1, span), jnp.int32),
            pltpu.SemaphoreType.DMA((4 * group + 3,)),
        ],
        limit=VMEM_BYTES - pack_bytes - (520 << 10),
    )
    kv, qd, table = packed[:group], packed[group : 2 * group], packed[2 * group]
    kv_got = [kv[0]] + [swap(kv[k], k) for k in range(1, group)]
    qd_got = [qd[0]] + [swap(qd[k], k) for k in range(1, group)]
    (kv_out,) = call(bind(kv_halo_kernel, z), [((z.halo * 2 * tok, z.cw), BF16)], kv_got)
    kv_halo = shifted(kv_out, group)
    (qd_out,) = call(bind(qd_halo_kernel, z), [((z.halo * z.rows, z.cw), BF16)], (*qd_got, *kv_got))
    qd_halo = shifted(qd_out, -group)

    def tile_outs(count):
        tile = ((count * z.pairs, tok, z.wide), F32)
        row = ((count * z.pairs, z.wide), F32)
        return [tile, tile, row, row, row]

    near, far = len(z.near), len(z.far)
    unit = 2 * 128 * tok * z.wide
    own_k, own_v, bias_near, bias_far, codes = call(
        bind(bias_kernel, z),
        [((group * tok, z.cw), BF16)] * 2
        + [((near * z.pairs, tok, z.wide), F32), ((far * z.pairs, tok, z.wide), F32)]
        + [((group * CODE_ROWS, z.wide), F32)],
        (*kv_got, table),
        scratch=[pltpu.VMEM((group * span * z.hg * 8, z.wide), F32)],
    )
    qm, dom, wnear, dnear, *sums = call(
        bind(near_kernel, z),
        [((z.pairs, group * z.wide, 128), BF16)] * 2 + tile_outs(near),
        (*qd_got, own_k, own_v, bias_near),
        flops=2 * near * z.pairs * unit,
    )
    stats, fnear, ffar, wfar, dfar, *_ = call(
        bind(far_kernel, z),
        [((2, group * z.pairs, z.wide), F32), ((near * z.pairs, z.wide), F32), ((far * z.pairs, z.wide), F32)]
        + tile_outs(far),
        (kv_halo, qm, dom, bias_far, *sums),
        flops=2 * far * z.pairs * unit,
    )
    stats_halo = lax.ppermute(stats, "seq", [(i, (i - group) % blocks) for i in range(blocks)])
    p16, s16, gb = call(
        bind(own_kernel, z),
        [
            ((z.pairs, group * tok, group * z.wide), BF16),
            ((z.pairs, z.ext * tok, group * z.wide), BF16),
            ((8, buckets), F32),
        ],
        (codes, stats, fnear, ffar, wnear, dnear, wfar, dfar),
        scratch=[pltpu.VMEM((group * span * z.hg * 8, z.wide), F32)],
    )
    by = group
    while by < blocks:
        other = swap(gb, by)
        gb = added(gb, other)
        by = by * 2
    sums_of = [gb] + [swap(gb, k, "head") for k in range(1, sides)]
    (dq,) = call(
        bind(grad_q_kernel, z),
        [((group * tok, z.cw), BF16)],
        (own_k, kv_halo, s16),
        flops=(near + far) * z.pairs * unit,
    )
    lanes_of = ((z.pairs, group * tok, z.halo * z.wide), BF16)
    rows_of = ((z.pairs, z.halo * z.wide, 128), BF16)
    halo_terms = call(
        bind(tail_kernel, z),
        [rows_of, rows_of, lanes_of, lanes_of],
        (own_k, own_v, qd_halo, stats_halo, table),
        scratch=[pltpu.VMEM((far * z.hg * 8, z.wide), F32)],
        flops=2 * far * z.pairs * unit,
    )
    dk, dv = call(
        bind(grad_kv_kernel, z),
        [((group * tok, z.cw), BF16)] * 2,
        (qm, dom, p16, s16, *halo_terms),
        flops=2 * (near + far) * z.pairs * unit,
    )
    ret = call(bind(seal_kernel, z, 3), [((3 * tok, z.cw), BF16)] * group, (dq, dk, dv))
    back = [ret[0]] + [swap(ret[k], k) for k in range(1, group)]
    (joined,) = call(join_kernel, [((8 * sides, buckets), F32)], sums_of)
    spread = [joined] + [swap(joined, k) for k in range(1, group)]
    return call(
        bind(unpack_kernel, z, sides),
        [((tok, width), BF16)] * 3 + [((heads * sides, buckets), F32)],
        (*back, *spread),
        out_space=hbm,
        scratch=[pltpu.VMEM((heads * sides, buckets), F32), pltpu.SemaphoreType.DMA((3 * group + 1,))],
    )


def solution(mesh):
    placed = (
        P("seq", "head"),
        P("seq", "head"),
        P("seq", "head"),
        P("seq", "head"),
        P("head", None),
        P("seq", None, None),
        P("seq", None),
    )

    return jax.shard_map(
        body,
        mesh=mesh,
        in_specs=placed,
        out_specs=(P("seq", "head"), P("seq", "head"), P("seq", "head"), P()),
        check_vma=False,
    )
```

```python
import math

import jax
import jax.numpy as jnp
from jax import lax
from jax.experimental import pallas as pl
from jax.experimental.pallas import tpu as pltpu
from jax.sharding import PartitionSpec as P


F32 = jnp.float32
BF16 = jnp.bfloat16
NEG = -1e30
NT = (((1,), (1,)), ((), ()))
NN = (((1,), (0,)), ((), ()))
CODE_ROWS = 16
VMEM_BYTES = 67043328


def dot(a, b, dims):
    return lax.dot_general(a, b, dims, preferred_element_type=F32)


def at(start, size):
    return pl.ds(pl.multiple_of(start, size), size)


def call(kernel, outs, args, scratch=(), spaces=None, out_space=pltpu.VMEM, flops=0, limit=16 << 20):
    spaces = spaces or [pltpu.VMEM] * len(args)
    moved = sum(a.size * a.dtype.itemsize for a in args)
    args = [
        pltpu.with_memory_space_constraint(a, s) if s == pltpu.VMEM else a for a, s in zip(args, spaces, strict=True)
    ]
    return pl.pallas_call(
        kernel,
        out_shape=tuple(out_space(s, d) for s, d in outs),
        in_specs=[pl.BlockSpec(memory_space=s) for s in spaces],
        out_specs=tuple(pl.BlockSpec(memory_space=out_space) for _ in outs),
        scratch_shapes=list(scratch),
        compiler_params=pltpu.CompilerParams(vmem_limit_bytes=limit),
        cost_estimate=pl.CostEstimate(flops=flops, bytes_accessed=moved, transcendentals=0),
    )(*args)


class Sizes:
    def __init__(self, tok, width, heads, span, buckets, group):
        self.tok, self.width, self.heads, self.span, self.buckets = tok, width, heads, span, buckets
        self.group = group
        self.hd = width // heads
        self.hg = heads // group
        self.cw = self.hg * self.hd
        self.pairs = self.hg // 2
        self.scale = self.hd ** (-0.5)
        self.halo = span - 1
        self.ext = group + self.halo
        self.wide = 2 * tok
        self.rows = 2 * tok + CODE_ROWS
        self.near = [(i, s) for i in range(group) for s in range(span) if s <= i]
        self.far = [(i, s) for i in range(group) for s in range(span) if s > i]
        assert heads % group == 0 and self.hg % 2 == 0 and 2 * self.hd == 128
        assert tok == 128 and buckets == 128 and group >= self.halo and self.hg <= 8
        assert math.frexp(self.scale)[0] == 0.5

    def me(self):
        return lax.rem(lax.axis_index("seq"), self.group)


def pack_kernel(z, q, k, v, d, bias, ids, mask, *refs):
    kv, qd = refs[: z.group], refs[z.group : 2 * z.group]
    table, slots, flags, sem = refs[2 * z.group :]
    index = lax.axis_index("seq")
    me = z.me()
    copies = [
        pltpu.make_async_copy(ids.at[0], slots, sem.at[0]),
        pltpu.make_async_copy(mask, flags, sem.at[1]),
        pltpu.make_async_copy(bias, table, sem.at[2]),
    ]
    for sources, dst in (((k, v), kv), ((q, d), qd)):
        for g in range(z.group):
            cols = at((me ^ g) * z.cw, z.cw)
            for n, src in enumerate(sources):
                rows = pl.ds(n * z.tok, z.tok)
                copies.append(pltpu.make_async_copy(src.at[:, cols], dst[g].at[rows, :], sem.at[len(copies)]))
    for copy in copies:
        copy.start()
    for copy in copies[:2]:
        copy.wait()
    rows = []
    for s in range(z.span):
        valid = True if s == 0 else (flags[0, s] == 1) & (index >= s)
        rows.append(jnp.where(valid, slots[s : s + 1, :] + 1, 0))
    rows.append(jnp.zeros((CODE_ROWS - z.span, z.wide), jnp.int32))
    codes = jnp.concatenate(rows, axis=0).astype(F32).astype(BF16)
    for g in range(z.group):
        kv[g][2 * z.tok :, :] = codes
    for copy in copies[2:]:
        copy.wait()


def kv_halo_kernel(z, *refs):
    out = refs[-1]
    me = z.me()
    first = z.group - z.halo
    for k in range(z.group):
        j = me ^ k

        @pl.when(j >= first)
        def _():
            out[at((j - first) * 2 * z.tok, 2 * z.tok), :] = refs[k][0 : 2 * z.tok, :]


def qd_halo_kernel(z, *refs):
    qd, kv, out = refs[: z.group], refs[z.group : -1], refs[-1]
    me = z.me()
    for k in range(z.group):
        j = me ^ k

        @pl.when(j < z.halo)
        def _():
            top = pl.multiple_of(j * z.rows, 16)
            out[pl.ds(top, 2 * z.tok), :] = qd[k][...]
            out[pl.ds(top + 2 * z.tok, CODE_ROWS), :] = kv[k][2 * z.tok :, :]


def onehot_of(codes, z):
    slots = lax.broadcasted_iota(jnp.int32, (z.buckets, codes.shape[1]), 0) + 1
    return jnp.where(codes.astype(jnp.int32) == slots, 1.0, 0.0).astype(BF16)


def thirds(x):
    hi = x.astype(BF16)
    rest = x - hi.astype(F32)
    mid = rest.astype(BF16)
    low = (rest - mid.astype(F32)).astype(BF16)
    return jnp.concatenate([hi.astype(F32), mid.astype(F32), low.astype(F32)], axis=0).astype(BF16)


def by_offset(split, codes, z):
    got = dot(split, onehot_of(codes, z), NN)
    return got[0:8] + got[8:16] + got[16:24] + jnp.where(codes == 0.0, NEG, 0.0)


def masked_pair(x, z):
    lane = lax.broadcasted_iota(jnp.int32, x.shape, 1)
    zero = jnp.zeros_like(x)
    return jnp.concatenate([jnp.where(lane < z.hd, x, zero), jnp.where(lane < z.hd, zero, x)], axis=0)


def slanted(row, z):
    return pltpu.roll(jnp.broadcast_to(row, (8, z.wide)), z.tok + 1, 1, stride=1, stride_axis=0)


def toeplitz(base, z):
    tok = z.tok
    lane = lax.broadcasted_iota(jnp.int32, (8, tok), 1)
    low, high = base[:, 0:tok], base[:, tok:]
    tiles = [low]
    for g in range(1, tok // 8):
        tiles.append(pltpu.roll(jnp.where(lane >= tok - 8 * g, high, low), 8 * g, 1))
    return jnp.concatenate(tiles, axis=0)


def my_table(table, z):
    head = lax.broadcasted_iota(jnp.int32, (8, z.buckets), 0)
    rows = jnp.zeros((8, z.buckets), F32)
    for h in range(z.hg):
        rows = jnp.where(head == h, table[pl.ds(z.me() * z.hg + h, 1), :], rows)
    return rows


def slant_tables(z, table, code_rows, bases):
    split = thirds(my_table(table, z))
    for n, codes in enumerate(code_rows):
        rows = by_offset(split, codes, z)
        for h in range(z.hg):
            at_row = (n * z.hg + h) * 8
            bases[at_row : at_row + 8, :] = slanted(rows[h : h + 1, :], z)


def diagonals(x, z):
    tok = z.tok
    lane = lax.broadcasted_iota(jnp.int32, (8, tok), 1)
    total = x[tok - 8 :]
    high = jnp.zeros((8, tok), F32)
    for g in range(tok // 8 - 1):
        by = tok - 8 - 8 * g
        part = pltpu.roll(x[8 * g : 8 * g + 8], by, 1)
        total = total + part
        high = high + jnp.where(lane < by, part, 0.0)
    return total - high, high


def aligned(both):
    left = 7 - (lax.broadcasted_iota(jnp.int32, both.shape, 0) & 7)
    for bit in (1, 2, 4):
        both = jnp.where((left & bit) != 0, pltpu.roll(both, bit, 1), both)
    return both


def causal(z):
    row = lax.broadcasted_iota(jnp.int32, (z.tok, z.wide), 0)
    col = lax.broadcasted_iota(jnp.int32, (z.tok, z.wide), 1) % z.tok
    return row <= col


def folded(x, how):
    return how(how(x.reshape(x.shape[0] // 8, 8, x.shape[1]), 0), 0, keepdims=True)


def bias_rows(z, bases, n, pair):
    rows = [toeplitz(bases[(n * z.hg + 2 * pair + e) * 8 : (n * z.hg + 2 * pair + e + 1) * 8, :], z) for e in range(2)]
    return jnp.concatenate(rows, axis=1)


def bias_kernel(z, *refs):
    kv, table = refs[: z.group], refs[z.group]
    keys, values, near, far, codes, bases = refs[z.group + 1 :]
    tok = z.tok
    me = z.me()
    for k in range(z.group):
        j = me ^ k
        keys[at(j * tok, tok), :] = kv[k][0:tok, :]
        values[at(j * tok, tok), :] = kv[k][tok : 2 * tok, :]
        codes[at(j * CODE_ROWS, CODE_ROWS), :] = kv[k][2 * tok :, :].astype(F32)
    tables = [(i, s) for i in range(z.group) for s in range(z.span)]
    slant_tables(z, table, [codes[i * CODE_ROWS + s : i * CODE_ROWS + s + 1, :] for i, s in tables], bases)
    for tiles, out in ((z.near, near), (z.far, far)):
        for t, (i, s) in enumerate(tiles):
            for pair in range(z.pairs):
                bias = bias_rows(z, bases, i * z.span + s, pair)
                out[t * z.pairs + pair] = jnp.where(causal(z), bias, NEG) if s == 0 else bias


def forward_tile(key, value, q, d, bias, row, outs):
    weights, dprobs, tops, totals, accums = outs
    scores = dot(key, q, NT) + bias[row]
    top = folded(scores, jnp.max)
    w = jnp.exp(scores - top)
    dprob = dot(value, d, NT)
    weights[row] = w
    dprobs[row] = dprob
    tops[pl.ds(row, 1), :] = top
    totals[pl.ds(row, 1), :] = folded(w, jnp.sum)
    accums[pl.ds(row, 1), :] = folded(w * dprob, jnp.sum)


def near_kernel(z, *refs):
    qd, keys, values, bias = refs[: z.group], *refs[z.group : z.group + 3]
    qm, dom, *outs = refs[z.group + 3 :]
    tok = z.tok
    me = z.me()
    for k in range(z.group):
        j = me ^ k
        for pair in range(z.pairs):
            lanes = slice(pair * 128, (pair + 1) * 128)
            rows = at(j * z.wide, z.wide)
            qm[pair, rows, :] = masked_pair(qd[k][0:tok, lanes] * jnp.asarray(z.scale, BF16), z)
            dom[pair, rows, :] = masked_pair(qd[k][tok : 2 * tok, lanes], z)

    def each(pair, _):
        lanes = at(pair * 128, 128)
        for t, (i, s) in enumerate(z.near):
            rows = slice((i - s) * tok, (i - s + 1) * tok)
            wide = slice(i * z.wide, (i + 1) * z.wide)
            forward_tile(
                keys[rows, lanes], values[rows, lanes], qm[pair, wide, :], dom[pair, wide, :],
                bias, t * z.pairs + pair, outs,
            )
        return 0

    lax.fori_loop(0, z.pairs, each, 0)


def far_kernel(z, halo, qm, dom, bias, tops, totals, accums, stats, fnear, ffar, *outs):
    tok = z.tok

    def each(pair, _):
        lanes = at(pair * 128, 128)
        for t, (i, s) in enumerate(z.far):
            b = z.halo + i - s
            wide = slice(i * z.wide, (i + 1) * z.wide)
            forward_tile(
                halo[2 * b * tok : (2 * b + 1) * tok, lanes], halo[(2 * b + 1) * tok : (2 * b + 2) * tok, lanes],
                qm[pair, wide, :], dom[pair, wide, :], bias, t * z.pairs + pair, outs,
            )
        for i in range(z.group):
            mine = [(tops, totals, accums, fnear, t) for t, (n, _) in enumerate(z.near) if n == i]
            mine += [(outs[2], outs[3], outs[4], ffar, t) for t, (n, _) in enumerate(z.far) if n == i]
            rows = [pl.ds(t * z.pairs + pair, 1) for *_, t in mine]
            peaks = [m[0][row, :] for m, row in zip(mine, rows, strict=True)]
            top = peaks[0]
            for peak in peaks[1:]:
                top = jnp.maximum(top, peak)
            total = jnp.zeros_like(top)
            accum = jnp.zeros_like(top)
            for m, row, peak in zip(mine, rows, peaks, strict=True):
                share = jnp.exp(peak - top)
                total = total + share * m[1][row, :]
                accum = accum + share * m[2][row, :]
            lse = top + jnp.log(total)
            for m, row, peak in zip(mine, rows, peaks, strict=True):
                m[3][row, :] = jnp.exp(peak - lse)
            stats[0, pl.ds(i * z.pairs + pair, 1), :] = lse
            stats[1, pl.ds(i * z.pairs + pair, 1), :] = accum / total
        return 0

    lax.fori_loop(0, z.pairs, each, 0)


def own_kernel(z, codes, stats, fnear, ffar, wnear, dnear, wfar, dfar, p16, s16, gb, offs):
    tok, span = z.tok, z.span

    def each(pair, _):
        for i in range(z.group):
            wide = slice(i * z.wide, (i + 1) * z.wide)
            delta = stats[1, pl.ds(i * z.pairs + pair, 1), :]
            for s in range(span):
                close = s <= i
                t = (z.near if close else z.far).index((i, s)) * z.pairs + pair
                w, d, f = (wnear, dnear, fnear) if close else (wfar, dfar, ffar)
                prob = w[t] * f[pl.ds(t, 1), :]
                dscore = prob * (d[t] - delta)
                rows = slice((z.halo + i - s) * tok, (z.halo + i - s + 1) * tok)
                s16[pair, rows, wide] = dscore.astype(BF16)
                if close:
                    p16[pair, (i - s) * tok : (i - s + 1) * tok, wide] = prob.astype(BF16)
                for e in range(2):
                    low, high = diagonals(dscore[:, e * tok : (e + 1) * tok], z)
                    row = at(((i * span + s) * z.hg + 2 * pair + e) * 8, 8)
                    offs[row, 0:tok] = low
                    offs[row, tok:] = high
        return 0

    lax.fori_loop(0, z.pairs, each, 0)
    head = lax.broadcasted_iota(jnp.int32, (8, z.wide), 0)
    total = jnp.zeros((8, z.buckets), F32)
    for n in range(z.group * span):
        both = aligned(offs[n * z.hg * 8 : (n + 1) * z.hg * 8, :])
        sums = jnp.zeros((8, z.wide), F32)
        for h in range(z.hg):
            sums = sums + jnp.where(head == h, both[8 * h : 8 * h + 8].sum(axis=0, keepdims=True), 0.0)
        row = n // span * CODE_ROWS + n % span
        got = dot(thirds(sums), onehot_of(codes[row : row + 1, :], z), NT)
        total = total + (got[0:8] + got[8:16] + got[16:24])
    gb[...] = total


def grad_q_kernel(z, keys, halo, s16, dq):
    tok, span = z.tok, z.span

    def each(pair, _):
        lanes = at(pair * 128, 128)
        blocks = [halo[2 * b * tok : (2 * b + 1) * tok, lanes] for b in range(z.halo)]
        blocks += [keys[j * tok : (j + 1) * tok, lanes] for j in range(z.group)]
        turned = jnp.concatenate([block.T for block in blocks], axis=1)
        for i in range(z.group):
            window = slice(i * tok, (i + span) * tok)
            cross = dot(turned[:, window], s16[pair, window, i * z.wide : (i + 1) * z.wide], NN)
            both = jnp.concatenate([cross[0 : z.hd, 0:tok], cross[z.hd :, tok:]], axis=0)
            dq[i * tok : (i + 1) * tok, lanes] = (z.scale * both.T).astype(BF16)
        return 0

    lax.fori_loop(0, z.pairs, each, 0)


def tail_kernel(z, keys, values, halo, stats, table, qh, dh, ph, sh, bases):
    tok, span = z.tok, z.span
    tables = [(b, s) for b in range(z.halo) for s in range(b + 1, span)]
    rows = []
    for b in range(z.halo):
        codes = halo[b * z.rows + 2 * tok : (b + 1) * z.rows, :].astype(F32)
        rows += [codes[s : s + 1, :] for s in range(b + 1, span)]
    slant_tables(z, table, rows, bases)
    for pair in range(z.pairs):
        lanes = slice(pair * 128, (pair + 1) * 128)
        for b in range(z.halo):
            top = b * z.rows
            wide = slice(b * z.wide, (b + 1) * z.wide)
            q = masked_pair(halo[top : top + tok, lanes] * jnp.asarray(z.scale, BF16), z)
            d = masked_pair(halo[top + tok : top + 2 * tok, lanes], z)
            qh[pair, wide, :] = q
            dh[pair, wide, :] = d
            u = b * z.pairs + pair
            lse, delta = stats[0, u : u + 1, :], stats[1, u : u + 1, :]
            for s in range(b + 1, span):
                j = z.group + b - s
                block = slice(j * tok, (j + 1) * tok)
                bias = bias_rows(z, bases, tables.index((b, s)), pair)
                prob = jnp.exp(dot(keys[block, lanes], q, NT) + bias - lse)
                dscore = prob * (dot(values[block, lanes], d, NT) - delta)
                ph[pair, block, wide] = prob.astype(BF16)
                sh[pair, block, wide] = dscore.astype(BF16)


def grad_kv_kernel(z, qm, dom, p16, s16, qh, dh, ph, sh, dk, dv):
    tok = z.tok

    def each(pair, _):
        lanes = at(pair * 128, 128)
        for j in range(z.group):
            rows = slice(j * tok, (j + 1) * tok)
            ext = slice((z.halo + j) * tok, (z.halo + j + 1) * tok)
            near = slice(j * z.wide, z.group * z.wide)
            gk = dot(s16[pair, ext, near], qm[pair, near, :], NN)
            gv = dot(p16[pair, rows, near], dom[pair, near, :], NN)
            count = min(z.halo, j + z.span - z.group)
            if count > 0:
                past = slice(0, count * z.wide)
                gk = gk + dot(sh[pair, rows, past], qh[pair, past, :], NN)
                gv = gv + dot(ph[pair, rows, past], dh[pair, past, :], NN)
            dk[rows, lanes] = gk.astype(BF16)
            dv[rows, lanes] = gv.astype(BF16)
        return 0

    lax.fori_loop(0, z.pairs, each, 0)


def seal_kernel(z, grads, *refs):
    sources, sends = refs[:grads], refs[grads:]
    for k in range(z.group):
        rows = at((z.me() ^ k) * z.tok, z.tok)
        for n, ref in enumerate(sources):
            sends[k][n * z.tok : (n + 1) * z.tok, :] = ref[rows, :]


def join_kernel(*refs):
    rows = refs[0].shape[0]
    for n, ref in enumerate(refs[:-1]):
        refs[-1][rows * n : rows * (n + 1), :] = ref[...]


def add_kernel(*refs):
    total = refs[0][...]
    for ref in refs[1:-1]:
        total = total + ref[...]
    refs[-1][...] = total


def unpack_kernel(z, *refs):
    got, outs, sem = refs[: z.group], refs[z.group : -1], refs[-1]
    me = z.me()
    copies = []
    for k in range(z.group):
        cols = at((me ^ k) * z.cw, z.cw)
        for n, out in enumerate(outs):
            src = got[k].at[n * z.tok : (n + 1) * z.tok, :]
            copies.append(pltpu.make_async_copy(src, out.at[:, cols], sem.at[len(copies)]))
    for copy in copies:
        copy.start()
    for copy in copies:
        copy.wait()


def spread_kernel(z, sides, mine, other, gb, held, sem):
    me = z.me()
    owner = lax.broadcasted_iota(jnp.int32, held.shape, 0) // z.hg
    total = jnp.zeros(held.shape, F32)
    half = z.group * sides // 2
    for m in range(z.group * sides):
        ref, row = (mine, 8 * m) if m < half else (other, 8 * (m - half))
        wide = jnp.concatenate([ref[row : row + z.hg, :]] * (held.shape[0] // z.hg), axis=0)
        side = lax.axis_index("head") ^ (m % sides)
        total = total + jnp.where(owner == side * z.group + (me ^ (m // sides)), wide, 0.0)
    held[...] = total
    copy = pltpu.make_async_copy(held, gb, sem.at[0])
    copy.start()
    copy.wait()


def bind(kernel, *fixed):
    def bound(*refs):
        return kernel(*fixed, *refs)

    return bound


def body(queries, keys, values, grad_out, bias_table, bucket_ids, block_mask):
    tok, width = queries.shape
    heads, buckets = bias_table.shape
    span = block_mask.shape[1]
    group = span
    z = Sizes(tok, width, heads, span, buckets, group)
    blocks = lax.axis_size("seq")
    sides = lax.axis_size("head")
    assert blocks % group == 0 and (blocks & (blocks - 1)) == 0 and (sides & (sides - 1)) == 0

    def swap(value, by, axis="seq"):
        return lax.ppermute(value, axis, [(i, i ^ by) for i in range(lax.axis_size(axis))])

    def shifted(value, by):
        return lax.ppermute(value, "seq", [(i, i + by) for i in range(blocks) if 0 <= i + by < blocks])

    def swapped(parts):
        got = {k: swap(parts[k], k) for k in (group - 1, *range(1, group - 1))}
        return [parts[0]] + [got[k] for k in range(1, group)]

    def added(*terms):
        (total,) = call(add_kernel, [(terms[0].shape, terms[0].dtype)], terms)
        return total

    hbm = pltpu.HBM
    pack_bytes = group * (z.rows + 2 * tok) * z.cw * 2
    packed = call(
        bind(pack_kernel, z),
        [((z.rows, z.cw), BF16)] * group + [((2 * tok, z.cw), BF16)] * group + [((heads, buckets), F32)],
        (queries, keys, values, grad_out, bias_table, bucket_ids, block_mask),
        spaces=[hbm] * 7,
        scratch=[
            pltpu.VMEM((span, z.wide), jnp.int32),
            pltpu.SMEM((1, span), jnp.int32),
            pltpu.SemaphoreType.DMA((4 * group + 3,)),
        ],
        limit=VMEM_BYTES - pack_bytes - (520 << 10),
    )
    kv, qd, table = packed[:group], packed[group : 2 * group], packed[2 * group]
    kv_got = swapped(kv)
    qd_got = swapped(qd)
    (kv_out,) = call(bind(kv_halo_kernel, z), [((z.halo * 2 * tok, z.cw), BF16)], kv_got)
    kv_halo = shifted(kv_out, group)
    (qd_out,) = call(bind(qd_halo_kernel, z), [((z.halo * z.rows, z.cw), BF16)], (*qd_got, *kv_got))
    qd_halo = shifted(qd_out, -group)

    def tile_outs(count):
        tile = ((count * z.pairs, tok, z.wide), F32)
        row = ((count * z.pairs, z.wide), F32)
        return [tile, tile, row, row, row]

    near, far = len(z.near), len(z.far)
    unit = 2 * 128 * tok * z.wide
    own_k, own_v, bias_near, bias_far, codes = call(
        bind(bias_kernel, z),
        [((group * tok, z.cw), BF16)] * 2
        + [((near * z.pairs, tok, z.wide), F32), ((far * z.pairs, tok, z.wide), F32)]
        + [((group * CODE_ROWS, z.wide), F32)],
        (*kv_got, table),
        scratch=[pltpu.VMEM((group * span * z.hg * 8, z.wide), F32)],
    )
    qm, dom, wnear, dnear, *sums = call(
        bind(near_kernel, z),
        [((z.pairs, group * z.wide, 128), BF16)] * 2 + tile_outs(near),
        (*qd_got, own_k, own_v, bias_near),
        flops=2 * near * z.pairs * unit,
    )
    stats, fnear, ffar, wfar, dfar, *_ = call(
        bind(far_kernel, z),
        [((2, group * z.pairs, z.wide), F32), ((near * z.pairs, z.wide), F32), ((far * z.pairs, z.wide), F32)]
        + tile_outs(far),
        (kv_halo, qm, dom, bias_far, *sums),
        flops=2 * far * z.pairs * unit,
    )
    stats_halo = lax.ppermute(stats, "seq", [(i, (i - group) % blocks) for i in range(blocks)])
    p16, s16, gb = call(
        bind(own_kernel, z),
        [
            ((z.pairs, group * tok, group * z.wide), BF16),
            ((z.pairs, z.ext * tok, group * z.wide), BF16),
            ((8, buckets), F32),
        ],
        (codes, stats, fnear, ffar, wnear, dnear, wfar, dfar),
        scratch=[pltpu.VMEM((group * span * z.hg * 8, z.wide), F32)],
    )
    by = group
    while by < blocks:
        other = swap(gb, by)
        gb = added(gb, other)
        by = by * 2
    sums_of = [gb] + [swap(gb, k, "head") for k in range(1, sides)]
    (dq,) = call(
        bind(grad_q_kernel, z),
        [((group * tok, z.cw), BF16)],
        (own_k, kv_halo, s16),
        flops=(near + far) * z.pairs * unit,
    )
    lanes_of = ((z.pairs, group * tok, z.halo * z.wide), BF16)
    rows_of = ((z.pairs, z.halo * z.wide, 128), BF16)
    halo_terms = call(
        bind(tail_kernel, z),
        [rows_of, rows_of, lanes_of, lanes_of],
        (own_k, own_v, qd_halo, stats_halo, table),
        scratch=[pltpu.VMEM((far * z.hg * 8, z.wide), F32)],
        flops=2 * far * z.pairs * unit,
    )
    dk, dv = call(
        bind(grad_kv_kernel, z),
        [((group * tok, z.cw), BF16)] * 2,
        (qm, dom, p16, s16, *halo_terms),
        flops=2 * (near + far) * z.pairs * unit,
    )
    ret = call(bind(seal_kernel, z, 3), [((3 * tok, z.cw), BF16)] * group, (dq, dk, dv))
    back = swapped(ret)

    def joined(*parts):
        rows = sum(p.shape[0] for p in parts)
        (whole,) = call(join_kernel, [((rows, buckets), F32)], parts)
        return whole

    mine, by = joined(*sums_of), 1
    while by * 2 < group:
        mine, by = joined(mine, swap(mine, by)), by * 2
    other = swap(mine, by)
    grads = call(
        bind(unpack_kernel, z),
        [((tok, width), BF16)] * 3,
        back,
        out_space=hbm,
        scratch=[pltpu.SemaphoreType.DMA((3 * group,))],
    )
    (grad_bias,) = call(
        bind(spread_kernel, z, sides),
        [((heads * sides, buckets), F32)],
        (mine, other),
        out_space=hbm,
        scratch=[pltpu.VMEM((heads * sides, buckets), F32), pltpu.SemaphoreType.DMA((1,))],
    )
    return (*grads, grad_bias)


def solution(mesh):
    placed = (
        P("seq", "head"),
        P("seq", "head"),
        P("seq", "head"),
        P("seq", "head"),
        P("head", None),
        P("seq", None, None),
        P("seq", None),
    )

    return jax.shard_map(
        body,
        mesh=mesh,
        in_specs=placed,
        out_specs=(P("seq", "head"), P("seq", "head"), P("seq", "head"), P()),
        check_vma=False,
    )
```

```python
import math

import jax
import jax.numpy as jnp
from jax import lax
from jax.experimental import pallas as pl
from jax.experimental.pallas import tpu as pltpu
from jax.sharding import PartitionSpec as P


F32 = jnp.float32
BF16 = jnp.bfloat16
NEG = -1e30
NT = (((1,), (1,)), ((), ()))
NN = (((1,), (0,)), ((), ()))
CODE_ROWS = 16
VMEM_BYTES = 67043328


def dot(a, b, dims):
    return lax.dot_general(a, b, dims, preferred_element_type=F32)


def at(start, size):
    return pl.ds(pl.multiple_of(start, size), size)


def call(kernel, outs, args, scratch=(), spaces=None, out_space=pltpu.VMEM, flops=0, limit=16 << 20):
    spaces = spaces or [pltpu.VMEM] * len(args)
    moved = sum(a.size * a.dtype.itemsize for a in args)
    args = [
        pltpu.with_memory_space_constraint(a, s) if s == pltpu.VMEM else a for a, s in zip(args, spaces, strict=True)
    ]
    return pl.pallas_call(
        kernel,
        out_shape=tuple(out_space(s, d) for s, d in outs),
        in_specs=[pl.BlockSpec(memory_space=s) for s in spaces],
        out_specs=tuple(pl.BlockSpec(memory_space=out_space) for _ in outs),
        scratch_shapes=list(scratch),
        compiler_params=pltpu.CompilerParams(vmem_limit_bytes=limit),
        cost_estimate=pl.CostEstimate(flops=flops, bytes_accessed=moved, transcendentals=0),
    )(*args)


class Sizes:
    def __init__(self, tok, width, heads, span, buckets, group):
        self.tok, self.width, self.heads, self.span, self.buckets = tok, width, heads, span, buckets
        self.group = group
        self.hd = width // heads
        self.hg = heads // group
        self.cw = self.hg * self.hd
        self.pairs = self.hg // 2
        self.scale = self.hd ** (-0.5)
        self.halo = span - 1
        self.ext = group + self.halo
        self.wide = 2 * tok
        self.rows = 2 * tok + CODE_ROWS
        self.near = [(i, s) for i in range(group) for s in range(span) if s <= i]
        self.far = [(i, s) for i in range(group) for s in range(span) if s > i]
        assert heads % group == 0 and self.hg % 2 == 0 and 2 * self.hd == 128
        assert tok == 128 and buckets == 128 and group >= self.halo and self.hg <= 8
        assert math.frexp(self.scale)[0] == 0.5

    def me(self):
        return lax.rem(lax.axis_index("seq"), self.group)


def chunk_copies(z, sources, dst, sem, first):
    copies = []
    for g in range(z.group):
        cols = at((z.me() ^ g) * z.cw, z.cw)
        for n, src in enumerate(sources):
            rows = pl.ds(n * z.tok, z.tok)
            copies.append(pltpu.make_async_copy(src.at[:, cols], dst[g].at[rows, :], sem.at[first + len(copies)]))
    return copies


def pack_kv_kernel(z, k, v, bias, ids, mask, *refs):
    kv = refs[: z.group]
    table, slots, flags, sem = refs[z.group :]
    index = lax.axis_index("seq")
    copies = [
        pltpu.make_async_copy(ids.at[0], slots, sem.at[0]),
        pltpu.make_async_copy(mask, flags, sem.at[1]),
        pltpu.make_async_copy(bias, table, sem.at[2]),
    ]
    copies += chunk_copies(z, (k, v), kv, sem, len(copies))
    for copy in copies:
        copy.start()
    for copy in copies[:2]:
        copy.wait()
    rows = []
    for s in range(z.span):
        valid = True if s == 0 else (flags[0, s] == 1) & (index >= s)
        rows.append(jnp.where(valid, slots[s : s + 1, :] + 1, 0))
    rows.append(jnp.zeros((CODE_ROWS - z.span, z.wide), jnp.int32))
    codes = jnp.concatenate(rows, axis=0).astype(F32).astype(BF16)
    for g in range(z.group):
        kv[g][2 * z.tok :, :] = codes
    for copy in copies[2:]:
        copy.wait()


def pack_qd_kernel(z, q, d, *refs):
    copies = chunk_copies(z, (q, d), refs[: z.group], refs[z.group], 0)
    for copy in copies:
        copy.start()
    for copy in copies:
        copy.wait()


def kv_halo_kernel(z, *refs):
    out = refs[-1]
    me = z.me()
    first = z.group - z.halo
    for k in range(z.group):
        j = me ^ k

        @pl.when(j >= first)
        def _():
            out[at((j - first) * 2 * z.tok, 2 * z.tok), :] = refs[k][0 : 2 * z.tok, :]


def qd_halo_kernel(z, *refs):
    qd, kv, out = refs[: z.group], refs[z.group : -1], refs[-1]
    me = z.me()
    for k in range(z.group):
        j = me ^ k

        @pl.when(j < z.halo)
        def _():
            top = pl.multiple_of(j * z.rows, 16)
            out[pl.ds(top, 2 * z.tok), :] = qd[k][...]
            out[pl.ds(top + 2 * z.tok, CODE_ROWS), :] = kv[k][2 * z.tok :, :]


def onehot_of(codes, z):
    slots = lax.broadcasted_iota(jnp.int32, (z.buckets, codes.shape[1]), 0) + 1
    return jnp.where(codes.astype(jnp.int32) == slots, 1.0, 0.0).astype(BF16)


def thirds(x):
    hi = x.astype(BF16)
    rest = x - hi.astype(F32)
    mid = rest.astype(BF16)
    low = (rest - mid.astype(F32)).astype(BF16)
    return jnp.concatenate([hi.astype(F32), mid.astype(F32), low.astype(F32)], axis=0).astype(BF16)


def by_offset(split, codes, z):
    got = dot(split, onehot_of(codes, z), NN)
    return got[0:8] + got[8:16] + got[16:24] + jnp.where(codes == 0.0, NEG, 0.0)


def masked_pair(x, z):
    lane = lax.broadcasted_iota(jnp.int32, x.shape, 1)
    zero = jnp.zeros_like(x)
    return jnp.concatenate([jnp.where(lane < z.hd, x, zero), jnp.where(lane < z.hd, zero, x)], axis=0)


def slanted(row, z):
    return pltpu.roll(jnp.broadcast_to(row, (8, z.wide)), z.tok + 1, 1, stride=1, stride_axis=0)


def toeplitz(base, z):
    tok = z.tok
    lane = lax.broadcasted_iota(jnp.int32, (8, tok), 1)
    low, high = base[:, 0:tok], base[:, tok:]
    tiles = [low]
    for g in range(1, tok // 8):
        tiles.append(pltpu.roll(jnp.where(lane >= tok - 8 * g, high, low), 8 * g, 1))
    return jnp.concatenate(tiles, axis=0)


def my_table(table, z):
    head = lax.broadcasted_iota(jnp.int32, (8, z.buckets), 0)
    rows = jnp.zeros((8, z.buckets), F32)
    for h in range(z.hg):
        rows = jnp.where(head == h, table[pl.ds(z.me() * z.hg + h, 1), :], rows)
    return rows


def slant_tables(z, table, code_rows, bases):
    split = thirds(my_table(table, z))
    for n, codes in enumerate(code_rows):
        rows = by_offset(split, codes, z)
        for h in range(z.hg):
            at_row = (n * z.hg + h) * 8
            bases[at_row : at_row + 8, :] = slanted(rows[h : h + 1, :], z)


def diagonals(x, z):
    tok = z.tok
    lane = lax.broadcasted_iota(jnp.int32, (8, tok), 1)
    total = x[tok - 8 :]
    high = jnp.zeros((8, tok), F32)
    for g in range(tok // 8 - 1):
        by = tok - 8 - 8 * g
        part = pltpu.roll(x[8 * g : 8 * g + 8], by, 1)
        total = total + part
        high = high + jnp.where(lane < by, part, 0.0)
    return total - high, high


def aligned(both):
    left = 7 - (lax.broadcasted_iota(jnp.int32, both.shape, 0) & 7)
    for bit in (1, 2, 4):
        both = jnp.where((left & bit) != 0, pltpu.roll(both, bit, 1), both)
    return both


def causal(z):
    row = lax.broadcasted_iota(jnp.int32, (z.tok, z.wide), 0)
    col = lax.broadcasted_iota(jnp.int32, (z.tok, z.wide), 1) % z.tok
    return row <= col


def folded(x, how):
    return how(how(x.reshape(x.shape[0] // 8, 8, x.shape[1]), 0), 0, keepdims=True)


def bias_rows(z, bases, n, pair):
    rows = [toeplitz(bases[(n * z.hg + 2 * pair + e) * 8 : (n * z.hg + 2 * pair + e + 1) * 8, :], z) for e in range(2)]
    return jnp.concatenate(rows, axis=1)


def bias_kernel(z, *refs):
    kv, table = refs[: z.group], refs[z.group]
    keys, values, near, far, codes, bases = refs[z.group + 1 :]
    tok = z.tok
    me = z.me()
    for k in range(z.group):
        j = me ^ k
        keys[at(j * tok, tok), :] = kv[k][0:tok, :]
        values[at(j * tok, tok), :] = kv[k][tok : 2 * tok, :]
        codes[at(j * CODE_ROWS, CODE_ROWS), :] = kv[k][2 * tok :, :].astype(F32)
    tables = [(i, s) for i in range(z.group) for s in range(z.span)]
    slant_tables(z, table, [codes[i * CODE_ROWS + s : i * CODE_ROWS + s + 1, :] for i, s in tables], bases)
    for tiles, out in ((z.near, near), (z.far, far)):
        for t, (i, s) in enumerate(tiles):
            for pair in range(z.pairs):
                bias = bias_rows(z, bases, i * z.span + s, pair)
                out[t * z.pairs + pair] = jnp.where(causal(z), bias, NEG) if s == 0 else bias


def forward_tile(key, value, q, d, bias, row, outs):
    weights, dprobs, tops, totals, accums = outs
    scores = dot(key, q, NT) + bias[row]
    top = folded(scores, jnp.max)
    w = jnp.exp(scores - top)
    dprob = dot(value, d, NT)
    weights[row] = w
    dprobs[row] = dprob
    tops[pl.ds(row, 1), :] = top
    totals[pl.ds(row, 1), :] = folded(w, jnp.sum)
    accums[pl.ds(row, 1), :] = folded(w * dprob, jnp.sum)


def near_kernel(z, *refs):
    qd, keys, values, bias = refs[: z.group], *refs[z.group : z.group + 3]
    qm, dom, *outs = refs[z.group + 3 :]
    tok = z.tok
    me = z.me()
    for k in range(z.group):
        j = me ^ k
        for pair in range(z.pairs):
            lanes = slice(pair * 128, (pair + 1) * 128)
            rows = at(j * z.wide, z.wide)
            qm[pair, rows, :] = masked_pair(qd[k][0:tok, lanes] * jnp.asarray(z.scale, BF16), z)
            dom[pair, rows, :] = masked_pair(qd[k][tok : 2 * tok, lanes], z)

    def each(pair, _):
        lanes = at(pair * 128, 128)
        for t, (i, s) in enumerate(z.near):
            rows = slice((i - s) * tok, (i - s + 1) * tok)
            wide = slice(i * z.wide, (i + 1) * z.wide)
            forward_tile(
                keys[rows, lanes], values[rows, lanes], qm[pair, wide, :], dom[pair, wide, :],
                bias, t * z.pairs + pair, outs,
            )
        return 0

    lax.fori_loop(0, z.pairs, each, 0)


def far_kernel(z, halo, qm, dom, bias, tops, totals, accums, stats, fnear, ffar, *outs):
    tok = z.tok

    def each(pair, _):
        lanes = at(pair * 128, 128)
        for t, (i, s) in enumerate(z.far):
            b = z.halo + i - s
            wide = slice(i * z.wide, (i + 1) * z.wide)
            forward_tile(
                halo[2 * b * tok : (2 * b + 1) * tok, lanes], halo[(2 * b + 1) * tok : (2 * b + 2) * tok, lanes],
                qm[pair, wide, :], dom[pair, wide, :], bias, t * z.pairs + pair, outs,
            )
        for i in range(z.group):
            mine = [(tops, totals, accums, fnear, t) for t, (n, _) in enumerate(z.near) if n == i]
            mine += [(outs[2], outs[3], outs[4], ffar, t) for t, (n, _) in enumerate(z.far) if n == i]
            rows = [pl.ds(t * z.pairs + pair, 1) for *_, t in mine]
            peaks = [m[0][row, :] for m, row in zip(mine, rows, strict=True)]
            top = peaks[0]
            for peak in peaks[1:]:
                top = jnp.maximum(top, peak)
            total = jnp.zeros_like(top)
            accum = jnp.zeros_like(top)
            for m, row, peak in zip(mine, rows, peaks, strict=True):
                share = jnp.exp(peak - top)
                total = total + share * m[1][row, :]
                accum = accum + share * m[2][row, :]
            lse = top + jnp.log(total)
            for m, row, peak in zip(mine, rows, peaks, strict=True):
                m[3][row, :] = jnp.exp(peak - lse)
            stats[0, pl.ds(i * z.pairs + pair, 1), :] = lse
            stats[1, pl.ds(i * z.pairs + pair, 1), :] = accum / total
        return 0

    lax.fori_loop(0, z.pairs, each, 0)


def own_kernel(z, codes, stats, fnear, ffar, wnear, dnear, wfar, dfar, p16, s16, gb, offs):
    tok, span = z.tok, z.span

    def each(pair, _):
        for i in range(z.group):
            wide = slice(i * z.wide, (i + 1) * z.wide)
            delta = stats[1, pl.ds(i * z.pairs + pair, 1), :]
            for s in range(span):
                close = s <= i
                t = (z.near if close else z.far).index((i, s)) * z.pairs + pair
                w, d, f = (wnear, dnear, fnear) if close else (wfar, dfar, ffar)
                prob = w[t] * f[pl.ds(t, 1), :]
                dscore = prob * (d[t] - delta)
                rows = slice((z.halo + i - s) * tok, (z.halo + i - s + 1) * tok)
                s16[pair, rows, wide] = dscore.astype(BF16)
                if close:
                    p16[pair, (i - s) * tok : (i - s + 1) * tok, wide] = prob.astype(BF16)
                for e in range(2):
                    low, high = diagonals(dscore[:, e * tok : (e + 1) * tok], z)
                    row = at(((i * span + s) * z.hg + 2 * pair + e) * 8, 8)
                    offs[row, 0:tok] = low
                    offs[row, tok:] = high
        return 0

    lax.fori_loop(0, z.pairs, each, 0)
    head = lax.broadcasted_iota(jnp.int32, (8, z.wide), 0)
    total = jnp.zeros((8, z.buckets), F32)
    for n in range(z.group * span):
        both = aligned(offs[n * z.hg * 8 : (n + 1) * z.hg * 8, :])
        sums = jnp.zeros((8, z.wide), F32)
        for h in range(z.hg):
            sums = sums + jnp.where(head == h, both[8 * h : 8 * h + 8].sum(axis=0, keepdims=True), 0.0)
        row = n // span * CODE_ROWS + n % span
        got = dot(thirds(sums), onehot_of(codes[row : row + 1, :], z), NT)
        total = total + (got[0:8] + got[8:16] + got[16:24])
    gb[...] = total


def grad_q_kernel(z, keys, halo, s16, dq):
    tok, span = z.tok, z.span

    def each(pair, _):
        lanes = at(pair * 128, 128)
        blocks = [halo[2 * b * tok : (2 * b + 1) * tok, lanes] for b in range(z.halo)]
        blocks += [keys[j * tok : (j + 1) * tok, lanes] for j in range(z.group)]
        turned = jnp.concatenate([block.T for block in blocks], axis=1)
        for i in range(z.group):
            window = slice(i * tok, (i + span) * tok)
            cross = dot(turned[:, window], s16[pair, window, i * z.wide : (i + 1) * z.wide], NN)
            both = jnp.concatenate([cross[0 : z.hd, 0:tok], cross[z.hd :, tok:]], axis=0)
            dq[i * tok : (i + 1) * tok, lanes] = (z.scale * both.T).astype(BF16)
        return 0

    lax.fori_loop(0, z.pairs, each, 0)


def tail_kernel(z, keys, values, halo, stats, table, qh, dh, ph, sh, bases):
    tok, span = z.tok, z.span
    tables = [(b, s) for b in range(z.halo) for s in range(b + 1, span)]
    rows = []
    for b in range(z.halo):
        codes = halo[b * z.rows + 2 * tok : (b + 1) * z.rows, :].astype(F32)
        rows += [codes[s : s + 1, :] for s in range(b + 1, span)]
    slant_tables(z, table, rows, bases)
    for pair in range(z.pairs):
        lanes = slice(pair * 128, (pair + 1) * 128)
        for b in range(z.halo):
            top = b * z.rows
            wide = slice(b * z.wide, (b + 1) * z.wide)
            q = masked_pair(halo[top : top + tok, lanes] * jnp.asarray(z.scale, BF16), z)
            d = masked_pair(halo[top + tok : top + 2 * tok, lanes], z)
            qh[pair, wide, :] = q
            dh[pair, wide, :] = d
            u = b * z.pairs + pair
            lse, delta = stats[0, u : u + 1, :], stats[1, u : u + 1, :]
            for s in range(b + 1, span):
                j = z.group + b - s
                block = slice(j * tok, (j + 1) * tok)
                bias = bias_rows(z, bases, tables.index((b, s)), pair)
                prob = jnp.exp(dot(keys[block, lanes], q, NT) + bias - lse)
                dscore = prob * (dot(values[block, lanes], d, NT) - delta)
                ph[pair, block, wide] = prob.astype(BF16)
                sh[pair, block, wide] = dscore.astype(BF16)


def grad_kv_kernel(z, qm, dom, p16, s16, qh, dh, ph, sh, dk, dv):
    tok = z.tok

    def each(pair, _):
        lanes = at(pair * 128, 128)
        for j in range(z.group):
            rows = slice(j * tok, (j + 1) * tok)
            ext = slice((z.halo + j) * tok, (z.halo + j + 1) * tok)
            near = slice(j * z.wide, z.group * z.wide)
            gk = dot(s16[pair, ext, near], qm[pair, near, :], NN)
            gv = dot(p16[pair, rows, near], dom[pair, near, :], NN)
            count = min(z.halo, j + z.span - z.group)
            if count > 0:
                past = slice(0, count * z.wide)
                gk = gk + dot(sh[pair, rows, past], qh[pair, past, :], NN)
                gv = gv + dot(ph[pair, rows, past], dh[pair, past, :], NN)
            dk[rows, lanes] = gk.astype(BF16)
            dv[rows, lanes] = gv.astype(BF16)
        return 0

    lax.fori_loop(0, z.pairs, each, 0)


def seal_kernel(z, grads, *refs):
    sources, sends = refs[:grads], refs[grads:]
    for k in range(z.group):
        rows = at((z.me() ^ k) * z.tok, z.tok)
        for n, ref in enumerate(sources):
            sends[k][n * z.tok : (n + 1) * z.tok, :] = ref[rows, :]


def join_kernel(*refs):
    for n, ref in enumerate(refs[:-1]):
        refs[-1][8 * n : 8 * n + 8, :] = ref[...]


def add_kernel(*refs):
    total = refs[0][...]
    for ref in refs[1:-1]:
        total = total + ref[...]
    refs[-1][...] = total


def unpack_kernel(z, *refs):
    got, outs, sem = refs[: z.group], refs[z.group : -1], refs[-1]
    me = z.me()
    copies = []
    for k in range(z.group):
        cols = at((me ^ k) * z.cw, z.cw)
        for n, out in enumerate(outs):
            src = got[k].at[n * z.tok : (n + 1) * z.tok, :]
            copies.append(pltpu.make_async_copy(src, out.at[:, cols], sem.at[len(copies)]))
    for copy in copies:
        copy.start()
    for copy in copies:
        copy.wait()


def spread_kernel(z, sides, *refs):
    sums, (gb, held, sem) = refs[: z.group], refs[z.group :]
    me = z.me()
    owner = lax.broadcasted_iota(jnp.int32, held.shape, 0) // z.hg
    total = jnp.zeros(held.shape, F32)
    for k in range(z.group):
        for n in range(sides):
            wide = jnp.concatenate([sums[k][8 * n : 8 * n + z.hg, :]] * (held.shape[0] // z.hg), axis=0)
            side = lax.axis_index("head") ^ n
            total = total + jnp.where(owner == side * z.group + (me ^ k), wide, 0.0)
    held[...] = total
    copy = pltpu.make_async_copy(held, gb, sem.at[0])
    copy.start()
    copy.wait()


def bind(kernel, *fixed):
    def bound(*refs):
        return kernel(*fixed, *refs)

    return bound


def body(queries, keys, values, grad_out, bias_table, bucket_ids, block_mask):
    tok, width = queries.shape
    heads, buckets = bias_table.shape
    span = block_mask.shape[1]
    group = span
    z = Sizes(tok, width, heads, span, buckets, group)
    blocks = lax.axis_size("seq")
    sides = lax.axis_size("head")
    assert blocks % group == 0 and (blocks & (blocks - 1)) == 0 and (sides & (sides - 1)) == 0

    def swap(value, by, axis="seq"):
        return lax.ppermute(value, axis, [(i, i ^ by) for i in range(lax.axis_size(axis))])

    def shifted(value, by):
        return lax.ppermute(value, "seq", [(i, i + by) for i in range(blocks) if 0 <= i + by < blocks])

    def swapped(parts):
        return [parts[0]] + [swap(parts[k], k) for k in range(1, group)]

    def added(*terms):
        (total,) = call(add_kernel, [(terms[0].shape, terms[0].dtype)], terms)
        return total

    hbm = pltpu.HBM
    pack_bytes = group * (z.rows + 2 * tok) * z.cw * 2
    room = VMEM_BYTES - pack_bytes - (520 << 10)
    *kv, table = call(
        bind(pack_kv_kernel, z),
        [((z.rows, z.cw), BF16)] * group + [((heads, buckets), F32)],
        (keys, values, bias_table, bucket_ids, block_mask),
        spaces=[hbm] * 5,
        scratch=[
            pltpu.VMEM((span, z.wide), jnp.int32),
            pltpu.SMEM((1, span), jnp.int32),
            pltpu.SemaphoreType.DMA((2 * group + 3,)),
        ],
        limit=room,
    )
    qd = call(
        bind(pack_qd_kernel, z),
        [((2 * tok, z.cw), BF16)] * group,
        (queries, grad_out),
        spaces=[hbm] * 2,
        scratch=[pltpu.SemaphoreType.DMA((2 * group,))],
        limit=room - (group - 1) * z.rows * z.cw * 2,
    )
    kv_got = swapped(kv)
    qd_got = swapped(qd)
    (kv_out,) = call(bind(kv_halo_kernel, z), [((z.halo * 2 * tok, z.cw), BF16)], kv_got)
    kv_halo = shifted(kv_out, group)
    (qd_out,) = call(bind(qd_halo_kernel, z), [((z.halo * z.rows, z.cw), BF16)], (*qd_got, *kv_got))
    qd_halo = shifted(qd_out, -group)

    def tile_outs(count):
        tile = ((count * z.pairs, tok, z.wide), F32)
        row = ((count * z.pairs, z.wide), F32)
        return [tile, tile, row, row, row]

    near, far = len(z.near), len(z.far)
    unit = 2 * 128 * tok * z.wide
    own_k, own_v, bias_near, bias_far, codes = call(
        bind(bias_kernel, z),
        [((group * tok, z.cw), BF16)] * 2
        + [((near * z.pairs, tok, z.wide), F32), ((far * z.pairs, tok, z.wide), F32)]
        + [((group * CODE_ROWS, z.wide), F32)],
        (*kv_got, table),
        scratch=[pltpu.VMEM((group * span * z.hg * 8, z.wide), F32)],
    )
    qm, dom, wnear, dnear, *sums = call(
        bind(near_kernel, z),
        [((z.pairs, group * z.wide, 128), BF16)] * 2 + tile_outs(near),
        (*qd_got, own_k, own_v, bias_near),
        flops=2 * near * z.pairs * unit,
    )
    stats, fnear, ffar, wfar, dfar, *_ = call(
        bind(far_kernel, z),
        [((2, group * z.pairs, z.wide), F32), ((near * z.pairs, z.wide), F32), ((far * z.pairs, z.wide), F32)]
        + tile_outs(far),
        (kv_halo, qm, dom, bias_far, *sums),
        flops=2 * far * z.pairs * unit,
    )
    stats_halo = lax.ppermute(stats, "seq", [(i, (i - group) % blocks) for i in range(blocks)])
    p16, s16, gb = call(
        bind(own_kernel, z),
        [
            ((z.pairs, group * tok, group * z.wide), BF16),
            ((z.pairs, z.ext * tok, group * z.wide), BF16),
            ((8, buckets), F32),
        ],
        (codes, stats, fnear, ffar, wnear, dnear, wfar, dfar),
        scratch=[pltpu.VMEM((group * span * z.hg * 8, z.wide), F32)],
    )
    by = group
    while by < blocks:
        other = swap(gb, by)
        gb = added(gb, other)
        by = by * 2
    sums_of = [gb] + [swap(gb, k, "head") for k in range(1, sides)]
    (dq,) = call(
        bind(grad_q_kernel, z),
        [((group * tok, z.cw), BF16)],
        (own_k, kv_halo, s16),
        flops=(near + far) * z.pairs * unit,
    )
    lanes_of = ((z.pairs, group * tok, z.halo * z.wide), BF16)
    rows_of = ((z.pairs, z.halo * z.wide, 128), BF16)
    halo_terms = call(
        bind(tail_kernel, z),
        [rows_of, rows_of, lanes_of, lanes_of],
        (own_k, own_v, qd_halo, stats_halo, table),
        scratch=[pltpu.VMEM((far * z.hg * 8, z.wide), F32)],
        flops=2 * far * z.pairs * unit,
    )
    dk, dv = call(
        bind(grad_kv_kernel, z),
        [((group * tok, z.cw), BF16)] * 2,
        (qm, dom, p16, s16, *halo_terms),
        flops=2 * (near + far) * z.pairs * unit,
    )
    ret = call(bind(seal_kernel, z, 3), [((3 * tok, z.cw), BF16)] * group, (dq, dk, dv))
    back = swapped(ret)

    (joined,) = call(join_kernel, [((8 * sides, buckets), F32)], sums_of)
    spread = swapped([joined] * group)
    grads = call(
        bind(unpack_kernel, z),
        [((tok, width), BF16)] * 3,
        back,
        out_space=hbm,
        scratch=[pltpu.SemaphoreType.DMA((3 * group,))],
    )
    (grad_bias,) = call(
        bind(spread_kernel, z, sides),
        [((heads * sides, buckets), F32)],
        spread,
        out_space=hbm,
        scratch=[pltpu.VMEM((heads * sides, buckets), F32), pltpu.SemaphoreType.DMA((1,))],
    )
    return (*grads, grad_bias)


def solution(mesh):
    placed = (
        P("seq", "head"),
        P("seq", "head"),
        P("seq", "head"),
        P("seq", "head"),
        P("head", None),
        P("seq", None, None),
        P("seq", None),
    )

    return jax.shard_map(
        body,
        mesh=mesh,
        in_specs=placed,
        out_specs=(P("seq", "head"), P("seq", "head"), P("seq", "head"), P()),
        check_vma=False,
    )
```

```python
import math

import jax
import jax.numpy as jnp
from jax import lax
from jax.experimental import pallas as pl
from jax.experimental.pallas import tpu as pltpu
from jax.sharding import PartitionSpec as P


F32 = jnp.float32
BF16 = jnp.bfloat16
NEG = -1e30
NT = (((1,), (1,)), ((), ()))
NN = (((1,), (0,)), ((), ()))
CODE_ROWS = 16
VMEM_BYTES = 67043328


def dot(a, b, dims):
    return lax.dot_general(a, b, dims, preferred_element_type=F32)


def at(start, size):
    return pl.ds(pl.multiple_of(start, size), size)


def call(kernel, outs, args, scratch=(), spaces=None, out_space=pltpu.VMEM, flops=0, limit=16 << 20):
    spaces = spaces or [pltpu.VMEM] * len(args)
    moved = sum(a.size * a.dtype.itemsize for a in args)
    args = [
        pltpu.with_memory_space_constraint(a, s) if s == pltpu.VMEM else a for a, s in zip(args, spaces, strict=True)
    ]
    return pl.pallas_call(
        kernel,
        out_shape=tuple(out_space(s, d) for s, d in outs),
        in_specs=[pl.BlockSpec(memory_space=s) for s in spaces],
        out_specs=tuple(pl.BlockSpec(memory_space=out_space) for _ in outs),
        scratch_shapes=list(scratch),
        compiler_params=pltpu.CompilerParams(vmem_limit_bytes=limit),
        cost_estimate=pl.CostEstimate(flops=flops, bytes_accessed=moved, transcendentals=0),
    )(*args)


class Sizes:
    def __init__(self, tok, width, heads, span, buckets, group):
        self.tok, self.width, self.heads, self.span, self.buckets = tok, width, heads, span, buckets
        self.group = group
        self.hd = width // heads
        self.hg = heads // group
        self.cw = self.hg * self.hd
        self.pairs = self.hg // 2
        self.scale = self.hd ** (-0.5)
        self.halo = span - 1
        self.ext = group + self.halo
        self.wide = 2 * tok
        self.rows = 2 * tok + CODE_ROWS
        self.near = [(i, s) for i in range(group) for s in range(span) if s <= i]
        self.far = [(i, s) for i in range(group) for s in range(span) if s > i]
        assert heads % group == 0 and self.hg % 2 == 0 and 2 * self.hd == 128
        assert tok == 128 and buckets == 128 and group >= self.halo and self.hg <= 8
        assert math.frexp(self.scale)[0] == 0.5

    def me(self):
        return lax.rem(lax.axis_index("seq"), self.group)


def chunk_copies(z, sources, dst, sem, first):
    copies = []
    for g in range(z.group):
        cols = at((z.me() ^ g) * z.cw, z.cw)
        for n, src in enumerate(sources):
            rows = pl.ds(n * z.tok, z.tok)
            copies.append(pltpu.make_async_copy(src.at[:, cols], dst[g].at[rows, :], sem.at[first + len(copies)]))
    return copies


def pack_kv_kernel(z, k, v, bias, ids, mask, *refs):
    kv = refs[: z.group]
    table, slots, flags, sem = refs[z.group :]
    index = lax.axis_index("seq")
    copies = [
        pltpu.make_async_copy(ids.at[0], slots, sem.at[0]),
        pltpu.make_async_copy(mask, flags, sem.at[1]),
        pltpu.make_async_copy(bias, table, sem.at[2]),
    ]
    copies += chunk_copies(z, (k, v), kv, sem, len(copies))
    for copy in copies:
        copy.start()
    for copy in copies[:2]:
        copy.wait()
    rows = []
    for s in range(z.span):
        valid = True if s == 0 else (flags[0, s] == 1) & (index >= s)
        rows.append(jnp.where(valid, slots[s : s + 1, :] + 1, 0))
    rows.append(jnp.zeros((CODE_ROWS - z.span, z.wide), jnp.int32))
    codes = jnp.concatenate(rows, axis=0).astype(F32).astype(BF16)
    for g in range(z.group):
        kv[g][2 * z.tok :, :] = codes
    for copy in copies[2:]:
        copy.wait()


def pack_qd_kernel(z, q, d, *refs):
    copies = chunk_copies(z, (q, d), refs[: z.group], refs[z.group], 0)
    for copy in copies:
        copy.start()
    for copy in copies:
        copy.wait()


def kv_halo_kernel(z, *refs):
    out = refs[-1]
    me = z.me()
    first = z.group - z.halo
    for k in range(z.group):
        j = me ^ k

        @pl.when(j >= first)
        def _():
            out[at((j - first) * 2 * z.tok, 2 * z.tok), :] = refs[k][0 : 2 * z.tok, :]


def qd_halo_kernel(z, *refs):
    qd, kv, out = refs[: z.group], refs[z.group : -1], refs[-1]
    me = z.me()
    for k in range(z.group):
        j = me ^ k

        @pl.when(j < z.halo)
        def _():
            top = pl.multiple_of(j * z.rows, 16)
            out[pl.ds(top, 2 * z.tok), :] = qd[k][...]
            out[pl.ds(top + 2 * z.tok, CODE_ROWS), :] = kv[k][2 * z.tok :, :]


def onehot_of(codes, z):
    slots = lax.broadcasted_iota(jnp.int32, (z.buckets, codes.shape[1]), 0) + 1
    return jnp.where(codes.astype(jnp.int32) == slots, 1.0, 0.0).astype(BF16)


def thirds(x):
    hi = x.astype(BF16)
    rest = x - hi.astype(F32)
    mid = rest.astype(BF16)
    low = (rest - mid.astype(F32)).astype(BF16)
    return jnp.concatenate([hi.astype(F32), mid.astype(F32), low.astype(F32)], axis=0).astype(BF16)


def by_offset(split, codes, z):
    got = dot(split, onehot_of(codes, z), NN)
    return got[0:8] + got[8:16] + got[16:24] + jnp.where(codes == 0.0, NEG, 0.0)


def masked_pair(x, z):
    lane = lax.broadcasted_iota(jnp.int32, x.shape, 1)
    zero = jnp.zeros_like(x)
    return jnp.concatenate([jnp.where(lane < z.hd, x, zero), jnp.where(lane < z.hd, zero, x)], axis=0)


def slanted(row, z):
    return pltpu.roll(jnp.broadcast_to(row, (8, z.wide)), z.tok + 1, 1, stride=1, stride_axis=0)


def toeplitz(base, z):
    tok = z.tok
    lane = lax.broadcasted_iota(jnp.int32, (8, tok), 1)
    low, high = base[:, 0:tok], base[:, tok:]
    tiles = [low]
    for g in range(1, tok // 8):
        tiles.append(pltpu.roll(jnp.where(lane >= tok - 8 * g, high, low), 8 * g, 1))
    return jnp.concatenate(tiles, axis=0)


def my_table(table, z):
    head = lax.broadcasted_iota(jnp.int32, (8, z.buckets), 0)
    rows = jnp.zeros((8, z.buckets), F32)
    for h in range(z.hg):
        rows = jnp.where(head == h, table[pl.ds(z.me() * z.hg + h, 1), :], rows)
    return rows


def slant_tables(z, table, code_rows, bases):
    split = thirds(my_table(table, z))
    for n, codes in enumerate(code_rows):
        rows = by_offset(split, codes, z)
        for h in range(z.hg):
            at_row = (n * z.hg + h) * 8
            bases[at_row : at_row + 8, :] = slanted(rows[h : h + 1, :], z)


def diagonals(x, z):
    tok = z.tok
    lane = lax.broadcasted_iota(jnp.int32, (8, tok), 1)
    total = x[tok - 8 :]
    high = jnp.zeros((8, tok), F32)
    for g in range(tok // 8 - 1):
        by = tok - 8 - 8 * g
        part = pltpu.roll(x[8 * g : 8 * g + 8], by, 1)
        total = total + part
        high = high + jnp.where(lane < by, part, 0.0)
    return total - high, high


def aligned(both):
    left = 7 - (lax.broadcasted_iota(jnp.int32, both.shape, 0) & 7)
    for bit in (1, 2, 4):
        both = jnp.where((left & bit) != 0, pltpu.roll(both, bit, 1), both)
    return both


def causal(z):
    row = lax.broadcasted_iota(jnp.int32, (z.tok, z.wide), 0)
    col = lax.broadcasted_iota(jnp.int32, (z.tok, z.wide), 1) % z.tok
    return row <= col


def folded(x, how):
    return how(how(x.reshape(x.shape[0] // 8, 8, x.shape[1]), 0), 0, keepdims=True)


def bias_rows(z, bases, n, pair):
    rows = [toeplitz(bases[(n * z.hg + 2 * pair + e) * 8 : (n * z.hg + 2 * pair + e + 1) * 8, :], z) for e in range(2)]
    return jnp.concatenate(rows, axis=1)


def bias_kernel(z, *refs):
    kv, table = refs[: z.group], refs[z.group]
    keys, values, near, far, codes, bases = refs[z.group + 1 :]
    tok = z.tok
    me = z.me()
    for k in range(z.group):
        j = me ^ k
        keys[at(j * tok, tok), :] = kv[k][0:tok, :]
        values[at(j * tok, tok), :] = kv[k][tok : 2 * tok, :]
        codes[at(j * CODE_ROWS, CODE_ROWS), :] = kv[k][2 * tok :, :].astype(F32)
    tables = [(i, s) for i in range(z.group) for s in range(z.span)]
    slant_tables(z, table, [codes[i * CODE_ROWS + s : i * CODE_ROWS + s + 1, :] for i, s in tables], bases)
    for tiles, out in ((z.near, near), (z.far, far)):
        for t, (i, s) in enumerate(tiles):
            for pair in range(z.pairs):
                bias = bias_rows(z, bases, i * z.span + s, pair)
                out[t * z.pairs + pair] = jnp.where(causal(z), bias, NEG) if s == 0 else bias


def forward_tile(key, value, q, d, bias, row, sum_row, outs):
    weights, dprobs, tops, totals, accums = outs
    scores = dot(key, q, NT) + bias[row]
    top = folded(scores, jnp.max)
    w = jnp.exp(scores - top)
    dprob = dot(value, d, NT)
    weights[row] = w
    dprobs[row] = dprob
    tops[pl.ds(sum_row, 1), :] = top
    totals[pl.ds(sum_row, 1), :] = folded(w, jnp.sum)
    accums[pl.ds(sum_row, 1), :] = folded(w * dprob, jnp.sum)


def near_kernel(z, *refs):
    qd, keys, values, bias = refs[: z.group], *refs[z.group : z.group + 3]
    qm, dom, *outs = refs[z.group + 3 :]
    tok = z.tok
    me = z.me()
    for k in range(z.group):
        j = me ^ k
        for pair in range(z.pairs):
            lanes = slice(pair * 128, (pair + 1) * 128)
            rows = at(j * z.wide, z.wide)
            qm[pair, rows, :] = masked_pair(qd[k][0:tok, lanes] * jnp.asarray(z.scale, BF16), z)
            dom[pair, rows, :] = masked_pair(qd[k][tok : 2 * tok, lanes], z)

    def each(pair, _):
        lanes = at(pair * 128, 128)
        for t, (i, s) in enumerate(z.near):
            rows = slice((i - s) * tok, (i - s + 1) * tok)
            wide = slice(i * z.wide, (i + 1) * z.wide)
            forward_tile(
                keys[rows, lanes], values[rows, lanes], qm[pair, wide, :], dom[pair, wide, :],
                bias, t * z.pairs + pair, (s * z.group + i) * z.pairs + pair, outs,
            )
        return 0

    lax.fori_loop(0, z.pairs, each, 0)


def far_kernel(z, halo, qm, dom, bias, tops, totals, accums, stats, factors, weights, dprobs, *sums):
    tok = z.tok
    units = z.group * z.pairs
    for mine, near in zip(sums, (tops, totals, accums), strict=True):
        mine[...] = near[...]

    def each(pair, _):
        lanes = at(pair * 128, 128)
        for t, (i, s) in enumerate(z.far):
            b = z.halo + i - s
            wide = slice(i * z.wide, (i + 1) * z.wide)
            forward_tile(
                halo[2 * b * tok : (2 * b + 1) * tok, lanes], halo[(2 * b + 1) * tok : (2 * b + 2) * tok, lanes],
                qm[pair, wide, :], dom[pair, wide, :],
                bias, t * z.pairs + pair, (s * z.group + i) * z.pairs + pair, (weights, dprobs, *sums),
            )
        return 0

    lax.fori_loop(0, z.pairs, each, 0)
    peaks, parts, products = ([ref[s * units : (s + 1) * units, :] for s in range(z.span)] for ref in sums)
    top = peaks[0]
    for peak in peaks[1:]:
        top = jnp.maximum(top, peak)
    total = jnp.zeros_like(top)
    accum = jnp.zeros_like(top)
    for peak, part, product in zip(peaks, parts, products, strict=True):
        share = jnp.exp(peak - top)
        total = total + share * part
        accum = accum + share * product
    lse = top + jnp.log(total)
    for s, peak in enumerate(peaks):
        factors[s * units : (s + 1) * units, :] = jnp.exp(peak - lse)
    stats[0:units, :] = lse
    stats[units:, :] = accum / total


def own_kernel(z, codes, stats, factors, wnear, dnear, wfar, dfar, p16, s16, sent, offs):
    tok, span = z.tok, z.span

    def each(pair, _):
        for i in range(z.group):
            wide = slice(i * z.wide, (i + 1) * z.wide)
            delta = stats[pl.ds((z.group + i) * z.pairs + pair, 1), :]
            for s in range(span):
                close = s <= i
                t = (z.near if close else z.far).index((i, s)) * z.pairs + pair
                w, d = (wnear, dnear) if close else (wfar, dfar)
                prob = w[t] * factors[pl.ds((s * z.group + i) * z.pairs + pair, 1), :]
                dscore = prob * (d[t] - delta)
                rows = slice((z.halo + i - s) * tok, (z.halo + i - s + 1) * tok)
                s16[pair, rows, wide] = dscore.astype(BF16)
                if close:
                    p16[pair, (i - s) * tok : (i - s + 1) * tok, wide] = prob.astype(BF16)
                for e in range(2):
                    low, high = diagonals(dscore[:, e * tok : (e + 1) * tok], z)
                    row = at(((i * span + s) * z.hg + 2 * pair + e) * 8, 8)
                    offs[row, 0:tok] = low
                    offs[row, tok:] = high
        return 0

    lax.fori_loop(0, z.pairs, each, 0)
    head = lax.broadcasted_iota(jnp.int32, (8, z.wide), 0)
    total = jnp.zeros((8, z.buckets), F32)
    for n in range(z.group * span):
        both = aligned(offs[n * z.hg * 8 : (n + 1) * z.hg * 8, :])
        sums = jnp.zeros((8, z.wide), F32)
        for h in range(z.hg):
            sums = sums + jnp.where(head == h, both[8 * h : 8 * h + 8].sum(axis=0, keepdims=True), 0.0)
        row = n // span * CODE_ROWS + n % span
        got = dot(thirds(sums), onehot_of(codes[row : row + 1, :], z), NT)
        total = total + (got[0:8] + got[8:16] + got[16:24])
    sent[0:8, :] = jnp.concatenate([total, jnp.zeros_like(total)], axis=1)
    sent[8:, :] = stats[...]


def grad_q_kernel(z, keys, halo, s16, dq):
    tok, span = z.tok, z.span

    def each(pair, _):
        lanes = at(pair * 128, 128)
        blocks = [halo[2 * b * tok : (2 * b + 1) * tok, lanes] for b in range(z.halo)]
        blocks += [keys[j * tok : (j + 1) * tok, lanes] for j in range(z.group)]
        turned = jnp.concatenate([block.T for block in blocks], axis=1)
        for i in range(z.group):
            window = slice(i * tok, (i + span) * tok)
            cross = dot(turned[:, window], s16[pair, window, i * z.wide : (i + 1) * z.wide], NN)
            both = jnp.concatenate([cross[0 : z.hd, 0:tok], cross[z.hd :, tok:]], axis=0)
            dq[i * tok : (i + 1) * tok, lanes] = (z.scale * both.T).astype(BF16)
        return 0

    lax.fori_loop(0, z.pairs, each, 0)


def tail_kernel(z, stages, keys, values, halo, *refs):
    received, (table, qh, dh, ph, sh, bases, stats) = refs[:stages], refs[stages:]
    tok, span = z.tok, z.span
    tables = [(b, s) for b in range(z.halo) for s in range(b + 1, span)]
    rows = []
    for b in range(z.halo):
        codes = halo[b * z.rows + 2 * tok : (b + 1) * z.rows, :].astype(F32)
        rows += [codes[s : s + 1, :] for s in range(b + 1, span)]
    slant_tables(z, table, rows, bases)
    mine = lax.div(lax.axis_index("seq"), z.group)
    stats[...] = received[0][8:, :]
    for t in range(1, stages):

        @pl.when(lax.rem(mine, 2**t) == 2**t - 1)
        def _():
            stats[...] = received[t][8:, :]

    for pair in range(z.pairs):
        lanes = slice(pair * 128, (pair + 1) * 128)
        for b in range(z.halo):
            top = b * z.rows
            wide = slice(b * z.wide, (b + 1) * z.wide)
            q = masked_pair(halo[top : top + tok, lanes] * jnp.asarray(z.scale, BF16), z)
            d = masked_pair(halo[top + tok : top + 2 * tok, lanes], z)
            qh[pair, wide, :] = q
            dh[pair, wide, :] = d
            u = b * z.pairs + pair
            lse, delta = (stats[r : r + 1, :] for r in (u, z.group * z.pairs + u))
            for s in range(b + 1, span):
                j = z.group + b - s
                block = slice(j * tok, (j + 1) * tok)
                bias = bias_rows(z, bases, tables.index((b, s)), pair)
                prob = jnp.exp(dot(keys[block, lanes], q, NT) + bias - lse)
                dscore = prob * (dot(values[block, lanes], d, NT) - delta)
                ph[pair, block, wide] = prob.astype(BF16)
                sh[pair, block, wide] = dscore.astype(BF16)


def grad_kv_kernel(z, qm, dom, p16, s16, dk, dv):
    def each(pair, _):
        lanes = at(pair * 128, 128)
        for j in range(z.group):
            rows = slice(j * z.tok, (j + 1) * z.tok)
            ext = slice((z.halo + j) * z.tok, (z.halo + j + 1) * z.tok)
            near = slice(j * z.wide, z.group * z.wide)
            dk[rows, lanes] = dot(s16[pair, ext, near], qm[pair, near, :], NN)
            dv[rows, lanes] = dot(p16[pair, rows, near], dom[pair, near, :], NN)
        return 0

    lax.fori_loop(0, z.pairs, each, 0)


def halo_kv_kernel(z, near_k, near_v, qh, dh, ph, sh, dk, dv):
    def each(pair, _):
        lanes = at(pair * 128, 128)
        for j in range(z.group):
            rows = slice(j * z.tok, (j + 1) * z.tok)
            gk, gv = near_k[rows, lanes], near_v[rows, lanes]
            count = min(z.halo, j + z.span - z.group)
            if count > 0:
                past = slice(0, count * z.wide)
                gk = gk + dot(sh[pair, rows, past], qh[pair, past, :], NN)
                gv = gv + dot(ph[pair, rows, past], dh[pair, past, :], NN)
            dk[rows, lanes] = gk.astype(BF16)
            dv[rows, lanes] = gv.astype(BF16)
        return 0

    lax.fori_loop(0, z.pairs, each, 0)


def seal_kernel(z, grads, *refs):
    sources, sends = refs[:grads], refs[grads:]
    for k in range(z.group):
        rows = at((z.me() ^ k) * z.tok, z.tok)
        for n, ref in enumerate(sources):
            sends[k][n * z.tok : (n + 1) * z.tok, :] = ref[rows, :]


def join_kernel(*refs):
    for n, ref in enumerate(refs[:-1]):
        refs[-1][8 * n : 8 * n + 8, :] = ref[...]


def total_kernel(mine, other, total):
    total[...] = (mine[0:8, :] + other[0:8, :])[:, 0 : total.shape[1]]


def stage_kernel(mine, other, sent):
    sent[0:8, :] = mine[0:8, :] + other[0:8, :]
    sent[8:, :] = other[8:, :]


def unpack_kernel(z, *refs):
    got, outs, sem = refs[: z.group], refs[z.group : -1], refs[-1]
    me = z.me()
    copies = []
    for k in range(z.group):
        cols = at((me ^ k) * z.cw, z.cw)
        for n, out in enumerate(outs):
            src = got[k].at[n * z.tok : (n + 1) * z.tok, :]
            copies.append(pltpu.make_async_copy(src, out.at[:, cols], sem.at[len(copies)]))
    for copy in copies:
        copy.start()
    for copy in copies:
        copy.wait()


def spread_kernel(z, sides, *refs):
    sums, (gb, held, sem) = refs[: z.group], refs[z.group :]
    me = z.me()
    owner = lax.broadcasted_iota(jnp.int32, held.shape, 0) // z.hg
    total = jnp.zeros(held.shape, F32)
    for k in range(z.group):
        for n in range(sides):
            wide = jnp.concatenate([sums[k][8 * n : 8 * n + z.hg, :]] * (held.shape[0] // z.hg), axis=0)
            side = lax.axis_index("head") ^ n
            total = total + jnp.where(owner == side * z.group + (me ^ k), wide, 0.0)
    held[...] = total
    copy = pltpu.make_async_copy(held, gb, sem.at[0])
    copy.start()
    copy.wait()


def bind(kernel, *fixed):
    def bound(*refs):
        return kernel(*fixed, *refs)

    return bound


def body(queries, keys, values, grad_out, bias_table, bucket_ids, block_mask):
    tok, width = queries.shape
    heads, buckets = bias_table.shape
    span = block_mask.shape[1]
    group = span
    z = Sizes(tok, width, heads, span, buckets, group)
    blocks = lax.axis_size("seq")
    sides = lax.axis_size("head")
    assert blocks % group == 0 and (blocks & (blocks - 1)) == 0 and (sides & (sides - 1)) == 0

    def swap(value, by, axis="seq"):
        return lax.ppermute(value, axis, [(i, i ^ by) for i in range(lax.axis_size(axis))])

    def shifted(value, by):
        return lax.ppermute(value, "seq", [(i, i + by) for i in range(blocks) if 0 <= i + by < blocks])

    def swapped(parts):
        return [parts[0]] + [swap(parts[k], k) for k in range(1, group)]

    hbm = pltpu.HBM
    pack_bytes = group * (z.rows + 2 * tok) * z.cw * 2
    room = VMEM_BYTES - pack_bytes - (520 << 10)
    *kv, table = call(
        bind(pack_kv_kernel, z),
        [((z.rows, z.cw), BF16)] * group + [((heads, buckets), F32)],
        (keys, values, bias_table, bucket_ids, block_mask),
        spaces=[hbm] * 5,
        scratch=[
            pltpu.VMEM((span, z.wide), jnp.int32),
            pltpu.SMEM((1, span), jnp.int32),
            pltpu.SemaphoreType.DMA((2 * group + 3,)),
        ],
        limit=room,
    )
    qd = call(
        bind(pack_qd_kernel, z),
        [((2 * tok, z.cw), BF16)] * group,
        (queries, grad_out),
        spaces=[hbm] * 2,
        scratch=[pltpu.SemaphoreType.DMA((2 * group,))],
        limit=room - (group - 1) * z.rows * z.cw * 2,
    )
    kv_got = swapped(kv)
    qd_got = swapped(qd)
    (kv_out,) = call(bind(kv_halo_kernel, z), [((z.halo * 2 * tok, z.cw), BF16)], kv_got)
    kv_halo = shifted(kv_out, group)
    (qd_out,) = call(bind(qd_halo_kernel, z), [((z.halo * z.rows, z.cw), BF16)], (*qd_got, *kv_got))
    qd_halo = shifted(qd_out, -group)

    def tile_outs(count):
        tile = ((count * z.pairs, tok, z.wide), F32)
        row = ((span * group * z.pairs, z.wide), F32)
        return [tile, tile, row, row, row]

    near, far = len(z.near), len(z.far)
    unit = 2 * 128 * tok * z.wide
    own_k, own_v, bias_near, bias_far, codes = call(
        bind(bias_kernel, z),
        [((group * tok, z.cw), BF16)] * 2
        + [((near * z.pairs, tok, z.wide), F32), ((far * z.pairs, tok, z.wide), F32)]
        + [((group * CODE_ROWS, z.wide), F32)],
        (*kv_got, table),
        scratch=[pltpu.VMEM((group * span * z.hg * 8, z.wide), F32)],
    )
    qm, dom, wnear, dnear, *sums = call(
        bind(near_kernel, z),
        [((z.pairs, group * z.wide, 128), BF16)] * 2 + tile_outs(near),
        (*qd_got, own_k, own_v, bias_near),
        flops=2 * near * z.pairs * unit,
    )
    stats, factors, wfar, dfar, *_ = call(
        bind(far_kernel, z),
        [((2 * group * z.pairs, z.wide), F32), ((span * group * z.pairs, z.wide), F32)] + tile_outs(far),
        (kv_halo, qm, dom, bias_far, *sums),
        flops=2 * far * z.pairs * unit,
    )
    p16, s16, gb = call(
        bind(own_kernel, z),
        [
            ((z.pairs, group * tok, group * z.wide), BF16),
            ((z.pairs, z.ext * tok, group * z.wide), BF16),
            ((8 + 2 * group * z.pairs, z.wide), F32),
        ],
        (codes, stats, factors, wnear, dnear, wfar, dfar),
        scratch=[pltpu.VMEM((group * span * z.hg * 8, z.wide), F32)],
    )
    by, received = group, []
    while by < blocks:
        received.append(swap(gb, by))
        by *= 2
        last = by == blocks
        (gb,) = call(
            total_kernel if last else stage_kernel,
            [((8, buckets), F32) if last else (gb.shape, F32)],
            (gb, received[-1]),
        )
    sums_of = [gb] + [swap(gb, k, "head") for k in range(1, sides)]
    (dq,) = call(
        bind(grad_q_kernel, z),
        [((group * tok, z.cw), BF16)],
        (own_k, kv_halo, s16),
        flops=(near + far) * z.pairs * unit,
    )
    lanes_of = ((z.pairs, group * tok, z.halo * z.wide), BF16)
    rows_of = ((z.pairs, z.halo * z.wide, 128), BF16)
    halo_terms = call(
        bind(tail_kernel, z, len(received)),
        [rows_of, rows_of, lanes_of, lanes_of],
        (own_k, own_v, qd_halo, *received, table),
        scratch=[pltpu.VMEM((far * z.hg * 8, z.wide), F32), pltpu.VMEM((2 * group * z.pairs, z.wide), F32)],
        flops=2 * far * z.pairs * unit,
    )
    near_grads = call(
        bind(grad_kv_kernel, z), [((group * tok, z.cw), F32)] * 2, (qm, dom, p16, s16), flops=2 * near * z.pairs * unit
    )
    dk, dv = call(
        bind(halo_kv_kernel, z),
        [((group * tok, z.cw), BF16)] * 2,
        (*near_grads, *halo_terms),
        flops=2 * far * z.pairs * unit,
    )
    ret = call(bind(seal_kernel, z, 3), [((3 * tok, z.cw), BF16)] * group, (dq, dk, dv))
    back = swapped(ret)

    (joined,) = call(join_kernel, [((8 * sides, buckets), F32)], sums_of)
    spread = swapped([joined] * group)
    grads = call(
        bind(unpack_kernel, z),
        [((tok, width), BF16)] * 3,
        back,
        out_space=hbm,
        scratch=[pltpu.SemaphoreType.DMA((3 * group,))],
    )
    (grad_bias,) = call(
        bind(spread_kernel, z, sides),
        [((heads * sides, buckets), F32)],
        spread,
        out_space=hbm,
        scratch=[pltpu.VMEM((heads * sides, buckets), F32), pltpu.SemaphoreType.DMA((1,))],
    )
    return (*grads, grad_bias)


def solution(mesh):
    placed = (
        P("seq", "head"),
        P("seq", "head"),
        P("seq", "head"),
        P("seq", "head"),
        P("head", None),
        P("seq", None, None),
        P("seq", None),
    )

    return jax.shard_map(
        body,
        mesh=mesh,
        in_specs=placed,
        out_specs=(P("seq", "head"), P("seq", "head"), P("seq", "head"), P()),
        check_vma=False,
    )
```

```python
import math

import jax
import jax.numpy as jnp
from jax import lax
from jax.experimental import pallas as pl
from jax.experimental.pallas import tpu as pltpu
from jax.sharding import PartitionSpec as P


F32 = jnp.float32
BF16 = jnp.bfloat16
NEG = -1e30
NT = (((1,), (1,)), ((), ()))
NN = (((1,), (0,)), ((), ()))
CODE_ROWS = 16
VMEM_BYTES = 67043328


def dot(a, b, dims):
    return lax.dot_general(a, b, dims, preferred_element_type=F32)


def at(start, size):
    return pl.ds(pl.multiple_of(start, size), size)


def call(kernel, outs, args, scratch=(), spaces=None, out_space=pltpu.VMEM, flops=0, limit=16 << 20):
    spaces = spaces or [pltpu.VMEM] * len(args)
    moved = sum(a.size * a.dtype.itemsize for a in args)
    args = [
        pltpu.with_memory_space_constraint(a, s) if s == pltpu.VMEM else a for a, s in zip(args, spaces, strict=True)
    ]
    return pl.pallas_call(
        kernel,
        out_shape=tuple(out_space(s, d) for s, d in outs),
        in_specs=[pl.BlockSpec(memory_space=s) for s in spaces],
        out_specs=tuple(pl.BlockSpec(memory_space=out_space) for _ in outs),
        scratch_shapes=list(scratch),
        compiler_params=pltpu.CompilerParams(vmem_limit_bytes=limit),
        cost_estimate=pl.CostEstimate(flops=flops, bytes_accessed=moved, transcendentals=0),
    )(*args)


class Sizes:
    def __init__(self, tok, width, heads, span, buckets, group):
        self.tok, self.width, self.heads, self.span, self.buckets = tok, width, heads, span, buckets
        self.group = group
        self.hd = width // heads
        self.hg = heads // group
        self.cw = self.hg * self.hd
        self.pairs = self.hg // 2
        self.scale = self.hd ** (-0.5)
        self.halo = span - 1
        self.ext = group + self.halo
        self.wide = 2 * tok
        self.rows = 2 * tok + CODE_ROWS
        self.near = [(i, s) for i in range(group) for s in range(span) if s <= i]
        self.far = [(i, s) for i in range(group) for s in range(span) if s > i]
        assert heads % group == 0 and self.hg % 2 == 0 and 2 * self.hd == 128
        assert tok == 128 and buckets == 128 and group >= self.halo and self.hg <= 8
        assert math.frexp(self.scale)[0] == 0.5

    def me(self):
        return lax.rem(lax.axis_index("seq"), self.group)


def chunk_copies(z, sources, dst, sem, first):
    copies = []
    for g in range(z.group):
        cols = at((z.me() ^ g) * z.cw, z.cw)
        for n, src in enumerate(sources):
            rows = pl.ds(n * z.tok, z.tok)
            copies.append(pltpu.make_async_copy(src.at[:, cols], dst[g].at[rows, :], sem.at[first + len(copies)]))
    return copies


def pack_kv_kernel(z, k, v, bias, ids, mask, *refs):
    kv = refs[: z.group]
    table, slots, flags, sem = refs[z.group :]
    index = lax.axis_index("seq")
    copies = [
        pltpu.make_async_copy(ids.at[0], slots, sem.at[0]),
        pltpu.make_async_copy(mask, flags, sem.at[1]),
        pltpu.make_async_copy(bias, table, sem.at[2]),
    ]
    copies += chunk_copies(z, (k, v), kv, sem, len(copies))
    for copy in copies:
        copy.start()
    for copy in copies[:2]:
        copy.wait()
    rows = []
    for s in range(z.span):
        valid = True if s == 0 else (flags[0, s] == 1) & (index >= s)
        rows.append(jnp.where(valid, slots[s : s + 1, :] + 1, 0))
    rows.append(jnp.zeros((CODE_ROWS - z.span, z.wide), jnp.int32))
    codes = jnp.concatenate(rows, axis=0).astype(F32).astype(BF16)
    for g in range(z.group):
        kv[g][2 * z.tok :, :] = codes
    for copy in copies[2:]:
        copy.wait()


def pack_qd_kernel(z, q, d, *refs):
    copies = chunk_copies(z, (q, d), refs[: z.group], refs[z.group], 0)
    for copy in copies:
        copy.start()
    for copy in copies:
        copy.wait()


def kv_halo_kernel(z, *refs):
    out = refs[-1]
    me = z.me()
    first = z.group - z.halo
    for k in range(z.group):
        j = me ^ k

        @pl.when(j >= first)
        def _():
            out[at((j - first) * 2 * z.tok, 2 * z.tok), :] = refs[k][0 : 2 * z.tok, :]


def qd_halo_kernel(z, *refs):
    qd, kv, out = refs[: z.group], refs[z.group : -1], refs[-1]
    me = z.me()
    for k in range(z.group):
        j = me ^ k

        @pl.when(j < z.halo)
        def _():
            top = pl.multiple_of(j * z.rows, 16)
            out[pl.ds(top, 2 * z.tok), :] = qd[k][...]
            out[pl.ds(top + 2 * z.tok, CODE_ROWS), :] = kv[k][2 * z.tok :, :]


def onehot_of(codes, z):
    slots = lax.broadcasted_iota(jnp.int32, (z.buckets, codes.shape[1]), 0) + 1
    return jnp.where(codes.astype(jnp.int32) == slots, 1.0, 0.0).astype(BF16)


def thirds(x):
    hi = x.astype(BF16)
    rest = x - hi.astype(F32)
    mid = rest.astype(BF16)
    low = (rest - mid.astype(F32)).astype(BF16)
    return jnp.concatenate([hi.astype(F32), mid.astype(F32), low.astype(F32)], axis=0).astype(BF16)


def by_offset(split, codes, z):
    got = dot(split, onehot_of(codes, z), NN)
    return got[0:8] + got[8:16] + got[16:24] + jnp.where(codes == 0.0, NEG, 0.0)


def masked_pair(x, z):
    lane = lax.broadcasted_iota(jnp.int32, x.shape, 1)
    zero = jnp.zeros_like(x)
    return jnp.concatenate([jnp.where(lane < z.hd, x, zero), jnp.where(lane < z.hd, zero, x)], axis=0)


def slanted(row, z):
    return pltpu.roll(jnp.broadcast_to(row, (8, z.wide)), z.tok + 1, 1, stride=1, stride_axis=0)


def toeplitz(base, z):
    tok = z.tok
    lane = lax.broadcasted_iota(jnp.int32, (8, tok), 1)
    low, high = base[:, 0:tok], base[:, tok:]
    tiles = [low]
    for g in range(1, tok // 8):
        tiles.append(pltpu.roll(jnp.where(lane >= tok - 8 * g, high, low), 8 * g, 1))
    return jnp.concatenate(tiles, axis=0)


def my_table(table, z):
    head = lax.broadcasted_iota(jnp.int32, (8, z.buckets), 0)
    rows = jnp.zeros((8, z.buckets), F32)
    for h in range(z.hg):
        rows = jnp.where(head == h, table[pl.ds(z.me() * z.hg + h, 1), :], rows)
    return rows


def slant_tables(z, table, code_rows, bases):
    split = thirds(my_table(table, z))
    for n, codes in enumerate(code_rows):
        rows = by_offset(split, codes, z)
        for h in range(z.hg):
            at_row = (n * z.hg + h) * 8
            bases[at_row : at_row + 8, :] = slanted(rows[h : h + 1, :], z)


def diagonals(x, z):
    tok = z.tok
    lane = lax.broadcasted_iota(jnp.int32, (8, tok), 1)
    total = x[tok - 8 :]
    high = jnp.zeros((8, tok), F32)
    for g in range(tok // 8 - 1):
        by = tok - 8 - 8 * g
        part = pltpu.roll(x[8 * g : 8 * g + 8], by, 1)
        total = total + part
        high = high + jnp.where(lane < by, part, 0.0)
    return total - high, high


def aligned(both):
    left = 7 - (lax.broadcasted_iota(jnp.int32, both.shape, 0) & 7)
    for bit in (1, 2, 4):
        both = jnp.where((left & bit) != 0, pltpu.roll(both, bit, 1), both)
    return both


def causal(z):
    row = lax.broadcasted_iota(jnp.int32, (z.tok, z.wide), 0)
    col = lax.broadcasted_iota(jnp.int32, (z.tok, z.wide), 1) % z.tok
    return row <= col


def folded(x, how):
    return how(how(x.reshape(x.shape[0] // 8, 8, x.shape[1]), 0), 0, keepdims=True)


def bias_rows(z, bases, n, pair):
    rows = [toeplitz(bases[(n * z.hg + 2 * pair + e) * 8 : (n * z.hg + 2 * pair + e + 1) * 8, :], z) for e in range(2)]
    return jnp.concatenate(rows, axis=1)


def bias_kernel(z, *refs):
    kv, table = refs[: z.group], refs[z.group]
    keys, values, near, far, codes, bases = refs[z.group + 1 :]
    tok = z.tok
    me = z.me()
    for k in range(z.group):
        j = me ^ k
        keys[at(j * tok, tok), :] = kv[k][0:tok, :]
        values[at(j * tok, tok), :] = kv[k][tok : 2 * tok, :]
        codes[at(j * CODE_ROWS, CODE_ROWS), :] = kv[k][2 * tok :, :].astype(F32)
    tables = [(i, s) for i in range(z.group) for s in range(z.span)]
    slant_tables(z, table, [codes[i * CODE_ROWS + s : i * CODE_ROWS + s + 1, :] for i, s in tables], bases)
    for tiles, out in ((z.near, near), (z.far, far)):
        for t, (i, s) in enumerate(tiles):
            for pair in range(z.pairs):
                bias = bias_rows(z, bases, i * z.span + s, pair)
                out[t * z.pairs + pair] = jnp.where(causal(z), bias, NEG) if s == 0 else bias


def forward_tile(key, value, q, d, bias, row, sum_row, outs):
    weights, dprobs, tops, totals, accums = outs
    scores = dot(key, q, NT) + bias[row]
    top = folded(scores, jnp.max)
    w = jnp.exp(scores - top)
    dprob = dot(value, d, NT)
    weights[row] = w
    dprobs[row] = dprob
    tops[pl.ds(sum_row, 1), :] = top
    totals[pl.ds(sum_row, 1), :] = folded(w, jnp.sum)
    accums[pl.ds(sum_row, 1), :] = folded(w * dprob, jnp.sum)


def near_kernel(z, *refs):
    qd, keys, values, bias = refs[: z.group], *refs[z.group : z.group + 3]
    qm, dom, *outs = refs[z.group + 3 :]
    tok = z.tok
    me = z.me()
    for k in range(z.group):
        j = me ^ k
        for pair in range(z.pairs):
            lanes = slice(pair * 128, (pair + 1) * 128)
            rows = at(j * z.wide, z.wide)
            qm[pair, rows, :] = masked_pair(qd[k][0:tok, lanes] * jnp.asarray(z.scale, BF16), z)
            dom[pair, rows, :] = masked_pair(qd[k][tok : 2 * tok, lanes], z)

    def each(pair, _):
        lanes = at(pair * 128, 128)
        for t, (i, s) in enumerate(z.near):
            rows = slice((i - s) * tok, (i - s + 1) * tok)
            wide = slice(i * z.wide, (i + 1) * z.wide)
            forward_tile(
                keys[rows, lanes], values[rows, lanes], qm[pair, wide, :], dom[pair, wide, :],
                bias, t * z.pairs + pair, (s * z.group + i) * z.pairs + pair, outs,
            )
        return 0

    lax.fori_loop(0, z.pairs, each, 0)


def far_kernel(z, halo, qm, dom, bias, tops, totals, accums, stats, factors, weights, dprobs, *sums):
    tok = z.tok
    units = z.group * z.pairs
    for mine, near in zip(sums, (tops, totals, accums), strict=True):
        mine[...] = near[...]

    def each(pair, _):
        lanes = at(pair * 128, 128)
        for t, (i, s) in enumerate(z.far):
            b = z.halo + i - s
            wide = slice(i * z.wide, (i + 1) * z.wide)
            forward_tile(
                halo[2 * b * tok : (2 * b + 1) * tok, lanes], halo[(2 * b + 1) * tok : (2 * b + 2) * tok, lanes],
                qm[pair, wide, :], dom[pair, wide, :],
                bias, t * z.pairs + pair, (s * z.group + i) * z.pairs + pair, (weights, dprobs, *sums),
            )
        return 0

    lax.fori_loop(0, z.pairs, each, 0)
    peaks, parts, products = ([ref[s * units : (s + 1) * units, :] for s in range(z.span)] for ref in sums)
    top = peaks[0]
    for peak in peaks[1:]:
        top = jnp.maximum(top, peak)
    total = jnp.zeros_like(top)
    accum = jnp.zeros_like(top)
    for peak, part, product in zip(peaks, parts, products, strict=True):
        share = jnp.exp(peak - top)
        total = total + share * part
        accum = accum + share * product
    lse = top + jnp.log(total)
    for s, peak in enumerate(peaks):
        factors[s * units : (s + 1) * units, :] = jnp.exp(peak - lse)
    stats[0:units, :] = lse
    stats[units:, :] = accum / total


def own_kernel(z, codes, stats, factors, wnear, dnear, wfar, dfar, p16, s16, gb, offs):
    tok, span = z.tok, z.span

    def each(pair, _):
        for i in range(z.group):
            wide = slice(i * z.wide, (i + 1) * z.wide)
            delta = stats[pl.ds((z.group + i) * z.pairs + pair, 1), :]
            for s in range(span):
                close = s <= i
                t = (z.near if close else z.far).index((i, s)) * z.pairs + pair
                w, d = (wnear, dnear) if close else (wfar, dfar)
                prob = w[t] * factors[pl.ds((s * z.group + i) * z.pairs + pair, 1), :]
                dscore = prob * (d[t] - delta)
                rows = slice((z.halo + i - s) * tok, (z.halo + i - s + 1) * tok)
                s16[pair, rows, wide] = dscore.astype(BF16)
                if close:
                    p16[pair, (i - s) * tok : (i - s + 1) * tok, wide] = prob.astype(BF16)
                for e in range(2):
                    low, high = diagonals(dscore[:, e * tok : (e + 1) * tok], z)
                    row = at(((i * span + s) * z.hg + 2 * pair + e) * 8, 8)
                    offs[row, 0:tok] = low
                    offs[row, tok:] = high
        return 0

    lax.fori_loop(0, z.pairs, each, 0)
    rows = z.hg * 8
    parts = jnp.zeros((3 * rows, z.buckets), F32)
    for n in range(z.group * span):
        both = aligned(offs[n * rows : (n + 1) * rows, :])
        row = n // span * CODE_ROWS + n % span
        parts = parts + dot(thirds(both), onehot_of(codes[row : row + 1, :], z), NT)
    parts = parts[0:rows] + parts[rows : 2 * rows] + parts[2 * rows :]
    head = lax.broadcasted_iota(jnp.int32, (8, z.buckets), 0)
    total = jnp.zeros((8, z.buckets), F32)
    for h in range(z.hg):
        total = jnp.where(head == h, parts[8 * h : 8 * h + 8].sum(axis=0, keepdims=True), total)
    gb[...] = total


def grad_q_kernel(z, keys, halo, s16, dq):
    tok, span = z.tok, z.span

    def each(pair, _):
        lanes = at(pair * 128, 128)
        blocks = [halo[2 * b * tok : (2 * b + 1) * tok, lanes] for b in range(z.halo)]
        blocks += [keys[j * tok : (j + 1) * tok, lanes] for j in range(z.group)]
        turned = jnp.concatenate([block.T for block in blocks], axis=1)
        for i in range(z.group):
            window = slice(i * tok, (i + span) * tok)
            cross = dot(turned[:, window], s16[pair, window, i * z.wide : (i + 1) * z.wide], NN)
            both = jnp.concatenate([cross[0 : z.hd, 0:tok], cross[z.hd :, tok:]], axis=0)
            dq[i * tok : (i + 1) * tok, lanes] = (z.scale * both.T).astype(BF16)
        return 0

    lax.fori_loop(0, z.pairs, each, 0)


def tail_kernel(z, keys, values, halo, stats, table, qh, dh, ph, sh, bases):
    tok, span = z.tok, z.span
    tables = [(b, s) for b in range(z.halo) for s in range(b + 1, span)]
    rows = []
    for b in range(z.halo):
        codes = halo[b * z.rows + 2 * tok : (b + 1) * z.rows, :].astype(F32)
        rows += [codes[s : s + 1, :] for s in range(b + 1, span)]
    slant_tables(z, table, rows, bases)
    for pair in range(z.pairs):
        lanes = slice(pair * 128, (pair + 1) * 128)
        for b in range(z.halo):
            top = b * z.rows
            wide = slice(b * z.wide, (b + 1) * z.wide)
            q = masked_pair(halo[top : top + tok, lanes] * jnp.asarray(z.scale, BF16), z)
            d = masked_pair(halo[top + tok : top + 2 * tok, lanes], z)
            qh[pair, wide, :] = q
            dh[pair, wide, :] = d
            u = b * z.pairs + pair
            lse, delta = (stats[r : r + 1, :] for r in (u, z.group * z.pairs + u))
            for s in range(b + 1, span):
                j = z.group + b - s
                block = slice(j * tok, (j + 1) * tok)
                bias = bias_rows(z, bases, tables.index((b, s)), pair)
                prob = jnp.exp(dot(keys[block, lanes], q, NT) + bias - lse)
                dscore = prob * (dot(values[block, lanes], d, NT) - delta)
                ph[pair, block, wide] = prob.astype(BF16)
                sh[pair, block, wide] = dscore.astype(BF16)


def grad_kv_kernel(z, qm, dom, p16, s16, qh, dh, ph, sh, dk, dv):
    tok = z.tok

    def each(pair, _):
        lanes = at(pair * 128, 128)
        for j in range(z.group):
            rows = slice(j * tok, (j + 1) * tok)
            ext = slice((z.halo + j) * tok, (z.halo + j + 1) * tok)
            near = slice(j * z.wide, z.group * z.wide)
            gk = dot(s16[pair, ext, near], qm[pair, near, :], NN)
            gv = dot(p16[pair, rows, near], dom[pair, near, :], NN)
            count = min(z.halo, j + z.span - z.group)
            if count > 0:
                past = slice(0, count * z.wide)
                gk = gk + dot(sh[pair, rows, past], qh[pair, past, :], NN)
                gv = gv + dot(ph[pair, rows, past], dh[pair, past, :], NN)
            dk[rows, lanes] = gk.astype(BF16)
            dv[rows, lanes] = gv.astype(BF16)
        return 0

    lax.fori_loop(0, z.pairs, each, 0)


def seal_kernel(z, grads, *refs):
    sources, sends = refs[:grads], refs[grads:]
    for k in range(z.group):
        rows = at((z.me() ^ k) * z.tok, z.tok)
        for n, ref in enumerate(sources):
            sends[k][n * z.tok : (n + 1) * z.tok, :] = ref[rows, :]


def join_kernel(*refs):
    for n, ref in enumerate(refs[:-1]):
        refs[-1][8 * n : 8 * n + 8, :] = ref[...]


def add_kernel(*refs):
    total = refs[0][...]
    for ref in refs[1:-1]:
        total = total + ref[...]
    refs[-1][...] = total


def unpack_kernel(z, *refs):
    got, outs, sem = refs[: z.group], refs[z.group : -1], refs[-1]
    me = z.me()
    copies = []
    for k in range(z.group):
        cols = at((me ^ k) * z.cw, z.cw)
        for n, out in enumerate(outs):
            src = got[k].at[n * z.tok : (n + 1) * z.tok, :]
            copies.append(pltpu.make_async_copy(src, out.at[:, cols], sem.at[len(copies)]))
    for copy in copies:
        copy.start()
    for copy in copies:
        copy.wait()


def spread_kernel(z, sides, *refs):
    sums, (gb, held, sem) = refs[: z.group], refs[z.group :]
    me = z.me()
    owner = lax.broadcasted_iota(jnp.int32, held.shape, 0) // z.hg
    total = jnp.zeros(held.shape, F32)
    for k in range(z.group):
        for n in range(sides):
            wide = jnp.concatenate([sums[k][8 * n : 8 * n + z.hg, :]] * (held.shape[0] // z.hg), axis=0)
            side = lax.axis_index("head") ^ n
            total = total + jnp.where(owner == side * z.group + (me ^ k), wide, 0.0)
    held[...] = total
    copy = pltpu.make_async_copy(held, gb, sem.at[0])
    copy.start()
    copy.wait()


def bind(kernel, *fixed):
    def bound(*refs):
        return kernel(*fixed, *refs)

    return bound


def body(queries, keys, values, grad_out, bias_table, bucket_ids, block_mask):
    tok, width = queries.shape
    heads, buckets = bias_table.shape
    span = block_mask.shape[1]
    group = span
    z = Sizes(tok, width, heads, span, buckets, group)
    blocks = lax.axis_size("seq")
    sides = lax.axis_size("head")
    assert blocks % group == 0 and (blocks & (blocks - 1)) == 0 and (sides & (sides - 1)) == 0

    def swap(value, by, axis="seq"):
        return lax.ppermute(value, axis, [(i, i ^ by) for i in range(lax.axis_size(axis))])

    def shifted(value, by):
        return lax.ppermute(value, "seq", [(i, i + by) for i in range(blocks) if 0 <= i + by < blocks])

    def swapped(parts):
        return [parts[0]] + [swap(parts[k], k) for k in range(1, group)]

    def added(*terms):
        (total,) = call(add_kernel, [(terms[0].shape, terms[0].dtype)], terms)
        return total

    hbm = pltpu.HBM
    pack_bytes = group * (z.rows + 2 * tok) * z.cw * 2
    room = VMEM_BYTES - pack_bytes - (520 << 10)
    *kv, table = call(
        bind(pack_kv_kernel, z),
        [((z.rows, z.cw), BF16)] * group + [((heads, buckets), F32)],
        (keys, values, bias_table, bucket_ids, block_mask),
        spaces=[hbm] * 5,
        scratch=[
            pltpu.VMEM((span, z.wide), jnp.int32),
            pltpu.SMEM((1, span), jnp.int32),
            pltpu.SemaphoreType.DMA((2 * group + 3,)),
        ],
        limit=room,
    )
    qd = call(
        bind(pack_qd_kernel, z),
        [((2 * tok, z.cw), BF16)] * group,
        (queries, grad_out),
        spaces=[hbm] * 2,
        scratch=[pltpu.SemaphoreType.DMA((2 * group,))],
        limit=room - (group - 1) * z.rows * z.cw * 2,
    )
    kv_got = swapped(kv)
    qd_got = swapped(qd)
    (kv_out,) = call(bind(kv_halo_kernel, z), [((z.halo * 2 * tok, z.cw), BF16)], kv_got)
    kv_halo = shifted(kv_out, group)
    (qd_out,) = call(bind(qd_halo_kernel, z), [((z.halo * z.rows, z.cw), BF16)], (*qd_got, *kv_got))
    qd_halo = shifted(qd_out, -group)

    def tile_outs(count):
        tile = ((count * z.pairs, tok, z.wide), F32)
        row = ((span * group * z.pairs, z.wide), F32)
        return [tile, tile, row, row, row]

    near, far = len(z.near), len(z.far)
    unit = 2 * 128 * tok * z.wide
    own_k, own_v, bias_near, bias_far, codes = call(
        bind(bias_kernel, z),
        [((group * tok, z.cw), BF16)] * 2
        + [((near * z.pairs, tok, z.wide), F32), ((far * z.pairs, tok, z.wide), F32)]
        + [((group * CODE_ROWS, z.wide), F32)],
        (*kv_got, table),
        scratch=[pltpu.VMEM((group * span * z.hg * 8, z.wide), F32)],
    )
    qm, dom, wnear, dnear, *sums = call(
        bind(near_kernel, z),
        [((z.pairs, group * z.wide, 128), BF16)] * 2 + tile_outs(near),
        (*qd_got, own_k, own_v, bias_near),
        flops=2 * near * z.pairs * unit,
    )
    stats, factors, wfar, dfar, *_ = call(
        bind(far_kernel, z),
        [((2 * group * z.pairs, z.wide), F32), ((span * group * z.pairs, z.wide), F32)] + tile_outs(far),
        (kv_halo, qm, dom, bias_far, *sums),
        flops=2 * far * z.pairs * unit,
    )
    stats_halo = shifted(stats, -group)
    p16, s16, gb = call(
        bind(own_kernel, z),
        [
            ((z.pairs, group * tok, group * z.wide), BF16),
            ((z.pairs, z.ext * tok, group * z.wide), BF16),
            ((8, buckets), F32),
        ],
        (codes, stats, factors, wnear, dnear, wfar, dfar),
        scratch=[pltpu.VMEM((group * span * z.hg * 8, z.wide), F32)],
    )
    by = group
    while by < blocks:
        other = swap(gb, by)
        gb = added(gb, other)
        by = by * 2
    sums_of = [gb] + [swap(gb, k, "head") for k in range(1, sides)]
    (dq,) = call(
        bind(grad_q_kernel, z),
        [((group * tok, z.cw), BF16)],
        (own_k, kv_halo, s16),
        flops=(near + far) * z.pairs * unit,
    )
    lanes_of = ((z.pairs, group * tok, z.halo * z.wide), BF16)
    rows_of = ((z.pairs, z.halo * z.wide, 128), BF16)
    halo_terms = call(
        bind(tail_kernel, z),
        [rows_of, rows_of, lanes_of, lanes_of],
        (own_k, own_v, qd_halo, stats_halo, table),
        scratch=[pltpu.VMEM((far * z.hg * 8, z.wide), F32)],
        flops=2 * far * z.pairs * unit,
    )
    dk, dv = call(
        bind(grad_kv_kernel, z),
        [((group * tok, z.cw), BF16)] * 2,
        (qm, dom, p16, s16, *halo_terms),
        flops=2 * (near + far) * z.pairs * unit,
    )
    ret = call(bind(seal_kernel, z, 3), [((3 * tok, z.cw), BF16)] * group, (dq, dk, dv))
    back = swapped(ret)

    (joined,) = call(join_kernel, [((8 * sides, buckets), F32)], sums_of)
    spread = swapped([joined] * group)
    grads = call(
        bind(unpack_kernel, z),
        [((tok, width), BF16)] * 3,
        back,
        out_space=hbm,
        scratch=[pltpu.SemaphoreType.DMA((3 * group,))],
    )
    (grad_bias,) = call(
        bind(spread_kernel, z, sides),
        [((heads * sides, buckets), F32)],
        spread,
        out_space=hbm,
        scratch=[pltpu.VMEM((heads * sides, buckets), F32), pltpu.SemaphoreType.DMA((1,))],
    )
    return (*grads, grad_bias)


def solution(mesh):
    placed = (
        P("seq", "head"),
        P("seq", "head"),
        P("seq", "head"),
        P("seq", "head"),
        P("head", None),
        P("seq", None, None),
        P("seq", None),
    )

    return jax.shard_map(
        body,
        mesh=mesh,
        in_specs=placed,
        out_specs=(P("seq", "head"), P("seq", "head"), P("seq", "head"), P()),
        check_vma=False,
    )
```

```python
import math

import jax
import jax.numpy as jnp
from jax import lax
from jax.experimental import pallas as pl
from jax.experimental.pallas import tpu as pltpu
from jax.sharding import PartitionSpec as P


F32 = jnp.float32
BF16 = jnp.bfloat16
NEG = -1e30
NT = (((1,), (1,)), ((), ()))
NN = (((1,), (0,)), ((), ()))
CODE_ROWS = 16
VMEM_BYTES = 67043328


def dot(a, b, dims):
    return lax.dot_general(a, b, dims, preferred_element_type=F32)


def at(start, size):
    return pl.ds(pl.multiple_of(start, size), size)


def call(kernel, outs, args, scratch=(), spaces=None, out_space=pltpu.VMEM, flops=0, limit=16 << 20):
    spaces = spaces or [pltpu.VMEM] * len(args)
    moved = sum(a.size * a.dtype.itemsize for a in args)
    args = [
        pltpu.with_memory_space_constraint(a, s) if s == pltpu.VMEM else a for a, s in zip(args, spaces, strict=True)
    ]
    return pl.pallas_call(
        kernel,
        out_shape=tuple(out_space(s, d) for s, d in outs),
        in_specs=[pl.BlockSpec(memory_space=s) for s in spaces],
        out_specs=tuple(pl.BlockSpec(memory_space=out_space) for _ in outs),
        scratch_shapes=list(scratch),
        compiler_params=pltpu.CompilerParams(vmem_limit_bytes=limit),
        cost_estimate=pl.CostEstimate(flops=flops, bytes_accessed=moved, transcendentals=0),
    )(*args)


class Sizes:
    def __init__(self, tok, width, heads, span, buckets, group):
        self.tok, self.width, self.heads, self.span, self.buckets = tok, width, heads, span, buckets
        self.group = group
        self.hd = width // heads
        self.hg = heads // group
        self.cw = self.hg * self.hd
        self.pairs = self.hg // 2
        self.scale = self.hd ** (-0.5)
        self.halo = span - 1
        self.ext = group + self.halo
        self.wide = 2 * tok
        self.rows = 2 * tok + CODE_ROWS
        self.near = [(i, s) for i in range(group) for s in range(span) if s <= i]
        self.far = [(i, s) for i in range(group) for s in range(span) if s > i]
        assert heads % group == 0 and self.hg % 2 == 0 and 2 * self.hd == 128
        assert tok == 128 and buckets == 128 and group >= self.halo and self.hg <= 8
        assert math.frexp(self.scale)[0] == 0.5

    def me(self):
        return lax.rem(lax.axis_index("seq"), self.group)


def chunk_copies(z, sources, dst, sem, first):
    copies = []
    for g in range(z.group):
        cols = at((z.me() ^ g) * z.cw, z.cw)
        for n, src in enumerate(sources):
            rows = pl.ds(n * z.tok, z.tok)
            copies.append(pltpu.make_async_copy(src.at[:, cols], dst[g].at[rows, :], sem.at[first + len(copies)]))
    return copies


def pack_kv_kernel(z, k, v, bias, ids, mask, *refs):
    kv = refs[: z.group]
    table, slots, flags, sem = refs[z.group :]
    index = lax.axis_index("seq")
    copies = [
        pltpu.make_async_copy(ids.at[0], slots, sem.at[0]),
        pltpu.make_async_copy(mask, flags, sem.at[1]),
        pltpu.make_async_copy(bias, table, sem.at[2]),
    ]
    copies += chunk_copies(z, (k, v), kv, sem, len(copies))
    for copy in copies:
        copy.start()
    for copy in copies[:2]:
        copy.wait()
    rows = []
    for s in range(z.span):
        valid = True if s == 0 else (flags[0, s] == 1) & (index >= s)
        rows.append(jnp.where(valid, slots[s : s + 1, :] + 1, 0))
    rows.append(jnp.zeros((CODE_ROWS - z.span, z.wide), jnp.int32))
    codes = jnp.concatenate(rows, axis=0).astype(F32).astype(BF16)
    for g in range(z.group):
        kv[g][2 * z.tok :, :] = codes
    for copy in copies[2:]:
        copy.wait()


def pack_qd_kernel(z, q, d, *refs):
    copies = chunk_copies(z, (q, d), refs[: z.group], refs[z.group], 0)
    for copy in copies:
        copy.start()
    for copy in copies:
        copy.wait()


def kv_halo_kernel(z, *refs):
    out = refs[-1]
    me = z.me()
    first = z.group - z.halo
    for k in range(z.group):
        j = me ^ k

        @pl.when(j >= first)
        def _():
            out[at((j - first) * 2 * z.tok, 2 * z.tok), :] = refs[k][0 : 2 * z.tok, :]


def qd_halo_kernel(z, *refs):
    qd, kv, out = refs[: z.group], refs[z.group : -1], refs[-1]
    me = z.me()
    for k in range(z.group):
        j = me ^ k

        @pl.when(j < z.halo)
        def _():
            top = pl.multiple_of(j * z.rows, 16)
            out[pl.ds(top, 2 * z.tok), :] = qd[k][...]
            out[pl.ds(top + 2 * z.tok, CODE_ROWS), :] = kv[k][2 * z.tok :, :]


def onehot_of(codes, z):
    slots = lax.broadcasted_iota(jnp.int32, (z.buckets, codes.shape[1]), 0) + 1
    return jnp.where(codes.astype(jnp.int32) == slots, 1.0, 0.0).astype(BF16)


def thirds(x):
    hi = x.astype(BF16)
    rest = x - hi.astype(F32)
    mid = rest.astype(BF16)
    low = (rest - mid.astype(F32)).astype(BF16)
    return jnp.concatenate([hi.astype(F32), mid.astype(F32), low.astype(F32)], axis=0).astype(BF16)


def by_offset(split, codes, z):
    got = dot(split, onehot_of(codes, z), NN)
    return got[0:8] + got[8:16] + got[16:24] + jnp.where(codes == 0.0, NEG, 0.0)


def masked_pair(x, z):
    lane = lax.broadcasted_iota(jnp.int32, x.shape, 1)
    zero = jnp.zeros_like(x)
    return jnp.concatenate([jnp.where(lane < z.hd, x, zero), jnp.where(lane < z.hd, zero, x)], axis=0)


def slanted(row, z):
    return pltpu.roll(jnp.broadcast_to(row, (8, z.wide)), z.tok + 1, 1, stride=1, stride_axis=0)


def toeplitz(base, z):
    tok = z.tok
    lane = lax.broadcasted_iota(jnp.int32, (8, tok), 1)
    low, high = base[:, 0:tok], base[:, tok:]
    tiles = [low]
    for g in range(1, tok // 8):
        tiles.append(pltpu.roll(jnp.where(lane >= tok - 8 * g, high, low), 8 * g, 1))
    return jnp.concatenate(tiles, axis=0)


def my_table(table, z):
    head = lax.broadcasted_iota(jnp.int32, (8, z.buckets), 0)
    rows = jnp.zeros((8, z.buckets), F32)
    for h in range(z.hg):
        rows = jnp.where(head == h, table[pl.ds(z.me() * z.hg + h, 1), :], rows)
    return rows


def slant_tables(z, table, code_rows, bases):
    split = thirds(my_table(table, z))
    for n, codes in enumerate(code_rows):
        rows = by_offset(split, codes, z)
        for h in range(z.hg):
            at_row = (n * z.hg + h) * 8
            bases[at_row : at_row + 8, :] = slanted(rows[h : h + 1, :], z)


def diagonals(x, z):
    tok = z.tok
    lane = lax.broadcasted_iota(jnp.int32, (8, tok), 1)
    total = x[tok - 8 :]
    high = jnp.zeros((8, tok), F32)
    for g in range(tok // 8 - 1):
        by = tok - 8 - 8 * g
        part = pltpu.roll(x[8 * g : 8 * g + 8], by, 1)
        total = total + part
        high = high + jnp.where(lane < by, part, 0.0)
    return total - high, high


def aligned(both):
    left = 7 - (lax.broadcasted_iota(jnp.int32, both.shape, 0) & 7)
    for bit in (1, 2, 4):
        both = jnp.where((left & bit) != 0, pltpu.roll(both, bit, 1), both)
    return both


def causal(z):
    row = lax.broadcasted_iota(jnp.int32, (z.tok, z.wide), 0)
    col = lax.broadcasted_iota(jnp.int32, (z.tok, z.wide), 1) % z.tok
    return row <= col


def folded(x, how):
    return how(how(x.reshape(x.shape[0] // 8, 8, x.shape[1]), 0), 0, keepdims=True)


def bias_rows(z, bases, n, pair):
    rows = [toeplitz(bases[(n * z.hg + 2 * pair + e) * 8 : (n * z.hg + 2 * pair + e + 1) * 8, :], z) for e in range(2)]
    return jnp.concatenate(rows, axis=1)


def bias_kernel(z, *refs):
    kv, table = refs[: z.group], refs[z.group]
    keys, values, near, far, codes, bases = refs[z.group + 1 :]
    tok = z.tok
    me = z.me()
    for k in range(z.group):
        j = me ^ k
        keys[at(j * tok, tok), :] = kv[k][0:tok, :]
        values[at(j * tok, tok), :] = kv[k][tok : 2 * tok, :]
        codes[at(j * CODE_ROWS, CODE_ROWS), :] = kv[k][2 * tok :, :].astype(F32)
    tables = [(i, s) for i in range(z.group) for s in range(z.span)]
    slant_tables(z, table, [codes[i * CODE_ROWS + s : i * CODE_ROWS + s + 1, :] for i, s in tables], bases)
    for tiles, out in ((z.near, near), (z.far, far)):
        for t, (i, s) in enumerate(tiles):
            for pair in range(z.pairs):
                bias = bias_rows(z, bases, i * z.span + s, pair)
                out[t * z.pairs + pair] = jnp.where(causal(z), bias, NEG) if s == 0 else bias


def forward_tile(key, value, q, d, bias, row, outs):
    weights, dprobs, tops, totals, accums = outs
    scores = dot(key, q, NT) + bias[row]
    top = folded(scores, jnp.max)
    w = jnp.exp(scores - top)
    dprob = dot(value, d, NT)
    weights[row] = w
    dprobs[row] = dprob
    tops[pl.ds(row, 1), :] = top
    totals[pl.ds(row, 1), :] = folded(w, jnp.sum)
    accums[pl.ds(row, 1), :] = folded(w * dprob, jnp.sum)


def near_kernel(z, *refs):
    qd, keys, values, bias = refs[: z.group], *refs[z.group : z.group + 3]
    qm, dom, *outs = refs[z.group + 3 :]
    tok = z.tok
    me = z.me()
    for k in range(z.group):
        j = me ^ k
        for pair in range(z.pairs):
            lanes = slice(pair * 128, (pair + 1) * 128)
            rows = at(j * z.wide, z.wide)
            qm[pair, rows, :] = masked_pair(qd[k][0:tok, lanes] * jnp.asarray(z.scale, BF16), z)
            dom[pair, rows, :] = masked_pair(qd[k][tok : 2 * tok, lanes], z)

    def each(pair, _):
        lanes = at(pair * 128, 128)
        for t, (i, s) in enumerate(z.near):
            rows = slice((i - s) * tok, (i - s + 1) * tok)
            wide = slice(i * z.wide, (i + 1) * z.wide)
            forward_tile(
                keys[rows, lanes], values[rows, lanes], qm[pair, wide, :], dom[pair, wide, :],
                bias, t * z.pairs + pair, outs,
            )
        return 0

    lax.fori_loop(0, z.pairs, each, 0)


def far_kernel(z, halo, qm, dom, bias, tops, totals, accums, stats, fnear, ffar, *outs):
    tok = z.tok

    def each(pair, _):
        lanes = at(pair * 128, 128)
        for t, (i, s) in enumerate(z.far):
            b = z.halo + i - s
            wide = slice(i * z.wide, (i + 1) * z.wide)
            forward_tile(
                halo[2 * b * tok : (2 * b + 1) * tok, lanes], halo[(2 * b + 1) * tok : (2 * b + 2) * tok, lanes],
                qm[pair, wide, :], dom[pair, wide, :], bias, t * z.pairs + pair, outs,
            )
        for i in range(z.group):
            mine = [(tops, totals, accums, fnear, t) for t, (n, _) in enumerate(z.near) if n == i]
            mine += [(outs[2], outs[3], outs[4], ffar, t) for t, (n, _) in enumerate(z.far) if n == i]
            rows = [pl.ds(t * z.pairs + pair, 1) for *_, t in mine]
            peaks = [m[0][row, :] for m, row in zip(mine, rows, strict=True)]
            top = peaks[0]
            for peak in peaks[1:]:
                top = jnp.maximum(top, peak)
            total = jnp.zeros_like(top)
            accum = jnp.zeros_like(top)
            for m, row, peak in zip(mine, rows, peaks, strict=True):
                share = jnp.exp(peak - top)
                total = total + share * m[1][row, :]
                accum = accum + share * m[2][row, :]
            lse = top + jnp.log(total)
            for m, row, peak in zip(mine, rows, peaks, strict=True):
                m[3][row, :] = jnp.exp(peak - lse)
            stats[0, pl.ds(i * z.pairs + pair, 1), :] = lse
            stats[1, pl.ds(i * z.pairs + pair, 1), :] = accum / total
        return 0

    lax.fori_loop(0, z.pairs, each, 0)


def own_kernel(z, codes, stats, fnear, ffar, wnear, dnear, wfar, dfar, p16, s16, gb, offs):
    tok, span = z.tok, z.span

    def each(pair, _):
        for i in range(z.group):
            wide = slice(i * z.wide, (i + 1) * z.wide)
            delta = stats[1, pl.ds(i * z.pairs + pair, 1), :]
            for s in range(span):
                close = s <= i
                t = (z.near if close else z.far).index((i, s)) * z.pairs + pair
                w, d, f = (wnear, dnear, fnear) if close else (wfar, dfar, ffar)
                prob = w[t] * f[pl.ds(t, 1), :]
                dscore = prob * (d[t] - delta)
                rows = slice((z.halo + i - s) * tok, (z.halo + i - s + 1) * tok)
                s16[pair, rows, wide] = dscore.astype(BF16)
                if close:
                    p16[pair, (i - s) * tok : (i - s + 1) * tok, wide] = prob.astype(BF16)
                for e in range(2):
                    low, high = diagonals(dscore[:, e * tok : (e + 1) * tok], z)
                    row = at(((i * span + s) * z.hg + 2 * pair + e) * 8, 8)
                    offs[row, 0:tok] = low
                    offs[row, tok:] = high
        return 0

    lax.fori_loop(0, z.pairs, each, 0)
    head = lax.broadcasted_iota(jnp.int32, (8, z.wide), 0)
    total = jnp.zeros((8, z.buckets), F32)
    for n in range(z.group * span):
        both = aligned(offs[n * z.hg * 8 : (n + 1) * z.hg * 8, :])
        sums = jnp.zeros((8, z.wide), F32)
        for h in range(z.hg):
            sums = sums + jnp.where(head == h, both[8 * h : 8 * h + 8].sum(axis=0, keepdims=True), 0.0)
        row = n // span * CODE_ROWS + n % span
        got = dot(thirds(sums), onehot_of(codes[row : row + 1, :], z), NT)
        total = total + (got[0:8] + got[8:16] + got[16:24])
    gb[...] = total


def grad_q_kernel(z, keys, halo, s16, dq):
    tok, span = z.tok, z.span

    def each(pair, _):
        lanes = at(pair * 128, 128)
        blocks = [halo[2 * b * tok : (2 * b + 1) * tok, lanes] for b in range(z.halo)]
        blocks += [keys[j * tok : (j + 1) * tok, lanes] for j in range(z.group)]
        turned = jnp.concatenate([block.T for block in blocks], axis=1)
        for i in range(z.group):
            window = slice(i * tok, (i + span) * tok)
            cross = dot(turned[:, window], s16[pair, window, i * z.wide : (i + 1) * z.wide], NN)
            both = jnp.concatenate([cross[0 : z.hd, 0:tok], cross[z.hd :, tok:]], axis=0)
            dq[i * tok : (i + 1) * tok, lanes] = (z.scale * both.T).astype(BF16)
        return 0

    lax.fori_loop(0, z.pairs, each, 0)


def tail_kernel(z, keys, values, halo, stats, table, qh, dh, ph, sh, bases):
    tok, span = z.tok, z.span
    tables = [(b, s) for b in range(z.halo) for s in range(b + 1, span)]
    rows = []
    for b in range(z.halo):
        codes = halo[b * z.rows + 2 * tok : (b + 1) * z.rows, :].astype(F32)
        rows += [codes[s : s + 1, :] for s in range(b + 1, span)]
    slant_tables(z, table, rows, bases)
    for pair in range(z.pairs):
        lanes = slice(pair * 128, (pair + 1) * 128)
        for b in range(z.halo):
            top = b * z.rows
            wide = slice(b * z.wide, (b + 1) * z.wide)
            q = masked_pair(halo[top : top + tok, lanes] * jnp.asarray(z.scale, BF16), z)
            d = masked_pair(halo[top + tok : top + 2 * tok, lanes], z)
            qh[pair, wide, :] = q
            dh[pair, wide, :] = d
            u = b * z.pairs + pair
            lse, delta = stats[0, u : u + 1, :], stats[1, u : u + 1, :]
            for s in range(b + 1, span):
                j = z.group + b - s
                block = slice(j * tok, (j + 1) * tok)
                bias = bias_rows(z, bases, tables.index((b, s)), pair)
                prob = jnp.exp(dot(keys[block, lanes], q, NT) + bias - lse)
                dscore = prob * (dot(values[block, lanes], d, NT) - delta)
                ph[pair, block, wide] = prob.astype(BF16)
                sh[pair, block, wide] = dscore.astype(BF16)


def grad_kv_kernel(z, qm, dom, p16, s16, qh, dh, ph, sh, dk, dv):
    tok = z.tok

    def each(pair, _):
        lanes = at(pair * 128, 128)
        for j in range(z.group):
            rows = slice(j * tok, (j + 1) * tok)
            ext = slice((z.halo + j) * tok, (z.halo + j + 1) * tok)
            near = slice(j * z.wide, z.group * z.wide)
            gk = dot(s16[pair, ext, near], qm[pair, near, :], NN)
            gv = dot(p16[pair, rows, near], dom[pair, near, :], NN)
            count = min(z.halo, j + z.span - z.group)
            if count > 0:
                past = slice(0, count * z.wide)
                gk = gk + dot(sh[pair, rows, past], qh[pair, past, :], NN)
                gv = gv + dot(ph[pair, rows, past], dh[pair, past, :], NN)
            dk[rows, lanes] = gk.astype(BF16)
            dv[rows, lanes] = gv.astype(BF16)
        return 0

    lax.fori_loop(0, z.pairs, each, 0)


def seal_kernel(z, grads, *refs):
    sources, sends = refs[:grads], refs[grads:]
    for k in range(z.group):
        rows = at((z.me() ^ k) * z.tok, z.tok)
        for n, ref in enumerate(sources):
            sends[k][n * z.tok : (n + 1) * z.tok, :] = ref[rows, :]


def add_kernel(*refs):
    total = refs[0][...]
    for ref in refs[1:-1]:
        total = total + ref[...]
    refs[-1][...] = total


def unpack_kernel(z, *refs):
    got, outs, sem = refs[: z.group], refs[z.group : -1], refs[-1]
    me = z.me()
    copies = []
    for k in range(z.group):
        cols = at((me ^ k) * z.cw, z.cw)
        for n, out in enumerate(outs):
            src = got[k].at[n * z.tok : (n + 1) * z.tok, :]
            copies.append(pltpu.make_async_copy(src, out.at[:, cols], sem.at[len(copies)]))
    for copy in copies:
        copy.start()
    for copy in copies:
        copy.wait()


def collect_kernel(z, *refs):
    sums, out = refs[:-1], refs[-1]
    owner = lax.broadcasted_iota(jnp.int32, out.shape, 0) // z.hg
    total = jnp.zeros(out.shape, F32)
    for k in range(z.group):
        wide = jnp.concatenate([sums[k][0 : z.hg, :]] * (out.shape[0] // z.hg), axis=0)
        total = total + jnp.where(owner == lax.axis_index("head") * z.group + (z.me() ^ k), wide, 0.0)
    out[...] = total


def final_kernel(*refs):
    parts, (gb, held, sem) = refs[:-3], refs[-3:]
    held[...] = sum(ref[...] for ref in parts)
    copy = pltpu.make_async_copy(held, gb, sem.at[0])
    copy.start()
    copy.wait()


def bind(kernel, *fixed):
    def bound(*refs):
        return kernel(*fixed, *refs)

    return bound


def body(queries, keys, values, grad_out, bias_table, bucket_ids, block_mask):
    tok, width = queries.shape
    heads, buckets = bias_table.shape
    span = block_mask.shape[1]
    group = span
    z = Sizes(tok, width, heads, span, buckets, group)
    blocks = lax.axis_size("seq")
    sides = lax.axis_size("head")
    assert blocks % group == 0 and (blocks & (blocks - 1)) == 0 and (sides & (sides - 1)) == 0

    def swap(value, by, axis="seq"):
        return lax.ppermute(value, axis, [(i, i ^ by) for i in range(lax.axis_size(axis))])

    def shifted(value, by):
        return lax.ppermute(value, "seq", [(i, i + by) for i in range(blocks) if 0 <= i + by < blocks])

    def swapped(parts):
        return [parts[0]] + [swap(parts[k], k) for k in range(1, group)]

    def added(*terms):
        (total,) = call(add_kernel, [(terms[0].shape, terms[0].dtype)], terms)
        return total

    hbm = pltpu.HBM
    pack_bytes = group * (z.rows + 2 * tok) * z.cw * 2
    room = VMEM_BYTES - pack_bytes - (520 << 10)
    *kv, table = call(
        bind(pack_kv_kernel, z),
        [((z.rows, z.cw), BF16)] * group + [((heads, buckets), F32)],
        (keys, values, bias_table, bucket_ids, block_mask),
        spaces=[hbm] * 5,
        scratch=[
            pltpu.VMEM((span, z.wide), jnp.int32),
            pltpu.SMEM((1, span), jnp.int32),
            pltpu.SemaphoreType.DMA((2 * group + 3,)),
        ],
        limit=room,
    )
    qd = call(
        bind(pack_qd_kernel, z),
        [((2 * tok, z.cw), BF16)] * group,
        (queries, grad_out),
        spaces=[hbm] * 2,
        scratch=[pltpu.SemaphoreType.DMA((2 * group,))],
        limit=room - (group - 1) * z.rows * z.cw * 2,
    )
    kv_got = swapped(kv)
    qd_got = swapped(qd)
    (kv_out,) = call(bind(kv_halo_kernel, z), [((z.halo * 2 * tok, z.cw), BF16)], kv_got)
    kv_halo = shifted(kv_out, group)
    (qd_out,) = call(bind(qd_halo_kernel, z), [((z.halo * z.rows, z.cw), BF16)], (*qd_got, *kv_got))
    qd_halo = shifted(qd_out, -group)

    def tile_outs(count):
        tile = ((count * z.pairs, tok, z.wide), F32)
        row = ((count * z.pairs, z.wide), F32)
        return [tile, tile, row, row, row]

    near, far = len(z.near), len(z.far)
    unit = 2 * 128 * tok * z.wide
    own_k, own_v, bias_near, bias_far, codes = call(
        bind(bias_kernel, z),
        [((group * tok, z.cw), BF16)] * 2
        + [((near * z.pairs, tok, z.wide), F32), ((far * z.pairs, tok, z.wide), F32)]
        + [((group * CODE_ROWS, z.wide), F32)],
        (*kv_got, table),
        scratch=[pltpu.VMEM((group * span * z.hg * 8, z.wide), F32)],
    )
    qm, dom, wnear, dnear, *sums = call(
        bind(near_kernel, z),
        [((z.pairs, group * z.wide, 128), BF16)] * 2 + tile_outs(near),
        (*qd_got, own_k, own_v, bias_near),
        flops=2 * near * z.pairs * unit,
    )
    stats, fnear, ffar, wfar, dfar, *_ = call(
        bind(far_kernel, z),
        [((2, group * z.pairs, z.wide), F32), ((near * z.pairs, z.wide), F32), ((far * z.pairs, z.wide), F32)]
        + tile_outs(far),
        (kv_halo, qm, dom, bias_far, *sums),
        flops=2 * far * z.pairs * unit,
    )
    stats_halo = lax.ppermute(stats, "seq", [(i, (i - group) % blocks) for i in range(blocks)])
    p16, s16, gb = call(
        bind(own_kernel, z),
        [
            ((z.pairs, group * tok, group * z.wide), BF16),
            ((z.pairs, z.ext * tok, group * z.wide), BF16),
            ((8, buckets), F32),
        ],
        (codes, stats, fnear, ffar, wnear, dnear, wfar, dfar),
        scratch=[pltpu.VMEM((group * span * z.hg * 8, z.wide), F32)],
    )
    by = group
    while by < blocks:
        other = swap(gb, by)
        gb = added(gb, other)
        by = by * 2
    (dq,) = call(
        bind(grad_q_kernel, z),
        [((group * tok, z.cw), BF16)],
        (own_k, kv_halo, s16),
        flops=(near + far) * z.pairs * unit,
    )
    lanes_of = ((z.pairs, group * tok, z.halo * z.wide), BF16)
    rows_of = ((z.pairs, z.halo * z.wide, 128), BF16)
    halo_terms = call(
        bind(tail_kernel, z),
        [rows_of, rows_of, lanes_of, lanes_of],
        (own_k, own_v, qd_halo, stats_halo, table),
        scratch=[pltpu.VMEM((far * z.hg * 8, z.wide), F32)],
        flops=2 * far * z.pairs * unit,
    )
    dk, dv = call(
        bind(grad_kv_kernel, z),
        [((group * tok, z.cw), BF16)] * 2,
        (qm, dom, p16, s16, *halo_terms),
        flops=2 * (near + far) * z.pairs * unit,
    )
    ret = call(bind(seal_kernel, z, 3), [((3 * tok, z.cw), BF16)] * group, (dq, dk, dv))
    back = swapped(ret)

    spread = swapped([gb] * group)
    (half,) = call(bind(collect_kernel, z), [((heads * sides, buckets), F32)], spread)
    halves = [half] + [swap(half, k, "head") for k in range(1, sides)]
    grads = call(
        bind(unpack_kernel, z),
        [((tok, width), BF16)] * 3,
        back,
        out_space=hbm,
        scratch=[pltpu.SemaphoreType.DMA((3 * group,))],
    )
    (grad_bias,) = call(
        final_kernel,
        [((heads * sides, buckets), F32)],
        halves,
        out_space=hbm,
        scratch=[pltpu.VMEM((heads * sides, buckets), F32), pltpu.SemaphoreType.DMA((1,))],
    )
    return (*grads, grad_bias)


def solution(mesh):
    placed = (
        P("seq", "head"),
        P("seq", "head"),
        P("seq", "head"),
        P("seq", "head"),
        P("head", None),
        P("seq", None, None),
        P("seq", None),
    )

    return jax.shard_map(
        body,
        mesh=mesh,
        in_specs=placed,
        out_specs=(P("seq", "head"), P("seq", "head"), P("seq", "head"), P()),
        check_vma=False,
    )
```
